128 devices in a mesh: req: 8 (over z, core), mlp: 16 (over x, y).
Axes of the slice: x: 4, y: 4, z: 4, core: 2. Of those that a mesh axis runs over, the one named last changes fastest.
Arguments:
- inputs: bfloat16 [2, 768, 4096], P(None, 'mlp', 'req'), may hold values from -6 to 6
- norm_gains: float32 [3, 4096], P(None, 'req'), may hold values from 0.25 to 1.75
- attn_weight: bfloat16 [4096, 12288], P('req', 'mlp'), may hold values from -0.09375 to 0.09375
- up_weight: bfloat16 [4096, 16384], P('req', 'mlp'), may hold values from -0.09375 to 0.09375
- dense_weight: bfloat16 [4096, 4096], P('mlp', 'req'), may hold values from -0.09375 to 0.09375
- down_weight: bfloat16 [16384, 4096], P('mlp', 'req'), may hold values from -0.046875 to 0.046875
- next_weight: bfloat16 [4096, 12288], P('req', 'mlp'), may hold values from -0.09375 to 0.09375
- cache_keys: bfloat16 [512, 128, 4096], P('req', None, 'mlp'), may hold values from -360 to 360
- cache_values: bfloat16 [512, 128, 4096], P('req', None, 'mlp'), may hold values from -6 to 6
- lengths: int32 [96], replicated, may hold values from 1 to 4096, as said below
- slot_table: int32 [2, 512], P(None, 'req'), may hold values from -1 to 95, as said below
- parents: int32 [1, 768], P(None, 'req'), may hold values from 0 to 7
Outputs:
- layer_out: bfloat16 [2, 768, 4096], P(None, 'mlp', 'req')
- next_qkv: bfloat16 [2, 768, 12288], P(None, 'req', 'mlp')
The draws below stay inside these ranges and needn't reach their ends.
Inputs may be any that keep to these rules, and one draw needn't show every extreme that they name: `lengths`: each request has between 1 and 32 pages of 128 tokens; the longest request has exactly 32 full pages. `slot_table`: every page of every request is held by exactly one slot; an empty slot has request -1 and page 0. All requests together hold 440 pages, and in every draw the slots of some index of req are all in use.
All inputs are finite; a program needn't handle non-finite values.
Results may differ from the reference program's by a relative error of at most 0.04.
Values may be sent and summed in bfloat16 or wider, within the bound.
A program may use at most 128 MiB of HBM per device.

```python
import math
import jax
import jax.numpy as jnp
from jax import lax

D = 4096
HEADS = 32
HD = 128
FF = 16384
ROT = 32
PAGE = 128
BEAM = 8
STEPS = 2
MAXPAGES = 32
SLOTS_DEV = 64
REQUESTS = 96
BEAMS = 768
SLOTS = 512


def page_layout(key):
    base = jax.random.fold_in(key, 11)
    order_key, offset_key, place_key, device_key = jax.random.split(base, 4)
    shifts = jnp.array([0, 2, 3, 4, 4, 5, 5, 5, 5, 5, 5, 5], jnp.int32)
    pattern = jnp.right_shift(jnp.full((12,), MAXPAGES, jnp.int32), shifts)
    counts = jnp.tile(pattern, REQUESTS // 12)
    counts = counts[jax.random.permutation(order_key, REQUESTS)]
    offsets = jax.random.randint(offset_key, (REQUESTS,), 0, PAGE)
    first_top = jnp.argmax(counts == MAXPAGES)
    offsets = jnp.where(jnp.arange(REQUESTS) == first_top, 0, offsets)
    lengths = counts * PAGE - offsets
    total_pages = REQUESTS // 12 * (MAXPAGES + MAXPAGES // 4 + MAXPAGES // 8 + 2 * (MAXPAGES // 16) + 7 * (MAXPAGES // 32))
    owners = jnp.repeat(jnp.arange(REQUESTS, dtype=jnp.int32), counts, total_repeat_length=total_pages)
    starts = jnp.cumsum(counts) - counts
    pages = jnp.arange(total_pages, dtype=jnp.int32) - starts[owners]
    ranking = jax.random.permutation(place_key, SLOTS)
    chosen_device = jax.random.randint(device_key, (), 0, SLOTS // SLOTS_DEV)
    priority = ranking + jnp.where(jnp.arange(SLOTS) // SLOTS_DEV == chosen_device, 0, SLOTS)
    places = jnp.argsort(priority)[:total_pages]
    slot_owner = jnp.full((SLOTS,), -1, jnp.int32).at[places].set(owners)
    slot_page = jnp.zeros((SLOTS,), jnp.int32).at[places].set(pages)
    return (lengths.astype(jnp.int32), jnp.stack([slot_owner, slot_page]))


def draw_lengths(key, part):
    return page_layout(key)[0]


def draw_slot_table(key, part):
    return page_layout(key)[1]


def draw_cache_keys(key, part):
    noise = jnp.clip(jax.random.normal(key, (SLOTS, PAGE, D), jnp.float32), -6.0, 6.0)
    return noise.astype(jnp.bfloat16)


def set_ends(result, rng, low, high):
    shape = result.shape
    spot = [jax.random.randint(jax.random.fold_in(rng, axis), (), 0, shape[axis]) for axis in range(len(shape))]
    result = result.at[tuple(spot)].set(low)
    longest = shape.index(max(shape))
    spot[longest] = (spot[longest] + 1) % shape[longest]
    return result.at[tuple(spot)].set(high)


def block_levels(key, shape, shards, least, high):
    def one(axis_at, blocks):
        heights = jax.random.uniform(jax.random.fold_in(jax.random.fold_in(key, 6), axis_at), (blocks,), jnp.float32, least / len(shards), high / len(shards))
        return jnp.repeat(jnp.exp(heights), shape[axis_at] // blocks).reshape((-1,) + (1,) * (len(shape) - axis_at - 1))

    level = one(*shards[0])
    for cut in shards[1:]:
        level = level * one(*cut)
    return level


def scatter_about(own_key, dims, deviation, most, pieces=(), held_as=jnp.bfloat16):
    gain = block_levels(own_key, dims, pieces, -0.22, 0.18) if pieces else 1.0
    entries = jax.random.normal(own_key, dims, jnp.float32) * deviation * gain
    return jnp.minimum(jnp.maximum(entries, -most), most).astype(held_as)


def setup_inputs(seed: int = 0) -> dict:
    seeds = jax.random.split(jax.random.key(seed), 13)
    inputs = scatter_about(seeds[0], (STEPS, BEAMS, D), 1.0, 6.0, ((1, 16), (2, 8)))
    norm_gains = jnp.clip(1.0 + 0.15 * jax.random.normal(seeds[1], (3, D), jnp.float32), 0.25, 1.75)
    attn_weight = scatter_about(seeds[2], (D, 3 * D), D ** -0.5, 0.09375, ((0, 8), (1, 16)))
    up_weight = scatter_about(seeds[3], (D, FF), D ** -0.5, 0.09375, ((0, 8), (1, 16)))
    dense_weight = scatter_about(seeds[4], (D, D), D ** -0.5, 0.09375, ((0, 16), (1, 8)))
    down_weight = scatter_about(seeds[5], (FF, D), FF ** -0.5, 0.046875, ((0, 16), (1, 8)))
    next_weight = scatter_about(seeds[6], (D, 3 * D), D ** -0.5, 0.09375, ((0, 8), (1, 16)))
    cache_keys = draw_cache_keys(jax.random.fold_in(seeds[12], 71), 0)
    cache_values = scatter_about(seeds[8], (SLOTS, PAGE, D), 1.0, 6.0, ((0, 8), (2, 16)))
    lengths = draw_lengths(jax.random.fold_in(seeds[12], 71), 0)
    slot_table = draw_slot_table(jax.random.fold_in(seeds[12], 71), 0)
    parents = set_ends(jax.random.randint(seeds[11], (STEPS - 1, BEAMS), 0, BEAM), jax.random.fold_in(seeds[11], 1), 0, BEAM - 1).astype(jnp.int32)
    return dict(inputs=inputs, norm_gains=norm_gains, attn_weight=attn_weight, up_weight=up_weight, dense_weight=dense_weight, down_weight=down_weight, next_weight=next_weight, cache_keys=cache_keys, cache_values=cache_values, lengths=lengths, slot_table=slot_table, parents=parents)


NEG_FILL = -1e+30
EPSILON = 1e-05

def normalize(block):
    values = block.astype(jnp.float32)
    row_mean = lax.optimization_barrier(jnp.mean(values, axis=1, keepdims=True))
    centred = values - row_mean
    row_var = lax.optimization_barrier(jnp.mean(centred * centred, axis=1, keepdims=True))
    return centred * lax.rsqrt(row_var + EPSILON)

def rotate(vectors, positions):
    half = ROT // 2
    freq = jnp.exp(jnp.arange(half, dtype=jnp.float32) * (-2.0 * math.log(10000.0) / ROT))
    angles = positions.astype(jnp.float32)[:, None] * freq[None, :]
    cosine = jnp.concatenate([jnp.cos(angles), jnp.cos(angles)], axis=1)[:, None, :]
    sine = jnp.concatenate([jnp.sin(angles), jnp.sin(angles)], axis=1)[:, None, :]
    turned = vectors[..., :ROT]
    swapped = jnp.concatenate([-turned[..., half:], turned[..., :half]], axis=-1)
    return jnp.concatenate([turned * cosine + swapped * sine, vectors[..., ROT:]], axis=-1)

def reference(inputs, norm_gains, attn_weight, up_weight, dense_weight, down_weight, next_weight, cache_keys, cache_values, lengths, slot_table, parents):
    scale = 1.0 / math.sqrt(HD)
    highest = lax.Precision.HIGHEST
    slot_owner = slot_table[0]
    slot_pageno = slot_table[1]
    valid_owner = jnp.maximum(slot_owner, 0)
    token_pos = slot_pageno[:, None] * PAGE + jnp.arange(PAGE, dtype=jnp.int32)[None, :]
    live = (slot_owner[:, None] >= 0) & (token_pos < lengths[valid_owner][:, None])
    owner_mask = slot_owner[:, None] == jnp.arange(REQUESTS, dtype=jnp.int32)[None, :]
    owner_float = owner_mask.astype(jnp.float32)
    gather_rows = valid_owner[:, None] * BEAM + jnp.arange(BEAM, dtype=jnp.int32)[None, :]
    beam_group = jnp.arange(BEAMS, dtype=jnp.int32) // BEAM
    tail_keys = jnp.zeros((STEPS, BEAMS, HEADS, HD), jnp.bfloat16)
    tail_values = jnp.zeros((STEPS, BEAMS, HEADS, HD), jnp.bfloat16)
    layer_list = []
    next_list = []
    for step_index in range(STEPS):
        if step_index > 0:
            source = (beam_group * BEAM + parents[step_index - 1]).astype(jnp.int32)
            tail_keys = tail_keys[:, source]
            tail_values = tail_values[:, source]
        block = inputs[step_index]
        normed = normalize(block)
        attn_in = (normed * norm_gains[0]).astype(jnp.bfloat16)
        mlp_in = (normed * norm_gains[1]).astype(jnp.bfloat16)
        mixed_qkv = jnp.dot(attn_in, attn_weight, preferred_element_type=jnp.float32).reshape(BEAMS, HEADS, 3, HD)
        hidden = jnp.dot(mlp_in, up_weight, preferred_element_type=jnp.float32)
        activated = jax.nn.gelu(hidden, approximate=False).astype(jnp.bfloat16)
        positions = lengths[beam_group] + step_index
        queries = rotate(mixed_qkv[:, :, 0], positions).astype(jnp.bfloat16)
        keys_new = rotate(mixed_qkv[:, :, 1], positions).astype(jnp.bfloat16)
        values_new = mixed_qkv[:, :, 2].astype(jnp.bfloat16)
        history_keys = jnp.concatenate([tail_keys[:step_index], keys_new[None]], axis=0)
        history_values = jnp.concatenate([tail_values[:step_index], values_new[None]], axis=0)

        def one_head(head):
            query = lax.dynamic_index_in_dim(queries, head, 1, keepdims=False).astype(jnp.float32)
            page_keys = lax.dynamic_slice_in_dim(cache_keys, head * HD, HD, 2).astype(jnp.float32)
            page_vals = lax.dynamic_slice_in_dim(cache_values, head * HD, HD, 2).astype(jnp.float32)
            chosen = query[gather_rows]
            scores = jnp.einsum('sbd,std->sbt', chosen, page_keys, precision=highest) * scale
            masked = jnp.where(live[:, None, :], scores, NEG_FILL)
            slot_top = lax.optimization_barrier(jnp.max(masked, axis=2))
            request_top = lax.optimization_barrier(jnp.max(jnp.where(owner_mask[:, :, None], slot_top[:, None, :], NEG_FILL), axis=0)).reshape(BEAMS)
            own_keys = lax.dynamic_index_in_dim(history_keys, head, 2, keepdims=False).astype(jnp.float32)
            own_vals = lax.dynamic_index_in_dim(history_values, head, 2, keepdims=False).astype(jnp.float32)
            own_scores = jnp.einsum('bd,nbd->bn', query, own_keys, precision=highest) * scale
            top = jnp.maximum(request_top, lax.optimization_barrier(jnp.max(own_scores, axis=1)))
            slot_ref = top.reshape(REQUESTS, BEAM)[valid_owner]
            weights = jnp.where(live[:, None, :], jnp.exp(masked - slot_ref[:, :, None]), 0.0)
            rounded = lax.optimization_barrier(weights.astype(jnp.bfloat16)).astype(jnp.float32)
            slot_out = jnp.einsum('sbt,std->sbd', rounded, page_vals, precision=highest)
            total = jnp.einsum('sr,sb->rb', owner_float, lax.optimization_barrier(jnp.sum(weights, axis=2)), precision=highest).reshape(BEAMS)
            summed = jnp.einsum('sr,sbd->rbd', owner_float, slot_out, precision=highest).reshape(BEAMS, HD)
            own_weights = jnp.exp(own_scores - top[:, None])
            own_rounded = lax.optimization_barrier(own_weights.astype(jnp.bfloat16)).astype(jnp.float32)
            total = total + lax.optimization_barrier(jnp.sum(own_weights, axis=1))
            summed = summed + jnp.einsum('bn,nbd->bd', own_rounded, own_vals, precision=highest)
            return summed / total[:, None]
        heads_out = lax.map(one_head, jnp.arange(HEADS, dtype=jnp.int32))
        attended = jnp.transpose(heads_out, (1, 0, 2)).reshape(BEAMS, D).astype(jnp.bfloat16)
        update = jnp.dot(attended, dense_weight, preferred_element_type=jnp.float32) + jnp.dot(activated, down_weight, preferred_element_type=jnp.float32)
        layer = (block.astype(jnp.float32) + update).astype(jnp.bfloat16)
        next_in = (normalize(layer) * norm_gains[2]).astype(jnp.bfloat16)
        next_out = jnp.dot(next_in, next_weight, preferred_element_type=jnp.float32).astype(jnp.bfloat16)
        tail_keys = tail_keys.at[step_index].set(keys_new)
        tail_values = tail_values.at[step_index].set(values_new)
        layer_list.append(layer)
        next_list.append(next_out)
    return (jnp.stack(layer_list), jnp.stack(next_list))
```

```python
import math

import jax
import jax.numpy as jnp
from jax import lax
from jax.sharding import PartitionSpec as P

HD = 128
ROT = 32
PAGE = 128
BEAM = 8
STEPS = 2


NEG_FILL = -1e30
EPSILON = 1e-05


def rotate(vectors, positions):
    half = ROT // 2
    freq = jnp.exp(jnp.arange(half, dtype=jnp.float32) * (-2.0 * math.log(10000.0) / ROT))
    angles = positions.astype(jnp.float32)[..., None] * freq
    cosine = jnp.concatenate([jnp.cos(angles), jnp.cos(angles)], axis=-1)[..., None, :]
    sine = jnp.concatenate([jnp.sin(angles), jnp.sin(angles)], axis=-1)[..., None, :]
    turned = vectors[..., :ROT]
    swapped = jnp.concatenate([-turned[..., half:], turned[..., :half]], axis=-1)
    return jnp.concatenate([turned * cosine + swapped * sine, vectors[..., ROT:]], axis=-1)


def row_normalize(values):
    width = values.shape[-1]
    local_mean = jnp.mean(values, axis=-1)
    centred = values - local_mean[..., None]
    local_m2 = jnp.sum(centred * centred, axis=-1)
    stats = lax.all_gather(jnp.stack([local_mean, local_m2], axis=-1), "req")
    means = stats[..., 0]
    row_mean = jnp.mean(means, axis=0)
    spread = means - row_mean
    row_m2 = jnp.sum(stats[..., 1], axis=0) + width * jnp.sum(spread * spread, axis=0)
    row_var = row_m2 / (width * stats.shape[0])
    return (values - row_mean[..., None]) * lax.rsqrt(row_var + EPSILON)[..., None]


def shards(
    inputs,
    norm_gains,
    attn_weight,
    up_weight,
    dense_weight,
    down_weight,
    next_weight,
    cache_keys,
    cache_values,
    lengths,
    slot_table,
    parents,
):
    scale = 1.0 / math.sqrt(HD)
    highest = lax.Precision.HIGHEST
    steps, local_rows, local_width = inputs.shape
    own_count = parents.shape[1]
    request_count = lengths.shape[0]
    beam_total = request_count * BEAM
    head_count = dense_weight.shape[0] // HD
    triple_width = attn_weight.shape[1]
    slot_count = slot_table.shape[1]
    req_size = beam_total // own_count
    mlp_size = beam_total // local_rows
    offset = lax.axis_index("req") * own_count
    beam_group = jnp.arange(beam_total, dtype=jnp.int32) // BEAM
    all_positions = lengths[beam_group][None, :] + jnp.arange(steps, dtype=jnp.int32)[:, None]
    own_group = jnp.arange(own_count, dtype=jnp.int32) // BEAM
    slot_owner = slot_table[0]
    slot_pageno = slot_table[1]
    valid_owner = jnp.maximum(slot_owner, 0)
    token_pos = slot_pageno[:, None] * PAGE + jnp.arange(PAGE, dtype=jnp.int32)[None, :]
    live = (slot_owner[:, None] >= 0) & (token_pos < lengths[valid_owner][:, None])
    live_wide = live[None, :, None, None, :]
    owner_mask = slot_owner[:, None] == jnp.arange(request_count, dtype=jnp.int32)[None, :]
    owner_float = owner_mask.astype(jnp.float32)
    gather_rows = valid_owner[:, None] * BEAM + jnp.arange(BEAM, dtype=jnp.int32)[None, :]
    page_keys = cache_keys.reshape(slot_count, PAGE, head_count, HD)
    page_values = cache_values.reshape(slot_count, PAGE, head_count, HD)

    block = inputs.astype(jnp.float32)
    normed = row_normalize(block)
    attn_in = (normed * norm_gains[0]).astype(jnp.bfloat16)
    mlp_in = (normed * norm_gains[1]).astype(jnp.bfloat16)
    joined = jnp.concatenate([attn_in, mlp_in], axis=-1)
    piece = lax.all_gather(joined, "mlp", axis=1, tiled=True).reshape(steps * beam_total, -1)
    first = jnp.dot(piece[:, :local_width], attn_weight, preferred_element_type=jnp.float32)
    second = jnp.dot(piece[:, local_width:], up_weight, preferred_element_type=jnp.float32)
    partial_sums = jnp.concatenate([first, second], axis=1)
    summed_all = lax.psum(partial_sums.astype(jnp.bfloat16), "req").astype(jnp.float32)
    mixed_all = summed_all[:, :triple_width].reshape(steps, beam_total, head_count, 3, HD)
    activated_all = jax.nn.gelu(summed_all[:, triple_width:], approximate=False).astype(
        jnp.bfloat16
    )
    queries_all = rotate(mixed_all[:, :, :, 0], all_positions).astype(jnp.bfloat16)
    mixed_own = lax.dynamic_slice_in_dim(mixed_all, offset, own_count, 1)
    own_positions = lax.dynamic_slice_in_dim(all_positions, offset, own_count, 1)
    queries_own = lax.dynamic_slice_in_dim(queries_all, offset, own_count, 1)
    keys_new = rotate(mixed_own[:, :, :, 1], own_positions).astype(jnp.bfloat16)
    values_new = mixed_own[:, :, :, 2].astype(jnp.bfloat16)

    chosen = queries_all[:, gather_rows]
    scores = (
        jnp.einsum("zsbhd,sthd->zsbht", chosen, page_keys, preferred_element_type=jnp.float32)
        * scale
    )
    masked = jnp.where(live_wide, scores, NEG_FILL)
    slot_top = jnp.max(masked, axis=4)
    weights = jnp.where(live_wide, jnp.exp(masked - slot_top[..., None]), 0.0)
    slot_total = jnp.sum(weights, axis=4)
    slot_out = jnp.einsum(
        "zsbht,sthd->zsbhd",
        weights.astype(jnp.bfloat16),
        page_values,
        preferred_element_type=jnp.float32,
    )
    request_top = jnp.max(
        jnp.where(owner_mask[None, :, :, None, None], slot_top[:, :, None], NEG_FILL), axis=1
    )
    factor = jnp.exp(slot_top - request_top[:, valid_owner])
    page_total = jnp.einsum(
        "sr,zsbh->zrbh", owner_float, slot_total * factor, precision=highest
    ).reshape(steps, beam_total, head_count)
    page_out = jnp.einsum(
        "sr,zsbhd->zrbhd", owner_float, slot_out * factor[..., None], precision=highest
    ).reshape(steps, beam_total, head_count, HD)
    page_top = request_top.reshape(steps, beam_total, head_count)
    global_top = lax.pmax(page_top, "req")
    rescale = jnp.exp(page_top - global_top)
    partial = jnp.concatenate(
        [page_out * rescale[..., None], (page_total * rescale)[..., None]], axis=-1
    )
    own_partial = lax.psum_scatter(
        partial.astype(jnp.bfloat16), "req", scatter_dimension=1, tiled=True
    ).astype(jnp.float32)
    own_top = lax.dynamic_slice_in_dim(global_top, offset, own_count, 1)
    own_out = own_partial[..., :HD]
    own_total = own_partial[..., HD]

    source = own_group * BEAM + parents[0]
    attended_steps = []
    for step_index in range(steps):
        tail_keys = [keys_new[prior][source] for prior in range(step_index)]
        tail_values = [values_new[prior][source] for prior in range(step_index)]
        history_keys = jnp.stack(tail_keys + [keys_new[step_index]], axis=0)
        history_values = jnp.stack(tail_values + [values_new[step_index]], axis=0)
        own_scores = (
            jnp.einsum(
                "bhd,nbhd->bhn",
                queries_own[step_index],
                history_keys,
                preferred_element_type=jnp.float32,
            )
            * scale
        )
        top = jnp.maximum(own_top[step_index], jnp.max(own_scores, axis=2))
        page_factor = jnp.exp(own_top[step_index] - top)
        own_weights = jnp.exp(own_scores - top[..., None])
        total = own_total[step_index] * page_factor + jnp.sum(own_weights, axis=2)
        summed = own_out[step_index] * page_factor[..., None] + jnp.einsum(
            "bhn,nbhd->bhd",
            own_weights.astype(jnp.bfloat16),
            history_values,
            preferred_element_type=jnp.float32,
        )
        attended_steps.append(
            (summed / total[..., None]).astype(jnp.bfloat16).reshape(own_count, head_count * HD)
        )
    attended = jnp.stack(attended_steps)
    attended_all = lax.all_gather(attended, "req", axis=1, tiled=True)

    def by_mlp(rows):
        return (
            rows.reshape(steps, mlp_size, local_rows, -1)
            .transpose(1, 0, 2, 3)
            .reshape(steps * beam_total, -1)
        )

    update = lax.psum_scatter(
        (
            jnp.dot(by_mlp(attended_all), dense_weight, preferred_element_type=jnp.float32)
            + jnp.dot(
                by_mlp(activated_all.reshape(steps, beam_total, -1)),
                down_weight,
                preferred_element_type=jnp.float32,
            )
        ).astype(jnp.bfloat16),
        "mlp",
        scatter_dimension=0,
        tiled=True,
    ).astype(jnp.float32)
    layer = (block + update.reshape(steps, local_rows, local_width)).astype(jnp.bfloat16)
    next_in = (row_normalize(layer.astype(jnp.float32)) * norm_gains[2]).astype(jnp.bfloat16)
    gathered = lax.all_gather(next_in, "mlp", axis=1, tiled=True)
    by_req = (
        gathered.reshape(steps, req_size, own_count, local_width)
        .transpose(1, 0, 2, 3)
        .reshape(steps * beam_total, local_width)
    )
    next_partial = jnp.dot(by_req, next_weight, preferred_element_type=jnp.float32)
    next_out = lax.psum_scatter(
        next_partial.astype(jnp.bfloat16), "req", scatter_dimension=0, tiled=True
    ).reshape(steps, own_count, -1)
    return (layer, next_out)


def solution(mesh):
    in_specs = (
        P(None, "mlp", "req"),
        P(None, "req"),
        P("req", "mlp"),
        P("req", "mlp"),
        P("mlp", "req"),
        P("mlp", "req"),
        P("req", "mlp"),
        P("req", None, "mlp"),
        P("req", None, "mlp"),
        P(),
        P(None, "req"),
        P(None, "req"),
    )
    out_specs = (P(None, "mlp", "req"), P(None, "req", "mlp"))
    return jax.shard_map(shards, mesh=mesh, in_specs=in_specs, out_specs=out_specs, check_vma=False)
```

```python
import functools
import math

import jax
import jax.numpy as jnp
from jax import lax
from jax.experimental import pallas as pl
from jax.experimental.pallas import tpu as pltpu
from jax.sharding import PartitionSpec as P

MESH = pl.DeviceIdType.MESH

HD = 128
ROT = 32
PAGE = 128
BEAM = 8
STEPS = 2


NEG_FILL = -1e30
EPSILON = 1e-05


def rotate(vectors, positions):
    half = ROT // 2
    freq = jnp.exp(jnp.arange(half, dtype=jnp.float32) * (-2.0 * math.log(10000.0) / ROT))
    angles = positions.astype(jnp.float32)[..., None] * freq
    cosine = jnp.concatenate([jnp.cos(angles), jnp.cos(angles)], axis=-1)[..., None, :]
    sine = jnp.concatenate([jnp.sin(angles), jnp.sin(angles)], axis=-1)[..., None, :]
    turned = vectors[..., :ROT]
    swapped = jnp.concatenate([-turned[..., half:], turned[..., :half]], axis=-1)
    return jnp.concatenate([turned * cosine + swapped * sine, vectors[..., ROT:]], axis=-1)


def exchange_kernel(axis, n, gather, x_ref, out_ref, send_sem, recv_sem, local_sem):
    me = lax.axis_index(axis)
    barrier = pltpu.get_barrier_semaphore()
    for k in range(1, n):
        pl.semaphore_signal(
            barrier, inc=1, device_id={axis: lax.rem(me + k, n)}, device_id_type=MESH
        )
    pl.semaphore_wait(barrier, n - 1)
    local = pltpu.make_async_copy(x_ref if gather else x_ref.at[me], out_ref.at[me], local_sem)
    local.start()
    copies = []
    for k in range(1, n):
        dest = lax.rem(me + k, n)
        copy = pltpu.make_async_remote_copy(
            src_ref=x_ref if gather else x_ref.at[dest],
            dst_ref=out_ref.at[me],
            send_sem=send_sem.at[k],
            recv_sem=recv_sem.at[k],
            device_id={axis: dest},
            device_id_type=MESH,
        )
        copy.start()
        copies.append(copy)
    for copy in copies:
        copy.wait()
    local.wait()


def exchange(x, axis, n, gather, collective_id):
    shape = (n,) + (x.shape if gather else x.shape[1:])
    return pl.pallas_call(
        functools.partial(exchange_kernel, axis, n, gather),
        out_shape=jax.ShapeDtypeStruct(shape, x.dtype),
        in_specs=[pl.BlockSpec(memory_space=pltpu.VMEM)],
        out_specs=pl.BlockSpec(memory_space=pltpu.VMEM),
        scratch_shapes=[
            pltpu.SemaphoreType.DMA((n,)),
            pltpu.SemaphoreType.DMA((n,)),
            pltpu.SemaphoreType.DMA(()),
        ],
        compiler_params=pltpu.CompilerParams(
            collective_id=collective_id, has_side_effects=True
        ),
    )(x)


def row_normalize(values):
    width = values.shape[-1]
    local_mean = jnp.mean(values, axis=-1)
    centred = values - local_mean[..., None]
    local_m2 = jnp.sum(centred * centred, axis=-1)
    stats = lax.all_gather(jnp.stack([local_mean, local_m2], axis=-1), "req")
    means = stats[..., 0]
    row_mean = jnp.mean(means, axis=0)
    spread = means - row_mean
    row_m2 = jnp.sum(stats[..., 1], axis=0) + width * jnp.sum(spread * spread, axis=0)
    row_var = row_m2 / (width * stats.shape[0])
    return (values - row_mean[..., None]) * lax.rsqrt(row_var + EPSILON)[..., None]


def shards(
    inputs,
    norm_gains,
    attn_weight,
    up_weight,
    dense_weight,
    down_weight,
    next_weight,
    cache_keys,
    cache_values,
    lengths,
    slot_table,
    parents,
):
    scale = 1.0 / math.sqrt(HD)
    highest = lax.Precision.HIGHEST
    steps, local_rows, local_width = inputs.shape
    own_count = parents.shape[1]
    request_count = lengths.shape[0]
    beam_total = request_count * BEAM
    head_count = dense_weight.shape[0] // HD
    triple_width = attn_weight.shape[1]
    slot_count = slot_table.shape[1]
    req_size = beam_total // own_count
    mlp_size = beam_total // local_rows
    offset = lax.axis_index("req") * own_count
    beam_group = jnp.arange(beam_total, dtype=jnp.int32) // BEAM
    all_positions = lengths[beam_group][None, :] + jnp.arange(steps, dtype=jnp.int32)[:, None]
    own_group = jnp.arange(own_count, dtype=jnp.int32) // BEAM
    slot_owner = slot_table[0]
    slot_pageno = slot_table[1]
    valid_owner = jnp.maximum(slot_owner, 0)
    token_pos = slot_pageno[:, None] * PAGE + jnp.arange(PAGE, dtype=jnp.int32)[None, :]
    live = (slot_owner[:, None] >= 0) & (token_pos < lengths[valid_owner][:, None])
    live_wide = live[None, :, None, None, :]
    owner_mask = slot_owner[:, None] == jnp.arange(request_count, dtype=jnp.int32)[None, :]
    owner_float = owner_mask.astype(jnp.float32)
    gather_rows = valid_owner[:, None] * BEAM + jnp.arange(BEAM, dtype=jnp.int32)[None, :]
    page_keys = cache_keys.reshape(slot_count, PAGE, head_count, HD)
    page_values = cache_values.reshape(slot_count, PAGE, head_count, HD)

    block = inputs.astype(jnp.float32)
    normed = row_normalize(block)
    attn_in = (normed * norm_gains[0]).astype(jnp.bfloat16)
    mlp_in = (normed * norm_gains[1]).astype(jnp.bfloat16)
    joined = jnp.concatenate([attn_in, mlp_in], axis=-1)
    piece = exchange(joined, "mlp", mlp_size, True, 0).reshape(steps * beam_total, -1)
    first = jnp.dot(piece[:, :local_width], attn_weight, preferred_element_type=jnp.float32)
    second = jnp.dot(piece[:, local_width:], up_weight, preferred_element_type=jnp.float32)
    partial_sums = jnp.concatenate([first, second], axis=1)
    summed_all = lax.psum(partial_sums.astype(jnp.bfloat16), "req").astype(jnp.float32)
    mixed_msi = summed_all[:, :triple_width].reshape(
        mlp_size, steps, local_rows, head_count, 3, HD
    )
    activated_all = jax.nn.gelu(summed_all[:, triple_width:], approximate=False).astype(
        jnp.bfloat16
    )
    mixed_all = mixed_msi[:, :, :, :, 0].transpose(1, 0, 2, 3, 4).reshape(
        steps, beam_total, head_count, HD
    )
    queries_all = rotate(mixed_all, all_positions).astype(jnp.bfloat16)
    per_own = own_count // local_rows
    mixed_own = (
        lax.dynamic_slice_in_dim(mixed_msi, lax.axis_index("req") * per_own, per_own, 0)
        .transpose(1, 0, 2, 3, 4, 5)
        .reshape(steps, own_count, head_count, 3, HD)
    )
    own_positions = lax.dynamic_slice_in_dim(all_positions, offset, own_count, 1)
    queries_own = lax.dynamic_slice_in_dim(queries_all, offset, own_count, 1)
    keys_new = rotate(mixed_own[:, :, :, 1], own_positions).astype(jnp.bfloat16)
    values_new = mixed_own[:, :, :, 2].astype(jnp.bfloat16)

    chosen = queries_all[:, gather_rows]
    scores = (
        jnp.einsum("zsbhd,sthd->zsbht", chosen, page_keys, preferred_element_type=jnp.float32)
        * scale
    )
    masked = jnp.where(live_wide, scores, NEG_FILL)
    slot_top = jnp.max(masked, axis=4)
    weights = jnp.where(live_wide, jnp.exp(masked - slot_top[..., None]), 0.0)
    slot_total = jnp.sum(weights, axis=4)
    slot_out = jnp.einsum(
        "zsbht,sthd->zsbhd",
        weights.astype(jnp.bfloat16),
        page_values,
        preferred_element_type=jnp.float32,
    )
    request_top = jnp.max(
        jnp.where(owner_mask[None, :, :, None, None], slot_top[:, :, None], NEG_FILL), axis=1
    )
    factor = jnp.exp(slot_top - request_top[:, valid_owner])
    page_total = jnp.einsum(
        "sr,zsbh->zrbh", owner_float, slot_total * factor, precision=highest
    ).reshape(steps, beam_total, head_count)
    page_out = jnp.einsum(
        "sr,zsbhd->zrbhd", owner_float, slot_out * factor[..., None], precision=highest
    ).reshape(steps, beam_total, head_count, HD)
    page_top = request_top.reshape(steps, beam_total, head_count)
    global_top = lax.pmax(page_top, "req")
    rescale = jnp.exp(page_top - global_top)
    partial = jnp.concatenate(
        [page_out * rescale[..., None], (page_total * rescale)[..., None]], axis=-1
    )
    own_partial = lax.psum_scatter(
        partial.astype(jnp.bfloat16), "req", scatter_dimension=1, tiled=True
    ).astype(jnp.float32)
    own_top = lax.dynamic_slice_in_dim(global_top, offset, own_count, 1)
    own_out = own_partial[..., :HD]
    own_total = own_partial[..., HD]

    source = own_group * BEAM + parents[0]
    attended_steps = []
    for step_index in range(steps):
        tail_keys = [keys_new[prior][source] for prior in range(step_index)]
        tail_values = [values_new[prior][source] for prior in range(step_index)]
        history_keys = jnp.stack(tail_keys + [keys_new[step_index]], axis=0)
        history_values = jnp.stack(tail_values + [values_new[step_index]], axis=0)
        own_scores = (
            jnp.einsum(
                "bhd,nbhd->bhn",
                queries_own[step_index],
                history_keys,
                preferred_element_type=jnp.float32,
            )
            * scale
        )
        top = jnp.maximum(own_top[step_index], jnp.max(own_scores, axis=2))
        page_factor = jnp.exp(own_top[step_index] - top)
        own_weights = jnp.exp(own_scores - top[..., None])
        total = own_total[step_index] * page_factor + jnp.sum(own_weights, axis=2)
        summed = own_out[step_index] * page_factor[..., None] + jnp.einsum(
            "bhn,nbhd->bhd",
            own_weights.astype(jnp.bfloat16),
            history_values,
            preferred_element_type=jnp.float32,
        )
        attended_steps.append(
            (summed / total[..., None]).astype(jnp.bfloat16).reshape(own_count, head_count * HD)
        )
    attended = jnp.stack(attended_steps)
    attended_all = lax.all_gather(attended, "req", axis=1, tiled=True)
    attended_msi = (
        attended_all.reshape(steps, mlp_size, local_rows, -1)
        .transpose(1, 0, 2, 3)
        .reshape(steps * beam_total, -1)
    )
    update_partial = (
        jnp.dot(attended_msi, dense_weight, preferred_element_type=jnp.float32)
        + jnp.dot(activated_all, down_weight, preferred_element_type=jnp.float32)
    ).astype(jnp.bfloat16)
    update = jnp.sum(
        exchange(
            update_partial.reshape(mlp_size, steps * local_rows, local_width),
            "mlp",
            mlp_size,
            False,
            1,
        ).astype(jnp.float32),
        axis=0,
    )
    layer = (block + update.reshape(steps, local_rows, local_width)).astype(jnp.bfloat16)
    next_in = (row_normalize(layer.astype(jnp.float32)) * norm_gains[2]).astype(jnp.bfloat16)
    gathered = exchange(next_in, "mlp", mlp_size, True, 2).reshape(steps * beam_total, -1)
    next_partial = jnp.dot(gathered, next_weight, preferred_element_type=jnp.float32)
    next_out = lax.psum_scatter(
        next_partial.astype(jnp.bfloat16), "req", scatter_dimension=0, tiled=True
    )
    next_out = (
        next_out.reshape(per_own, steps, local_rows, -1)
        .transpose(1, 0, 2, 3)
        .reshape(steps, own_count, -1)
    )
    return (layer, next_out)


def solution(mesh):
    in_specs = (
        P(None, "mlp", "req"),
        P(None, "req"),
        P("req", "mlp"),
        P("req", "mlp"),
        P("mlp", "req"),
        P("mlp", "req"),
        P("req", "mlp"),
        P("req", None, "mlp"),
        P("req", None, "mlp"),
        P(),
        P(None, "req"),
        P(None, "req"),
    )
    out_specs = (P(None, "mlp", "req"), P(None, "req", "mlp"))
    return jax.shard_map(shards, mesh=mesh, in_specs=in_specs, out_specs=out_specs, check_vma=False)
```

```python
import functools
import math

import jax
import jax.numpy as jnp
from jax import lax
from jax.experimental import pallas as pl
from jax.experimental.pallas import tpu as pltpu
from jax.sharding import PartitionSpec as P

MESH = pl.DeviceIdType.MESH

HD = 128
ROT = 32
PAGE = 128
BEAM = 8
STEPS = 2


NEG_FILL = -1e30
EPSILON = 1e-05


def rotate(vectors, positions):
    half = ROT // 2
    freq = jnp.exp(jnp.arange(half, dtype=jnp.float32) * (-2.0 * math.log(10000.0) / ROT))
    angles = positions.astype(jnp.float32)[..., None] * freq
    cosine = jnp.concatenate([jnp.cos(angles), jnp.cos(angles)], axis=-1)[..., None, :]
    sine = jnp.concatenate([jnp.sin(angles), jnp.sin(angles)], axis=-1)[..., None, :]
    turned = vectors[..., :ROT]
    swapped = jnp.concatenate([-turned[..., half:], turned[..., :half]], axis=-1)
    return jnp.concatenate([turned * cosine + swapped * sine, vectors[..., ROT:]], axis=-1)


def exchange_kernel(axis, n, gather, x_ref, out_ref, send_sem, recv_sem, local_sem):
    me = lax.axis_index(axis)
    barrier = pltpu.get_barrier_semaphore()
    for k in range(1, n):
        pl.semaphore_signal(
            barrier, inc=1, device_id={axis: lax.rem(me + k, n)}, device_id_type=MESH
        )
    pl.semaphore_wait(barrier, n - 1)
    local = pltpu.make_async_copy(x_ref if gather else x_ref.at[me], out_ref.at[me], local_sem)
    local.start()
    copies = []
    for k in range(1, n):
        dest = lax.rem(me + k, n)
        copy = pltpu.make_async_remote_copy(
            src_ref=x_ref if gather else x_ref.at[dest],
            dst_ref=out_ref.at[me],
            send_sem=send_sem.at[k],
            recv_sem=recv_sem.at[k],
            device_id={axis: dest},
            device_id_type=MESH,
        )
        copy.start()
        copies.append(copy)
    for copy in copies:
        copy.wait()
    local.wait()


def exchange(x, axis, n, gather, collective_id):
    shape = (n,) + (x.shape if gather else x.shape[1:])
    return pl.pallas_call(
        functools.partial(exchange_kernel, axis, n, gather),
        out_shape=jax.ShapeDtypeStruct(shape, x.dtype),
        in_specs=[pl.BlockSpec(memory_space=pltpu.VMEM)],
        out_specs=pl.BlockSpec(memory_space=pltpu.VMEM),
        scratch_shapes=[
            pltpu.SemaphoreType.DMA((n,)),
            pltpu.SemaphoreType.DMA((n,)),
            pltpu.SemaphoreType.DMA(()),
        ],
        compiler_params=pltpu.CompilerParams(
            collective_id=collective_id, has_side_effects=True
        ),
    )(x)


def row_normalize(values):
    width = values.shape[-1]
    local_mean = jnp.mean(values, axis=-1)
    centred = values - local_mean[..., None]
    local_m2 = jnp.sum(centred * centred, axis=-1)
    stats = lax.all_gather(jnp.stack([local_mean, local_m2], axis=-1), "req")
    means = stats[..., 0]
    row_mean = jnp.mean(means, axis=0)
    spread = means - row_mean
    row_m2 = jnp.sum(stats[..., 1], axis=0) + width * jnp.sum(spread * spread, axis=0)
    row_var = row_m2 / (width * stats.shape[0])
    return (values - row_mean[..., None]) * lax.rsqrt(row_var + EPSILON)[..., None]


def shards(
    inputs,
    norm_gains,
    attn_weight,
    up_weight,
    dense_weight,
    down_weight,
    next_weight,
    cache_keys,
    cache_values,
    lengths,
    slot_table,
    parents,
):
    scale = 1.0 / math.sqrt(HD)
    highest = lax.Precision.HIGHEST
    steps, local_rows, local_width = inputs.shape
    own_count = parents.shape[1]
    request_count = lengths.shape[0]
    beam_total = request_count * BEAM
    head_count = dense_weight.shape[0] // HD
    triple_width = attn_weight.shape[1]
    slot_count = slot_table.shape[1]
    req_size = beam_total // own_count
    mlp_size = beam_total // local_rows
    offset = lax.axis_index("req") * own_count
    beam_group = jnp.arange(beam_total, dtype=jnp.int32) // BEAM
    all_positions = lengths[beam_group][None, :] + jnp.arange(steps, dtype=jnp.int32)[:, None]
    own_group = jnp.arange(own_count, dtype=jnp.int32) // BEAM
    slot_owner = slot_table[0]
    slot_pageno = slot_table[1]
    valid_owner = jnp.maximum(slot_owner, 0)
    token_pos = slot_pageno[:, None] * PAGE + jnp.arange(PAGE, dtype=jnp.int32)[None, :]
    live = (slot_owner[:, None] >= 0) & (token_pos < lengths[valid_owner][:, None])
    live_wide = live[None, :, None, None, :]
    owner_mask = slot_owner[:, None] == jnp.arange(request_count, dtype=jnp.int32)[None, :]
    owner_float = owner_mask.astype(jnp.float32)
    gather_rows = valid_owner[:, None] * BEAM + jnp.arange(BEAM, dtype=jnp.int32)[None, :]

    block = inputs.astype(jnp.float32)
    rows_all = exchange(inputs, "mlp", mlp_size, True, 0).reshape(steps * beam_total, -1)
    normed = row_normalize(rows_all.astype(jnp.float32))
    attn_in = (normed * norm_gains[0]).astype(jnp.bfloat16)
    mlp_in = (normed * norm_gains[1]).astype(jnp.bfloat16)
    piece = jnp.concatenate([attn_in, mlp_in], axis=-1)
    first = jnp.dot(piece[:, :local_width], attn_weight, preferred_element_type=jnp.float32)
    second = jnp.dot(piece[:, local_width:], up_weight, preferred_element_type=jnp.float32)
    partial_sums = jnp.concatenate([first, second], axis=1)
    summed_all = lax.psum(partial_sums.astype(jnp.bfloat16), "req").astype(jnp.float32)
    mixed_msi = summed_all[:, :triple_width].reshape(
        mlp_size, steps, local_rows, head_count, 3, HD
    )
    activated_all = jax.nn.gelu(summed_all[:, triple_width:], approximate=False).astype(
        jnp.bfloat16
    )
    mixed_all = mixed_msi[:, :, :, :, 0].transpose(1, 0, 2, 3, 4).reshape(
        steps, beam_total, head_count, HD
    )
    queries_all = rotate(mixed_all, all_positions).astype(jnp.bfloat16)
    per_own = own_count // local_rows
    mixed_own = (
        lax.dynamic_slice_in_dim(mixed_msi, lax.axis_index("req") * per_own, per_own, 0)
        .transpose(1, 0, 2, 3, 4, 5)
        .reshape(steps, own_count, head_count, 3, HD)
    )
    own_positions = lax.dynamic_slice_in_dim(all_positions, offset, own_count, 1)
    queries_own = lax.dynamic_slice_in_dim(queries_all, offset, own_count, 1)
    keys_new = rotate(mixed_own[:, :, :, 1], own_positions).astype(jnp.bfloat16)
    values_new = mixed_own[:, :, :, 2].astype(jnp.bfloat16)

    chosen = queries_all[:, gather_rows]
    head_scores = [
        jnp.einsum(
            "zsbd,std->zsbt",
            chosen[:, :, :, head],
            cache_keys[:, :, head * HD : (head + 1) * HD],
            preferred_element_type=jnp.float32,
        )
        for head in range(head_count)
    ]
    scores = jnp.stack(head_scores, axis=3) * scale
    masked = jnp.where(live_wide, scores, NEG_FILL)
    slot_top = jnp.max(masked, axis=4)
    weights = jnp.where(live_wide, jnp.exp(masked - slot_top[..., None]), 0.0)
    slot_total = jnp.sum(weights, axis=4)
    rounded = weights.astype(jnp.bfloat16)
    slot_out = jnp.stack(
        [
            jnp.einsum(
                "zsbt,std->zsbd",
                rounded[:, :, :, head],
                cache_values[:, :, head * HD : (head + 1) * HD],
                preferred_element_type=jnp.float32,
            )
            for head in range(head_count)
        ],
        axis=3,
    )
    request_top = jnp.max(
        jnp.where(owner_mask[None, :, :, None, None], slot_top[:, :, None], NEG_FILL), axis=1
    )
    factor = jnp.exp(slot_top - request_top[:, valid_owner])
    page_total = jnp.einsum(
        "sr,zsbh->zrbh", owner_float, slot_total * factor, precision=highest
    ).reshape(steps, beam_total, head_count)
    page_out = jnp.einsum(
        "sr,zsbhd->zrbhd", owner_float, slot_out * factor[..., None], precision=highest
    ).reshape(steps, beam_total, head_count, HD)
    page_top = request_top.reshape(steps, beam_total, head_count)
    global_top = lax.pmax(page_top, "req")
    rescale = jnp.exp(page_top - global_top)
    partial = jnp.concatenate(
        [page_out * rescale[..., None], (page_total * rescale)[..., None]], axis=-1
    )
    own_partial = lax.psum_scatter(
        partial.astype(jnp.bfloat16), "req", scatter_dimension=1, tiled=True
    ).astype(jnp.float32)
    own_top = lax.dynamic_slice_in_dim(global_top, offset, own_count, 1)
    own_out = own_partial[..., :HD]
    own_total = own_partial[..., HD]

    source = own_group * BEAM + parents[0]
    attended_steps = []
    for step_index in range(steps):
        tail_keys = [keys_new[prior][source] for prior in range(step_index)]
        tail_values = [values_new[prior][source] for prior in range(step_index)]
        history_keys = jnp.stack(tail_keys + [keys_new[step_index]], axis=0)
        history_values = jnp.stack(tail_values + [values_new[step_index]], axis=0)
        own_scores = (
            jnp.einsum(
                "bhd,nbhd->bhn",
                queries_own[step_index],
                history_keys,
                preferred_element_type=jnp.float32,
            )
            * scale
        )
        top = jnp.maximum(own_top[step_index], jnp.max(own_scores, axis=2))
        page_factor = jnp.exp(own_top[step_index] - top)
        own_weights = jnp.exp(own_scores - top[..., None])
        total = own_total[step_index] * page_factor + jnp.sum(own_weights, axis=2)
        summed = own_out[step_index] * page_factor[..., None] + jnp.einsum(
            "bhn,nbhd->bhd",
            own_weights.astype(jnp.bfloat16),
            history_values,
            preferred_element_type=jnp.float32,
        )
        attended_steps.append(
            (summed / total[..., None]).astype(jnp.bfloat16).reshape(own_count, head_count * HD)
        )
    attended = jnp.stack(attended_steps)
    attended_all = lax.all_gather(attended, "req", axis=1, tiled=True)
    attended_msi = (
        attended_all.reshape(steps, mlp_size, local_rows, -1)
        .transpose(1, 0, 2, 3)
        .reshape(steps * beam_total, -1)
    )
    update_partial = (
        jnp.dot(attended_msi, dense_weight, preferred_element_type=jnp.float32)
        + jnp.dot(activated_all, down_weight, preferred_element_type=jnp.float32)
    ).astype(jnp.bfloat16)
    update = jnp.sum(
        exchange(
            update_partial.reshape(mlp_size, steps * local_rows, local_width),
            "mlp",
            mlp_size,
            False,
            1,
        ).astype(jnp.float32),
        axis=0,
    )
    layer = (block + update.reshape(steps, local_rows, local_width)).astype(jnp.bfloat16)
    next_in = (row_normalize(layer.astype(jnp.float32)) * norm_gains[2]).astype(jnp.bfloat16)
    gathered = exchange(next_in, "mlp", mlp_size, True, 2).reshape(steps * beam_total, -1)
    next_partial = jnp.dot(gathered, next_weight, preferred_element_type=jnp.float32)
    next_out = lax.psum_scatter(
        next_partial.astype(jnp.bfloat16), "req", scatter_dimension=0, tiled=True
    )
    next_out = (
        next_out.reshape(per_own, steps, local_rows, -1)
        .transpose(1, 0, 2, 3)
        .reshape(steps, own_count, -1)
    )
    return (layer, next_out)


def solution(mesh):
    in_specs = (
        P(None, "mlp", "req"),
        P(None, "req"),
        P("req", "mlp"),
        P("req", "mlp"),
        P("mlp", "req"),
        P("mlp", "req"),
        P("req", "mlp"),
        P("req", None, "mlp"),
        P("req", None, "mlp"),
        P(),
        P(None, "req"),
        P(None, "req"),
    )
    out_specs = (P(None, "mlp", "req"), P(None, "req", "mlp"))
    return jax.shard_map(shards, mesh=mesh, in_specs=in_specs, out_specs=out_specs, check_vma=False)
```

```python
import functools
import math

import jax
import jax.numpy as jnp
from jax import lax
from jax.experimental import pallas as pl
from jax.experimental.pallas import tpu as pltpu
from jax.sharding import PartitionSpec as P

MESH = pl.DeviceIdType.MESH

HD = 128
ROT = 32
PAGE = 128
BEAM = 8
STEPS = 2


NEG_FILL = -1e30
EPSILON = 1e-05


def rotate(vectors, positions):
    half = ROT // 2
    freq = jnp.exp(jnp.arange(half, dtype=jnp.float32) * (-2.0 * math.log(10000.0) / ROT))
    angles = positions.astype(jnp.float32)[..., None] * freq
    cosine = jnp.concatenate([jnp.cos(angles), jnp.cos(angles)], axis=-1)[..., None, :]
    sine = jnp.concatenate([jnp.sin(angles), jnp.sin(angles)], axis=-1)[..., None, :]
    turned = vectors[..., :ROT]
    swapped = jnp.concatenate([-turned[..., half:], turned[..., :half]], axis=-1)
    return jnp.concatenate([turned * cosine + swapped * sine, vectors[..., ROT:]], axis=-1)


def exchange_kernel(axis, n, gather, x_ref, out_ref, send_sem, recv_sem, local_sem):
    me = lax.axis_index(axis)
    barrier = pltpu.get_barrier_semaphore()
    for k in range(1, n):
        pl.semaphore_signal(
            barrier, inc=1, device_id={axis: lax.rem(me + k, n)}, device_id_type=MESH
        )
    pl.semaphore_wait(barrier, n - 1)
    local = pltpu.make_async_copy(x_ref if gather else x_ref.at[me], out_ref.at[me], local_sem)
    local.start()
    copies = []
    for k in range(1, n):
        dest = lax.rem(me + k, n)
        copy = pltpu.make_async_remote_copy(
            src_ref=x_ref if gather else x_ref.at[dest],
            dst_ref=out_ref.at[me],
            send_sem=send_sem.at[k],
            recv_sem=recv_sem.at[k],
            device_id={axis: dest},
            device_id_type=MESH,
        )
        copy.start()
        copies.append(copy)
    for copy in copies:
        copy.wait()
    local.wait()


def exchange(x, axis, n, gather, collective_id):
    shape = (n,) + (x.shape if gather else x.shape[1:])
    return pl.pallas_call(
        functools.partial(exchange_kernel, axis, n, gather),
        out_shape=jax.ShapeDtypeStruct(shape, x.dtype),
        in_specs=[pl.BlockSpec(memory_space=pltpu.VMEM)],
        out_specs=pl.BlockSpec(memory_space=pltpu.VMEM),
        scratch_shapes=[
            pltpu.SemaphoreType.DMA((n,)),
            pltpu.SemaphoreType.DMA((n,)),
            pltpu.SemaphoreType.DMA(()),
        ],
        compiler_params=pltpu.CompilerParams(
            collective_id=collective_id, has_side_effects=True
        ),
    )(x)


def exchange_flat(x, axis, n, gather, collective_id):
    lead = () if gather else x.shape[:1]
    block_shape = x.shape if gather else x.shape[1:]
    size = math.prod(block_shape)
    padded = -(-size // 128) * 128
    flat = x.reshape(lead + (size,))
    flat = jnp.pad(flat, [(0, 0)] * len(lead) + [(0, padded - size)])
    flat = flat.reshape(lead + (padded // 128, 128))
    out = exchange(flat, axis, n, gather, collective_id)
    return out.reshape(n, padded)[:, :size].reshape((n,) + block_shape)


def row_normalize(values, collective_id):
    width = values.shape[-1]
    local_mean = jnp.mean(values, axis=-1)
    centred = values - local_mean[..., None]
    local_m2 = jnp.sum(centred * centred, axis=-1)
    stats = jnp.stack([local_mean, local_m2], axis=0)
    stats = exchange_flat(stats, "req", lax.axis_size("req"), True, collective_id)
    stats = jnp.moveaxis(stats, 1, -1)
    means = stats[..., 0]
    row_mean = jnp.mean(means, axis=0)
    spread = means - row_mean
    row_m2 = jnp.sum(stats[..., 1], axis=0) + width * jnp.sum(spread * spread, axis=0)
    row_var = row_m2 / (width * stats.shape[0])
    return (values - row_mean[..., None]) * lax.rsqrt(row_var + EPSILON)[..., None]


def shards(
    inputs,
    norm_gains,
    attn_weight,
    up_weight,
    dense_weight,
    down_weight,
    next_weight,
    cache_keys,
    cache_values,
    lengths,
    slot_table,
    parents,
):
    scale = 1.0 / math.sqrt(HD)
    highest = lax.Precision.HIGHEST
    steps, local_rows, local_width = inputs.shape
    own_count = parents.shape[1]
    request_count = lengths.shape[0]
    beam_total = request_count * BEAM
    head_count = dense_weight.shape[0] // HD
    triple_width = attn_weight.shape[1]
    slot_count = slot_table.shape[1]
    req_size = beam_total // own_count
    mlp_size = beam_total // local_rows
    offset = lax.axis_index("req") * own_count
    beam_group = jnp.arange(beam_total, dtype=jnp.int32) // BEAM
    all_positions = lengths[beam_group][None, :] + jnp.arange(steps, dtype=jnp.int32)[:, None]
    own_group = jnp.arange(own_count, dtype=jnp.int32) // BEAM
    slot_owner = slot_table[0]
    slot_pageno = slot_table[1]
    valid_owner = jnp.maximum(slot_owner, 0)
    token_pos = slot_pageno[:, None] * PAGE + jnp.arange(PAGE, dtype=jnp.int32)[None, :]
    live = (slot_owner[:, None] >= 0) & (token_pos < lengths[valid_owner][:, None])
    live_wide = live[None, :, None, None, :]
    owner_mask = slot_owner[:, None] == jnp.arange(request_count, dtype=jnp.int32)[None, :]
    owner_float = owner_mask.astype(jnp.float32)
    gather_rows = valid_owner[:, None] * BEAM + jnp.arange(BEAM, dtype=jnp.int32)[None, :]

    block = inputs.astype(jnp.float32)
    rows_all = exchange(inputs, "mlp", mlp_size, True, 0).reshape(steps * beam_total, -1)
    normed = row_normalize(rows_all.astype(jnp.float32), 3)
    attn_in = (normed * norm_gains[0]).astype(jnp.bfloat16)
    mlp_in = (normed * norm_gains[1]).astype(jnp.bfloat16)
    piece = jnp.concatenate([attn_in, mlp_in], axis=-1)
    first = jnp.dot(piece[:, :local_width], attn_weight, preferred_element_type=jnp.float32)
    second = jnp.dot(piece[:, local_width:], up_weight, preferred_element_type=jnp.float32)
    partial_sums = jnp.concatenate([first, second], axis=1)
    summed_all = lax.psum(partial_sums.astype(jnp.bfloat16), "req").astype(jnp.float32)
    mixed_msi = summed_all[:, :triple_width].reshape(
        mlp_size, steps, local_rows, head_count, 3, HD
    )
    activated_all = jax.nn.gelu(summed_all[:, triple_width:], approximate=False).astype(
        jnp.bfloat16
    )
    mixed_all = mixed_msi[:, :, :, :, 0].transpose(1, 0, 2, 3, 4).reshape(
        steps, beam_total, head_count, HD
    )
    queries_all = rotate(mixed_all, all_positions).astype(jnp.bfloat16)
    per_own = own_count // local_rows
    mixed_own = (
        lax.dynamic_slice_in_dim(mixed_msi, lax.axis_index("req") * per_own, per_own, 0)
        .transpose(1, 0, 2, 3, 4, 5)
        .reshape(steps, own_count, head_count, 3, HD)
    )
    own_positions = lax.dynamic_slice_in_dim(all_positions, offset, own_count, 1)
    queries_own = lax.dynamic_slice_in_dim(queries_all, offset, own_count, 1)
    keys_new = rotate(mixed_own[:, :, :, 1], own_positions).astype(jnp.bfloat16)
    values_new = mixed_own[:, :, :, 2].astype(jnp.bfloat16)

    chosen = queries_all[:, gather_rows]
    head_scores = [
        jnp.einsum(
            "zsbd,std->zsbt",
            chosen[:, :, :, head],
            cache_keys[:, :, head * HD : (head + 1) * HD],
            preferred_element_type=jnp.float32,
        )
        for head in range(head_count)
    ]
    scores = jnp.stack(head_scores, axis=3) * scale
    masked = jnp.where(live_wide, scores, NEG_FILL)
    slot_top = jnp.max(masked, axis=4)
    weights = jnp.where(live_wide, jnp.exp(masked - slot_top[..., None]), 0.0)
    slot_total = jnp.sum(weights, axis=4)
    rounded = weights.astype(jnp.bfloat16)
    slot_out = jnp.stack(
        [
            jnp.einsum(
                "zsbt,std->zsbd",
                rounded[:, :, :, head],
                cache_values[:, :, head * HD : (head + 1) * HD],
                preferred_element_type=jnp.float32,
            )
            for head in range(head_count)
        ],
        axis=3,
    )
    request_top = jnp.max(
        jnp.where(owner_mask[None, :, :, None, None], slot_top[:, :, None], NEG_FILL), axis=1
    )
    top_high = request_top.astype(jnp.bfloat16)
    top_low = (request_top - top_high.astype(jnp.float32)).astype(jnp.bfloat16)
    request_top = top_high.astype(jnp.float32) + top_low.astype(jnp.float32)
    factor = jnp.where(
        slot_owner[None, :, None, None] >= 0,
        jnp.exp(slot_top - request_top[:, valid_owner]),
        0.0,
    )
    page_total = jnp.einsum(
        "sr,zsbh->zrbh", owner_float, slot_total * factor, precision=highest
    ).reshape(steps, beam_total, head_count)
    page_out = jnp.einsum(
        "sr,zsbhd->zrbhd", owner_float, slot_out * factor[..., None], precision=highest
    ).reshape(steps, beam_total, head_count, HD)
    packed = jnp.concatenate(
        [
            page_out.astype(jnp.bfloat16),
            page_total.astype(jnp.bfloat16)[..., None],
            top_high.reshape(steps, beam_total, head_count, 1),
            top_low.reshape(steps, beam_total, head_count, 1),
        ],
        axis=-1,
    )
    packed = packed.reshape(steps, req_size, own_count, head_count, HD + 3).transpose(
        1, 0, 2, 3, 4
    )
    held = exchange_flat(packed, "req", req_size, False, 5).astype(jnp.float32)
    held_top = held[..., HD + 1] + held[..., HD + 2]
    own_top = jnp.max(held_top, axis=0)
    rescale = jnp.exp(held_top - own_top)
    own_out = jnp.sum(held[..., :HD] * rescale[..., None], axis=0)
    own_total = jnp.sum(held[..., HD] * rescale, axis=0)

    source = own_group * BEAM + parents[0]
    attended_steps = []
    for step_index in range(steps):
        tail_keys = [keys_new[prior][source] for prior in range(step_index)]
        tail_values = [values_new[prior][source] for prior in range(step_index)]
        history_keys = jnp.stack(tail_keys + [keys_new[step_index]], axis=0)
        history_values = jnp.stack(tail_values + [values_new[step_index]], axis=0)
        own_scores = (
            jnp.einsum(
                "bhd,nbhd->bhn",
                queries_own[step_index],
                history_keys,
                preferred_element_type=jnp.float32,
            )
            * scale
        )
        top = jnp.maximum(own_top[step_index], jnp.max(own_scores, axis=2))
        page_factor = jnp.exp(own_top[step_index] - top)
        own_weights = jnp.exp(own_scores - top[..., None])
        total = own_total[step_index] * page_factor + jnp.sum(own_weights, axis=2)
        summed = own_out[step_index] * page_factor[..., None] + jnp.einsum(
            "bhn,nbhd->bhd",
            own_weights.astype(jnp.bfloat16),
            history_values,
            preferred_element_type=jnp.float32,
        )
        attended_steps.append(
            (summed / total[..., None]).astype(jnp.bfloat16).reshape(own_count, head_count * HD)
        )
    attended = jnp.stack(attended_steps)
    attended_all = exchange(attended, "req", req_size, True, 6)
    attended_msi = (
        attended_all.reshape(req_size, steps, per_own, local_rows, -1)
        .transpose(0, 2, 1, 3, 4)
        .reshape(steps * beam_total, -1)
    )
    update_partial = (
        jnp.dot(attended_msi, dense_weight, preferred_element_type=jnp.float32)
        + jnp.dot(activated_all, down_weight, preferred_element_type=jnp.float32)
    ).astype(jnp.bfloat16)
    update = jnp.sum(
        exchange(
            update_partial.reshape(mlp_size, steps * local_rows, local_width),
            "mlp",
            mlp_size,
            False,
            1,
        ).astype(jnp.float32),
        axis=0,
    )
    layer = (block + update.reshape(steps, local_rows, local_width)).astype(jnp.bfloat16)
    next_in = (row_normalize(layer.astype(jnp.float32), 4) * norm_gains[2]).astype(jnp.bfloat16)
    gathered = exchange(next_in, "mlp", mlp_size, True, 2).reshape(steps * beam_total, -1)
    next_partial = jnp.dot(gathered, next_weight, preferred_element_type=jnp.float32)
    next_out = lax.psum_scatter(
        next_partial.astype(jnp.bfloat16), "req", scatter_dimension=0, tiled=True
    )
    next_out = (
        next_out.reshape(per_own, steps, local_rows, -1)
        .transpose(1, 0, 2, 3)
        .reshape(steps, own_count, -1)
    )
    return (layer, next_out)


def solution(mesh):
    in_specs = (
        P(None, "mlp", "req"),
        P(None, "req"),
        P("req", "mlp"),
        P("req", "mlp"),
        P("mlp", "req"),
        P("mlp", "req"),
        P("req", "mlp"),
        P("req", None, "mlp"),
        P("req", None, "mlp"),
        P(),
        P(None, "req"),
        P(None, "req"),
    )
    out_specs = (P(None, "mlp", "req"), P(None, "req", "mlp"))
    return jax.shard_map(shards, mesh=mesh, in_specs=in_specs, out_specs=out_specs, check_vma=False)
```

```python
import functools
import math

import jax
import jax.numpy as jnp
from jax import lax
from jax.experimental import pallas as pl
from jax.experimental.pallas import tpu as pltpu
from jax.sharding import PartitionSpec as P

MESH = pl.DeviceIdType.MESH

HD = 128
ROT = 32
PAGE = 128
BEAM = 8
STEPS = 2


NEG_FILL = -1e30
EPSILON = 1e-05


def rotate(vectors, positions):
    half = ROT // 2
    freq = jnp.exp(jnp.arange(half, dtype=jnp.float32) * (-2.0 * math.log(10000.0) / ROT))
    angles = positions.astype(jnp.float32)[..., None] * freq
    cosine = jnp.concatenate([jnp.cos(angles), jnp.cos(angles)], axis=-1)[..., None, :]
    sine = jnp.concatenate([jnp.sin(angles), jnp.sin(angles)], axis=-1)[..., None, :]
    turned = vectors[..., :ROT]
    swapped = jnp.concatenate([-turned[..., half:], turned[..., :half]], axis=-1)
    return jnp.concatenate([turned * cosine + swapped * sine, vectors[..., ROT:]], axis=-1)


def exchange_kernel(axis, n, gather, x_ref, out_ref, send_sem, recv_sem, local_sem):
    me = lax.axis_index(axis)
    barrier = pltpu.get_barrier_semaphore()
    for k in range(1, n):
        pl.semaphore_signal(
            barrier, inc=1, device_id={axis: lax.rem(me + k, n)}, device_id_type=MESH
        )
    pl.semaphore_wait(barrier, n - 1)
    local = pltpu.make_async_copy(x_ref if gather else x_ref.at[me], out_ref.at[me], local_sem)
    local.start()
    copies = []
    for k in range(1, n):
        dest = lax.rem(me + k, n)
        copy = pltpu.make_async_remote_copy(
            src_ref=x_ref if gather else x_ref.at[dest],
            dst_ref=out_ref.at[me],
            send_sem=send_sem.at[k],
            recv_sem=recv_sem.at[k],
            device_id={axis: dest},
            device_id_type=MESH,
        )
        copy.start()
        copies.append(copy)
    for copy in copies:
        copy.wait()
    local.wait()


def exchange(x, axis, n, gather, collective_id):
    shape = (n,) + (x.shape if gather else x.shape[1:])
    return pl.pallas_call(
        functools.partial(exchange_kernel, axis, n, gather),
        out_shape=jax.ShapeDtypeStruct(shape, x.dtype),
        in_specs=[pl.BlockSpec(memory_space=pltpu.VMEM)],
        out_specs=pl.BlockSpec(memory_space=pltpu.VMEM),
        scratch_shapes=[
            pltpu.SemaphoreType.DMA((n,)),
            pltpu.SemaphoreType.DMA((n,)),
            pltpu.SemaphoreType.DMA(()),
        ],
        compiler_params=pltpu.CompilerParams(
            collective_id=collective_id, has_side_effects=True
        ),
        cost_estimate=pl.CostEstimate(
            flops=0, transcendentals=0, bytes_accessed=2 * n * x.size * x.dtype.itemsize
        ),
    )(x)


def exchange_flat(x, axis, n, gather, collective_id):
    lead = () if gather else x.shape[:1]
    block_shape = x.shape if gather else x.shape[1:]
    size = math.prod(block_shape)
    padded = -(-size // 128) * 128
    flat = x.reshape(lead + (size,))
    flat = jnp.pad(flat, [(0, 0)] * len(lead) + [(0, padded - size)])
    flat = flat.reshape(lead + (padded // 128, 128))
    out = exchange(flat, axis, n, gather, collective_id)
    return out.reshape(n, padded)[:, :size].reshape((n,) + block_shape)


def row_normalize(values, collective_id):
    width = values.shape[-1]
    local_mean = jnp.mean(values, axis=-1)
    centred = values - local_mean[..., None]
    local_m2 = jnp.sum(centred * centred, axis=-1)
    stats = jnp.stack([local_mean, local_m2], axis=0)
    stats = exchange_flat(stats, "req", lax.axis_size("req"), True, collective_id)
    stats = jnp.moveaxis(stats, 1, -1)
    means = stats[..., 0]
    row_mean = jnp.mean(means, axis=0)
    spread = means - row_mean
    row_m2 = jnp.sum(stats[..., 1], axis=0) + width * jnp.sum(spread * spread, axis=0)
    row_var = row_m2 / (width * stats.shape[0])
    return (values - row_mean[..., None]) * lax.rsqrt(row_var + EPSILON)[..., None]


def shards(
    inputs,
    norm_gains,
    attn_weight,
    up_weight,
    dense_weight,
    down_weight,
    next_weight,
    cache_keys,
    cache_values,
    lengths,
    slot_table,
    parents,
):
    scale = 1.0 / math.sqrt(HD)
    highest = lax.Precision.HIGHEST
    steps, local_rows, local_width = inputs.shape
    own_count = parents.shape[1]
    request_count = lengths.shape[0]
    beam_total = request_count * BEAM
    head_count = dense_weight.shape[0] // HD
    triple_width = attn_weight.shape[1]
    slot_count = slot_table.shape[1]
    req_size = beam_total // own_count
    mlp_size = beam_total // local_rows
    offset = lax.axis_index("req") * own_count
    beam_group = jnp.arange(beam_total, dtype=jnp.int32) // BEAM
    all_positions = lengths[beam_group][None, :] + jnp.arange(steps, dtype=jnp.int32)[:, None]
    own_group = jnp.arange(own_count, dtype=jnp.int32) // BEAM
    slot_owner = slot_table[0]
    slot_pageno = slot_table[1]
    valid_owner = jnp.maximum(slot_owner, 0)
    token_pos = slot_pageno[:, None] * PAGE + jnp.arange(PAGE, dtype=jnp.int32)[None, :]
    live = (slot_owner[:, None] >= 0) & (token_pos < lengths[valid_owner][:, None])
    live_wide = live[None, :, None, None, :]
    owner_mask = slot_owner[:, None] == jnp.arange(request_count, dtype=jnp.int32)[None, :]
    owner_float = owner_mask.astype(jnp.float32)
    gather_rows = valid_owner[:, None] * BEAM + jnp.arange(BEAM, dtype=jnp.int32)[None, :]

    block = inputs.astype(jnp.float32)
    rows_all = exchange(inputs, "mlp", mlp_size, True, 0).reshape(steps * beam_total, -1)
    normed = row_normalize(rows_all.astype(jnp.float32), 3)
    attn_in = (normed * norm_gains[0]).astype(jnp.bfloat16)
    mlp_in = (normed * norm_gains[1]).astype(jnp.bfloat16)
    first = jnp.dot(attn_in, attn_weight, preferred_element_type=jnp.float32)
    second = jnp.dot(mlp_in, up_weight, preferred_element_type=jnp.float32)
    mixed_sum = lax.psum(first.astype(jnp.bfloat16), "req")
    mixed_sum, second = lax.optimization_barrier((mixed_sum, second.astype(jnp.bfloat16)))
    hidden_sum = lax.psum(second, "req")
    mixed_msi = mixed_sum.astype(jnp.float32).reshape(
        mlp_size, steps, local_rows, head_count, 3, HD
    )
    activated_all = jax.nn.gelu(hidden_sum.astype(jnp.float32), approximate=False).astype(
        jnp.bfloat16
    )
    mixed_all = mixed_msi[:, :, :, :, 0].transpose(1, 0, 2, 3, 4).reshape(
        steps, beam_total, head_count, HD
    )
    queries_all = rotate(mixed_all, all_positions).astype(jnp.bfloat16)
    per_own = own_count // local_rows
    mixed_own = (
        lax.dynamic_slice_in_dim(mixed_msi, lax.axis_index("req") * per_own, per_own, 0)
        .transpose(1, 0, 2, 3, 4, 5)
        .reshape(steps, own_count, head_count, 3, HD)
    )
    own_positions = lax.dynamic_slice_in_dim(all_positions, offset, own_count, 1)
    queries_own = lax.dynamic_slice_in_dim(queries_all, offset, own_count, 1)
    keys_new = rotate(mixed_own[:, :, :, 1], own_positions).astype(jnp.bfloat16)
    values_new = mixed_own[:, :, :, 2].astype(jnp.bfloat16)

    chosen = queries_all[:, gather_rows]
    head_scores = [
        jnp.einsum(
            "zsbd,std->zsbt",
            chosen[:, :, :, head],
            cache_keys[:, :, head * HD : (head + 1) * HD],
            preferred_element_type=jnp.float32,
        )
        for head in range(head_count)
    ]
    scores = jnp.stack(head_scores, axis=3) * scale
    masked = jnp.where(live_wide, scores, NEG_FILL)
    slot_top = jnp.max(masked, axis=4)
    weights = jnp.where(live_wide, jnp.exp(masked - slot_top[..., None]), 0.0)
    slot_total = jnp.sum(weights, axis=4)
    rounded = weights.astype(jnp.bfloat16)
    slot_out = jnp.stack(
        [
            jnp.einsum(
                "zsbt,std->zsbd",
                rounded[:, :, :, head],
                cache_values[:, :, head * HD : (head + 1) * HD],
                preferred_element_type=jnp.float32,
            )
            for head in range(head_count)
        ],
        axis=3,
    )
    request_top = jnp.max(
        jnp.where(owner_mask[None, :, :, None, None], slot_top[:, :, None], NEG_FILL), axis=1
    )
    top_high = request_top.astype(jnp.bfloat16)
    top_low = (request_top - top_high.astype(jnp.float32)).astype(jnp.bfloat16)
    request_top = top_high.astype(jnp.float32) + top_low.astype(jnp.float32)
    factor = jnp.where(
        slot_owner[None, :, None, None] >= 0,
        jnp.exp(slot_top - request_top[:, valid_owner]),
        0.0,
    )
    page_total = jnp.einsum(
        "sr,zsbh->zrbh", owner_float, slot_total * factor, precision=highest
    ).reshape(steps, beam_total, head_count)
    page_out = jnp.einsum(
        "sr,zsbhd->zrbhd", owner_float, slot_out * factor[..., None], precision=highest
    ).reshape(steps, beam_total, head_count, HD)
    packed = jnp.concatenate(
        [
            page_out.astype(jnp.bfloat16),
            page_total.astype(jnp.bfloat16)[..., None],
            top_high.reshape(steps, beam_total, head_count, 1),
            top_low.reshape(steps, beam_total, head_count, 1),
        ],
        axis=-1,
    )
    packed = packed.reshape(steps, req_size, own_count, head_count, HD + 3).transpose(
        1, 0, 2, 3, 4
    )
    held = exchange_flat(packed, "req", req_size, False, 5).astype(jnp.float32)
    held_top = held[..., HD + 1] + held[..., HD + 2]
    own_top = jnp.max(held_top, axis=0)
    rescale = jnp.exp(held_top - own_top)
    own_out = jnp.sum(held[..., :HD] * rescale[..., None], axis=0)
    own_total = jnp.sum(held[..., HD] * rescale, axis=0)

    source = own_group * BEAM + parents[0]
    attended_steps = []
    for step_index in range(steps):
        tail_keys = [keys_new[prior][source] for prior in range(step_index)]
        tail_values = [values_new[prior][source] for prior in range(step_index)]
        history_keys = jnp.stack(tail_keys + [keys_new[step_index]], axis=0)
        history_values = jnp.stack(tail_values + [values_new[step_index]], axis=0)
        own_scores = (
            jnp.einsum(
                "bhd,nbhd->bhn",
                queries_own[step_index],
                history_keys,
                preferred_element_type=jnp.float32,
            )
            * scale
        )
        top = jnp.maximum(own_top[step_index], jnp.max(own_scores, axis=2))
        page_factor = jnp.exp(own_top[step_index] - top)
        own_weights = jnp.exp(own_scores - top[..., None])
        total = own_total[step_index] * page_factor + jnp.sum(own_weights, axis=2)
        summed = own_out[step_index] * page_factor[..., None] + jnp.einsum(
            "bhn,nbhd->bhd",
            own_weights.astype(jnp.bfloat16),
            history_values,
            preferred_element_type=jnp.float32,
        )
        attended_steps.append(
            (summed / total[..., None]).astype(jnp.bfloat16).reshape(own_count, head_count * HD)
        )
    attended = jnp.stack(attended_steps)
    attended_all = exchange(attended, "req", req_size, True, 6)
    attended_msi = (
        attended_all.reshape(req_size, steps, per_own, local_rows, -1)
        .transpose(0, 2, 1, 3, 4)
        .reshape(steps * beam_total, -1)
    )
    update_partial = (
        jnp.dot(attended_msi, dense_weight, preferred_element_type=jnp.float32)
        + jnp.dot(activated_all, down_weight, preferred_element_type=jnp.float32)
    ).astype(jnp.bfloat16)
    update = jnp.sum(
        exchange(
            update_partial.reshape(mlp_size, steps * local_rows, local_width),
            "mlp",
            mlp_size,
            False,
            1,
        ).astype(jnp.float32),
        axis=0,
    )
    layer = (block + update.reshape(steps, local_rows, local_width)).astype(jnp.bfloat16)
    next_in = (row_normalize(layer.astype(jnp.float32), 4) * norm_gains[2]).astype(jnp.bfloat16)
    gathered = exchange(next_in, "mlp", mlp_size, True, 2).reshape(steps * beam_total, -1)
    next_partial = jnp.dot(gathered, next_weight, preferred_element_type=jnp.float32)
    next_out = lax.psum_scatter(
        next_partial.astype(jnp.bfloat16), "req", scatter_dimension=0, tiled=True
    )
    next_out = (
        next_out.reshape(per_own, steps, local_rows, -1)
        .transpose(1, 0, 2, 3)
        .reshape(steps, own_count, -1)
    )
    return (layer, next_out)


def solution(mesh):
    in_specs = (
        P(None, "mlp", "req"),
        P(None, "req"),
        P("req", "mlp"),
        P("req", "mlp"),
        P("mlp", "req"),
        P("mlp", "req"),
        P("req", "mlp"),
        P("req", None, "mlp"),
        P("req", None, "mlp"),
        P(),
        P(None, "req"),
        P(None, "req"),
    )
    out_specs = (P(None, "mlp", "req"), P(None, "req", "mlp"))
    return jax.shard_map(shards, mesh=mesh, in_specs=in_specs, out_specs=out_specs, check_vma=False)
```

```python
import functools
import math

import jax
import jax.numpy as jnp
from jax import lax
from jax.experimental import pallas as pl
from jax.experimental.pallas import tpu as pltpu
from jax.sharding import PartitionSpec as P

MESH = pl.DeviceIdType.MESH

HD = 128
ROT = 32
PAGE = 128
BEAM = 8
STEPS = 2


NEG_FILL = -1e30
EPSILON = 1e-05


def rotate(vectors, positions):
    half = ROT // 2
    freq = jnp.exp(jnp.arange(half, dtype=jnp.float32) * (-2.0 * math.log(10000.0) / ROT))
    angles = positions.astype(jnp.float32)[..., None] * freq
    cosine = jnp.concatenate([jnp.cos(angles), jnp.cos(angles)], axis=-1)[..., None, :]
    sine = jnp.concatenate([jnp.sin(angles), jnp.sin(angles)], axis=-1)[..., None, :]
    turned = vectors[..., :ROT]
    swapped = jnp.concatenate([-turned[..., half:], turned[..., :half]], axis=-1)
    return jnp.concatenate([turned * cosine + swapped * sine, vectors[..., ROT:]], axis=-1)


def rotate_rows(rows, positions, head_count):
    half = ROT // 2
    freq = jnp.exp(jnp.arange(half, dtype=jnp.float32) * (-2.0 * math.log(10000.0) / ROT))
    angles = positions.astype(jnp.float32)[:, None] * freq[None, :]
    cosine = jnp.concatenate([jnp.cos(angles), jnp.cos(angles)], axis=1)
    sine = jnp.concatenate([jnp.sin(angles), jnp.sin(angles)], axis=1)
    parts = []
    for head in range(head_count):
        base = head * HD
        turned = rows[:, base : base + ROT]
        swapped = jnp.concatenate([-turned[:, half:], turned[:, :half]], axis=1)
        parts += [turned * cosine + swapped * sine, rows[:, base + ROT : base + HD]]
    return jnp.concatenate(parts, axis=1)


def exchange_kernel(axis, n, gather, x_ref, out_ref, send_sem, recv_sem, local_sem):
    me = lax.axis_index(axis)
    barrier = pltpu.get_barrier_semaphore()
    for k in range(1, n):
        pl.semaphore_signal(
            barrier, inc=1, device_id={axis: lax.rem(me + k, n)}, device_id_type=MESH
        )
    pl.semaphore_wait(barrier, n - 1)
    local = pltpu.make_async_copy(x_ref if gather else x_ref.at[me], out_ref.at[me], local_sem)
    local.start()
    copies = []
    for k in range(1, n):
        dest = lax.rem(me + k, n)
        copy = pltpu.make_async_remote_copy(
            src_ref=x_ref if gather else x_ref.at[dest],
            dst_ref=out_ref.at[me],
            send_sem=send_sem.at[k],
            recv_sem=recv_sem.at[k],
            device_id={axis: dest},
            device_id_type=MESH,
        )
        copy.start()
        copies.append(copy)
    for copy in copies:
        copy.wait()
    local.wait()


def exchange(x, axis, n, gather, collective_id):
    shape = (n,) + (x.shape if gather else x.shape[1:])
    return pl.pallas_call(
        functools.partial(exchange_kernel, axis, n, gather),
        out_shape=jax.ShapeDtypeStruct(shape, x.dtype),
        in_specs=[pl.BlockSpec(memory_space=pltpu.VMEM)],
        out_specs=pl.BlockSpec(memory_space=pltpu.VMEM),
        scratch_shapes=[
            pltpu.SemaphoreType.DMA((n,)),
            pltpu.SemaphoreType.DMA((n,)),
            pltpu.SemaphoreType.DMA(()),
        ],
        compiler_params=pltpu.CompilerParams(
            collective_id=collective_id, has_side_effects=True
        ),
        cost_estimate=pl.CostEstimate(
            flops=0, transcendentals=0, bytes_accessed=2 * n * x.size * x.dtype.itemsize
        ),
    )(x)


def exchange_flat(x, axis, n, gather, collective_id):
    lead = () if gather else x.shape[:1]
    block_shape = x.shape if gather else x.shape[1:]
    size = math.prod(block_shape)
    padded = -(-size // 128) * 128
    flat = x.reshape(lead + (size,))
    flat = jnp.pad(flat, [(0, 0)] * len(lead) + [(0, padded - size)])
    flat = flat.reshape(lead + (padded // 128, 128))
    out = exchange(flat, axis, n, gather, collective_id)
    return out.reshape(n, padded)[:, :size].reshape((n,) + block_shape)


def row_normalize(values, collective_id):
    width = values.shape[-1]
    local_mean = jnp.mean(values, axis=-1)
    centred = values - local_mean[..., None]
    local_m2 = jnp.sum(centred * centred, axis=-1)
    stats = jnp.stack([local_mean, local_m2], axis=0)
    stats = exchange_flat(stats, "req", lax.axis_size("req"), True, collective_id)
    stats = jnp.moveaxis(stats, 1, -1)
    means = stats[..., 0]
    row_mean = jnp.mean(means, axis=0)
    spread = means - row_mean
    row_m2 = jnp.sum(stats[..., 1], axis=0) + width * jnp.sum(spread * spread, axis=0)
    row_var = row_m2 / (width * stats.shape[0])
    return (values - row_mean[..., None]) * lax.rsqrt(row_var + EPSILON)[..., None]


def shards(
    inputs,
    norm_gains,
    attn_weight,
    up_weight,
    dense_weight,
    down_weight,
    next_weight,
    cache_keys,
    cache_values,
    lengths,
    slot_table,
    parents,
):
    scale = 1.0 / math.sqrt(HD)
    highest = lax.Precision.HIGHEST
    steps, local_rows, local_width = inputs.shape
    own_count = parents.shape[1]
    request_count = lengths.shape[0]
    beam_total = request_count * BEAM
    head_count = dense_weight.shape[0] // HD
    triple_width = attn_weight.shape[1]
    slot_count = slot_table.shape[1]
    req_size = beam_total // own_count
    mlp_size = beam_total // local_rows
    offset = lax.axis_index("req") * own_count
    beam_group = jnp.arange(beam_total, dtype=jnp.int32) // BEAM
    all_positions = lengths[beam_group][None, :] + jnp.arange(steps, dtype=jnp.int32)[:, None]
    own_group = jnp.arange(own_count, dtype=jnp.int32) // BEAM
    slot_owner = slot_table[0]
    slot_pageno = slot_table[1]
    valid_owner = jnp.maximum(slot_owner, 0)
    token_pos = slot_pageno[:, None] * PAGE + jnp.arange(PAGE, dtype=jnp.int32)[None, :]
    live = (slot_owner[:, None] >= 0) & (token_pos < lengths[valid_owner][:, None])
    live_wide = live[None, :, None, None, :]
    owner_mask = slot_owner[:, None] == jnp.arange(request_count, dtype=jnp.int32)[None, :]
    owner_float = owner_mask.astype(jnp.float32)
    gather_rows = valid_owner[:, None] * BEAM + jnp.arange(BEAM, dtype=jnp.int32)[None, :]

    block = inputs.astype(jnp.float32)
    rows_all = exchange(inputs, "mlp", mlp_size, True, 0).reshape(steps * beam_total, -1)
    normed = row_normalize(rows_all.astype(jnp.float32), 3)
    attn_in = (normed * norm_gains[0]).astype(jnp.bfloat16)
    mlp_in = (normed * norm_gains[1]).astype(jnp.bfloat16)
    grouped = (
        attn_weight.reshape(local_width, head_count, 3, HD)
        .transpose(0, 2, 1, 3)
        .reshape(local_width, triple_width)
    )
    first = jnp.dot(attn_in, grouped, preferred_element_type=jnp.float32)
    second = jnp.dot(mlp_in, up_weight, preferred_element_type=jnp.float32)
    partial_sums = jnp.concatenate([first, second], axis=1)
    summed_all = lax.psum(partial_sums.astype(jnp.bfloat16), "req")
    width = head_count * HD
    activated_all = jax.nn.gelu(
        summed_all[:, triple_width:].astype(jnp.float32), approximate=False
    ).astype(jnp.bfloat16)
    row = jnp.arange(steps * beam_total, dtype=jnp.int32)
    row_beam = (row // (steps * local_rows)) * local_rows + row % local_rows
    row_positions = lengths[row_beam // BEAM] + (row // local_rows) % steps
    queries_rows = rotate_rows(
        summed_all[:, :width].astype(jnp.float32), row_positions, head_count
    ).astype(jnp.bfloat16)
    keys_rows = rotate_rows(
        summed_all[:, width : 2 * width].astype(jnp.float32), row_positions, head_count
    ).astype(jnp.bfloat16)
    per_own = own_count // local_rows
    own_start = lax.axis_index("req") * (per_own * steps * local_rows)

    def own_of(rows):
        return (
            lax.dynamic_slice_in_dim(rows, own_start, per_own * steps * local_rows, 0)
            .reshape(per_own, steps, local_rows, -1)
            .transpose(1, 0, 2, 3)
            .reshape(steps, own_count, head_count, HD)
        )

    queries_own = own_of(queries_rows)
    keys_new = own_of(keys_rows)
    values_new = own_of(summed_all[:, 2 * width : 3 * width])

    chosen_rows = (
        (gather_rows // local_rows) * (steps * local_rows)
        + jnp.arange(steps, dtype=jnp.int32)[:, None, None] * local_rows
        + gather_rows % local_rows
    )
    chosen = queries_rows[chosen_rows]
    head_scores = [
        jnp.einsum(
            "zsbd,std->zsbt",
            chosen[..., head * HD : (head + 1) * HD],
            cache_keys[:, :, head * HD : (head + 1) * HD],
            preferred_element_type=jnp.float32,
        )
        for head in range(head_count)
    ]
    scores = jnp.stack(head_scores, axis=3) * scale
    masked = jnp.where(live_wide, scores, NEG_FILL)
    slot_top = jnp.max(masked, axis=4)
    weights = jnp.where(live_wide, jnp.exp(masked - slot_top[..., None]), 0.0)
    slot_total = jnp.sum(weights, axis=4)
    rounded = weights.astype(jnp.bfloat16)
    slot_out = jnp.stack(
        [
            jnp.einsum(
                "zsbt,std->zsbd",
                rounded[:, :, :, head],
                cache_values[:, :, head * HD : (head + 1) * HD],
                preferred_element_type=jnp.float32,
            )
            for head in range(head_count)
        ],
        axis=3,
    )
    request_top = jnp.max(
        jnp.where(owner_mask[None, :, :, None, None], slot_top[:, :, None], NEG_FILL), axis=1
    )
    top_high = request_top.astype(jnp.bfloat16)
    top_low = (request_top - top_high.astype(jnp.float32)).astype(jnp.bfloat16)
    request_top = top_high.astype(jnp.float32) + top_low.astype(jnp.float32)
    factor = jnp.where(
        slot_owner[None, :, None, None] >= 0,
        jnp.exp(slot_top - request_top[:, valid_owner]),
        0.0,
    )
    page_total = jnp.einsum(
        "sr,zsbh->zrbh", owner_float, slot_total * factor, precision=highest
    ).reshape(steps, beam_total, head_count)
    page_out = jnp.einsum(
        "sr,zsbhd->zrbhd", owner_float, slot_out * factor[..., None], precision=highest
    ).reshape(steps, beam_total, head_count, HD)
    packed = jnp.concatenate(
        [
            page_out.astype(jnp.bfloat16),
            page_total.astype(jnp.bfloat16)[..., None],
            top_high.reshape(steps, beam_total, head_count, 1),
            top_low.reshape(steps, beam_total, head_count, 1),
        ],
        axis=-1,
    )
    packed = packed.reshape(steps, req_size, own_count, head_count, HD + 3).transpose(
        1, 0, 2, 3, 4
    )
    held = exchange_flat(packed, "req", req_size, False, 5).astype(jnp.float32)
    held_top = held[..., HD + 1] + held[..., HD + 2]
    own_top = jnp.max(held_top, axis=0)
    rescale = jnp.exp(held_top - own_top)
    own_out = jnp.sum(held[..., :HD] * rescale[..., None], axis=0)
    own_total = jnp.sum(held[..., HD] * rescale, axis=0)

    source = own_group * BEAM + parents[0]
    attended_steps = []
    for step_index in range(steps):
        tail_keys = [keys_new[prior][source] for prior in range(step_index)]
        tail_values = [values_new[prior][source] for prior in range(step_index)]
        history_keys = jnp.stack(tail_keys + [keys_new[step_index]], axis=0)
        history_values = jnp.stack(tail_values + [values_new[step_index]], axis=0)
        own_scores = (
            jnp.einsum(
                "bhd,nbhd->bhn",
                queries_own[step_index],
                history_keys,
                preferred_element_type=jnp.float32,
            )
            * scale
        )
        top = jnp.maximum(own_top[step_index], jnp.max(own_scores, axis=2))
        page_factor = jnp.exp(own_top[step_index] - top)
        own_weights = jnp.exp(own_scores - top[..., None])
        total = own_total[step_index] * page_factor + jnp.sum(own_weights, axis=2)
        summed = own_out[step_index] * page_factor[..., None] + jnp.einsum(
            "bhn,nbhd->bhd",
            own_weights.astype(jnp.bfloat16),
            history_values,
            preferred_element_type=jnp.float32,
        )
        attended_steps.append(
            (summed / total[..., None]).astype(jnp.bfloat16).reshape(own_count, head_count * HD)
        )
    attended = jnp.stack(attended_steps)
    attended_all = exchange(attended, "req", req_size, True, 6)
    attended_msi = (
        attended_all.reshape(req_size, steps, per_own, local_rows, -1)
        .transpose(0, 2, 1, 3, 4)
        .reshape(steps * beam_total, -1)
    )
    update_partial = (
        jnp.dot(attended_msi, dense_weight, preferred_element_type=jnp.float32)
        + jnp.dot(activated_all, down_weight, preferred_element_type=jnp.float32)
    ).astype(jnp.bfloat16)
    update = jnp.sum(
        exchange(
            update_partial.reshape(mlp_size, steps * local_rows, local_width),
            "mlp",
            mlp_size,
            False,
            1,
        ).astype(jnp.float32),
        axis=0,
    )
    layer = (block + update.reshape(steps, local_rows, local_width)).astype(jnp.bfloat16)
    next_in = (row_normalize(layer.astype(jnp.float32), 4) * norm_gains[2]).astype(jnp.bfloat16)
    gathered = exchange(next_in, "mlp", mlp_size, True, 2).reshape(steps * beam_total, -1)
    next_partial = jnp.dot(gathered, next_weight, preferred_element_type=jnp.float32)
    next_out = lax.psum_scatter(
        next_partial.astype(jnp.bfloat16), "req", scatter_dimension=0, tiled=True
    )
    next_out = (
        next_out.reshape(per_own, steps, local_rows, -1)
        .transpose(1, 0, 2, 3)
        .reshape(steps, own_count, -1)
    )
    return (layer, next_out)


def solution(mesh):
    in_specs = (
        P(None, "mlp", "req"),
        P(None, "req"),
        P("req", "mlp"),
        P("req", "mlp"),
        P("mlp", "req"),
        P("mlp", "req"),
        P("req", "mlp"),
        P("req", None, "mlp"),
        P("req", None, "mlp"),
        P(),
        P(None, "req"),
        P(None, "req"),
    )
    out_specs = (P(None, "mlp", "req"), P(None, "req", "mlp"))
    return jax.shard_map(shards, mesh=mesh, in_specs=in_specs, out_specs=out_specs, check_vma=False)
```

```python
import functools
import math

import jax
import jax.numpy as jnp
from jax import lax
from jax.experimental import pallas as pl
from jax.experimental.pallas import tpu as pltpu
from jax.sharding import PartitionSpec as P

MESH = pl.DeviceIdType.MESH

HD = 128
ROT = 32
PAGE = 128
BEAM = 8
STEPS = 2


NEG_FILL = -1e30
EPSILON = 1e-05


def rotate(vectors, positions):
    half = ROT // 2
    freq = jnp.exp(jnp.arange(half, dtype=jnp.float32) * (-2.0 * math.log(10000.0) / ROT))
    angles = positions.astype(jnp.float32)[..., None] * freq
    cosine = jnp.concatenate([jnp.cos(angles), jnp.cos(angles)], axis=-1)[..., None, :]
    sine = jnp.concatenate([jnp.sin(angles), jnp.sin(angles)], axis=-1)[..., None, :]
    turned = vectors[..., :ROT]
    swapped = jnp.concatenate([-turned[..., half:], turned[..., :half]], axis=-1)
    return jnp.concatenate([turned * cosine + swapped * sine, vectors[..., ROT:]], axis=-1)


def pick_rows(table, index):
    flat = table.reshape(table.shape[0], -1)
    hot = (index.reshape(-1)[:, None] == jnp.arange(table.shape[0], dtype=jnp.int32)[None, :])
    taken = jnp.dot(hot.astype(table.dtype), flat, preferred_element_type=jnp.float32)
    return taken.astype(table.dtype).reshape(index.shape + table.shape[1:])


def rotate_rows(rows, positions, head_count):
    half = ROT // 2
    freq = jnp.exp(jnp.arange(half, dtype=jnp.float32) * (-2.0 * math.log(10000.0) / ROT))
    angles = positions.astype(jnp.float32)[:, None] * freq[None, :]
    cosine = jnp.concatenate([jnp.cos(angles), jnp.cos(angles)], axis=1)
    sine = jnp.concatenate([jnp.sin(angles), jnp.sin(angles)], axis=1)
    parts = []
    for head in range(head_count):
        base = head * HD
        turned = rows[:, base : base + ROT]
        swapped = jnp.concatenate([-turned[:, half:], turned[:, :half]], axis=1)
        parts += [turned * cosine + swapped * sine, rows[:, base + ROT : base + HD]]
    return jnp.concatenate(parts, axis=1)


def exchange_kernel(axis, n, gather, x_ref, out_ref, send_sem, recv_sem, local_sem):
    me = lax.axis_index(axis)
    barrier = pltpu.get_barrier_semaphore()
    for k in range(1, n):
        pl.semaphore_signal(
            barrier, inc=1, device_id={axis: lax.rem(me + k, n)}, device_id_type=MESH
        )
    pl.semaphore_wait(barrier, n - 1)
    local = pltpu.make_async_copy(x_ref if gather else x_ref.at[me], out_ref.at[me], local_sem)
    local.start()
    copies = []
    for k in range(1, n):
        dest = lax.rem(me + k, n)
        copy = pltpu.make_async_remote_copy(
            src_ref=x_ref if gather else x_ref.at[dest],
            dst_ref=out_ref.at[me],
            send_sem=send_sem.at[k],
            recv_sem=recv_sem.at[k],
            device_id={axis: dest},
            device_id_type=MESH,
        )
        copy.start()
        copies.append(copy)
    for copy in copies:
        copy.wait()
    local.wait()


def exchange(x, axis, n, gather, collective_id):
    shape = (n,) + (x.shape if gather else x.shape[1:])
    return pl.pallas_call(
        functools.partial(exchange_kernel, axis, n, gather),
        out_shape=jax.ShapeDtypeStruct(shape, x.dtype),
        in_specs=[pl.BlockSpec(memory_space=pltpu.VMEM)],
        out_specs=pl.BlockSpec(memory_space=pltpu.VMEM),
        scratch_shapes=[
            pltpu.SemaphoreType.DMA((n,)),
            pltpu.SemaphoreType.DMA((n,)),
            pltpu.SemaphoreType.DMA(()),
        ],
        compiler_params=pltpu.CompilerParams(
            collective_id=collective_id, has_side_effects=True
        ),
        cost_estimate=pl.CostEstimate(
            flops=0, transcendentals=0, bytes_accessed=2 * n * x.size * x.dtype.itemsize
        ),
    )(x)


def exchange_flat(x, axis, n, gather, collective_id):
    lead = () if gather else x.shape[:1]
    block_shape = x.shape if gather else x.shape[1:]
    size = math.prod(block_shape)
    padded = -(-size // 128) * 128
    flat = x.reshape(lead + (size,))
    flat = jnp.pad(flat, [(0, 0)] * len(lead) + [(0, padded - size)])
    flat = flat.reshape(lead + (padded // 128, 128))
    out = exchange(flat, axis, n, gather, collective_id)
    return out.reshape(n, padded)[:, :size].reshape((n,) + block_shape)


def row_normalize(values, collective_id):
    width = values.shape[-1]
    local_mean = jnp.mean(values, axis=-1)
    centred = values - local_mean[..., None]
    local_m2 = jnp.sum(centred * centred, axis=-1)
    stats = jnp.stack([local_mean, local_m2], axis=0)
    stats = exchange_flat(stats, "req", lax.axis_size("req"), True, collective_id)
    stats = jnp.moveaxis(stats, 1, -1)
    means = stats[..., 0]
    row_mean = jnp.mean(means, axis=0)
    spread = means - row_mean
    row_m2 = jnp.sum(stats[..., 1], axis=0) + width * jnp.sum(spread * spread, axis=0)
    row_var = row_m2 / (width * stats.shape[0])
    return (values - row_mean[..., None]) * lax.rsqrt(row_var + EPSILON)[..., None]


def shards(
    inputs,
    norm_gains,
    attn_weight,
    up_weight,
    dense_weight,
    down_weight,
    next_weight,
    cache_keys,
    cache_values,
    lengths,
    slot_table,
    parents,
):
    scale = 1.0 / math.sqrt(HD)
    highest = lax.Precision.HIGHEST
    steps, local_rows, local_width = inputs.shape
    own_count = parents.shape[1]
    request_count = lengths.shape[0]
    beam_total = request_count * BEAM
    head_count = dense_weight.shape[0] // HD
    triple_width = attn_weight.shape[1]
    slot_count = slot_table.shape[1]
    req_size = beam_total // own_count
    mlp_size = beam_total // local_rows
    offset = lax.axis_index("req") * own_count
    beam_group = jnp.arange(beam_total, dtype=jnp.int32) // BEAM
    all_positions = lengths[beam_group][None, :] + jnp.arange(steps, dtype=jnp.int32)[:, None]
    own_group = jnp.arange(own_count, dtype=jnp.int32) // BEAM
    slot_owner = slot_table[0]
    slot_pageno = slot_table[1]
    valid_owner = jnp.maximum(slot_owner, 0)
    token_pos = slot_pageno[:, None] * PAGE + jnp.arange(PAGE, dtype=jnp.int32)[None, :]
    live = (slot_owner[:, None] >= 0) & (token_pos < lengths[valid_owner][:, None])
    live_wide = live[None, :, None, None, :]
    owner_mask = slot_owner[:, None] == jnp.arange(request_count, dtype=jnp.int32)[None, :]
    owner_float = owner_mask.astype(jnp.float32)
    gather_rows = valid_owner[:, None] * BEAM + jnp.arange(BEAM, dtype=jnp.int32)[None, :]

    block = inputs.astype(jnp.float32)
    rows_all = exchange(inputs, "mlp", mlp_size, True, 0).reshape(steps * beam_total, -1)
    normed = row_normalize(rows_all.astype(jnp.float32), 3)
    attn_in = (normed * norm_gains[0]).astype(jnp.bfloat16)
    mlp_in = (normed * norm_gains[1]).astype(jnp.bfloat16)
    grouped = (
        attn_weight.reshape(local_width, head_count, 3, HD)
        .transpose(0, 2, 1, 3)
        .reshape(local_width, triple_width)
    )
    first = jnp.dot(attn_in, grouped, preferred_element_type=jnp.float32)
    second = jnp.dot(mlp_in, up_weight, preferred_element_type=jnp.float32)
    partial_sums = jnp.concatenate([first, second], axis=1)
    summed_all = lax.psum(partial_sums.astype(jnp.bfloat16), "req")
    width = head_count * HD
    activated_all = lax.optimization_barrier(
        jax.nn.gelu(summed_all[:, triple_width:].astype(jnp.float32), approximate=False).astype(
            jnp.bfloat16
        )
    )
    row = jnp.arange(steps * beam_total, dtype=jnp.int32)
    beam_lengths = jnp.broadcast_to(lengths[:, None], (request_count, BEAM)).reshape(
        mlp_size, 1, local_rows
    )
    row_positions = (
        beam_lengths + jnp.arange(steps, dtype=jnp.int32)[None, :, None]
    ).reshape(steps * beam_total)
    queries_rows = rotate_rows(
        summed_all[:, :width].astype(jnp.float32), row_positions, head_count
    ).astype(jnp.bfloat16)
    keys_rows = rotate_rows(
        summed_all[:, width : 2 * width].astype(jnp.float32), row_positions, head_count
    ).astype(jnp.bfloat16)
    per_own = own_count // local_rows
    own_start = lax.axis_index("req") * (per_own * steps * local_rows)

    def own_of(rows):
        return (
            lax.dynamic_slice_in_dim(rows, own_start, per_own * steps * local_rows, 0)
            .reshape(per_own, steps, local_rows, -1)
            .transpose(1, 0, 2, 3)
            .reshape(steps, own_count, head_count, HD)
        )

    queries_own = own_of(queries_rows)
    keys_new = own_of(keys_rows)
    values_new = own_of(summed_all[:, 2 * width : 3 * width])

    chosen_rows = (
        (gather_rows // local_rows) * (steps * local_rows)
        + jnp.arange(steps, dtype=jnp.int32)[:, None, None] * local_rows
        + gather_rows % local_rows
    )
    chosen = pick_rows(queries_rows, chosen_rows)
    head_scores = [
        jnp.einsum(
            "zsbd,std->zsbt",
            chosen[..., head * HD : (head + 1) * HD],
            cache_keys[:, :, head * HD : (head + 1) * HD],
            preferred_element_type=jnp.float32,
        )
        for head in range(head_count)
    ]
    scores = jnp.stack(head_scores, axis=3) * scale
    masked = jnp.where(live_wide, scores, NEG_FILL)
    slot_top = jnp.max(masked, axis=4)
    weights = jnp.where(live_wide, jnp.exp(masked - slot_top[..., None]), 0.0)
    slot_total = jnp.sum(weights, axis=4)
    rounded = weights.astype(jnp.bfloat16)
    slot_out = jnp.stack(
        [
            jnp.einsum(
                "zsbt,std->zsbd",
                rounded[:, :, :, head],
                cache_values[:, :, head * HD : (head + 1) * HD],
                preferred_element_type=jnp.float32,
            )
            for head in range(head_count)
        ],
        axis=3,
    )
    request_top = jnp.max(
        jnp.where(owner_mask[None, :, :, None, None], slot_top[:, :, None], NEG_FILL), axis=1
    )
    top_high = request_top.astype(jnp.bfloat16)
    top_low = (request_top - top_high.astype(jnp.float32)).astype(jnp.bfloat16)
    request_top = top_high.astype(jnp.float32) + top_low.astype(jnp.float32)
    factor = jnp.where(
        slot_owner[None, :, None, None] >= 0,
        jnp.exp(slot_top - request_top[:, valid_owner]),
        0.0,
    )
    page_total = jnp.einsum(
        "sr,zsbh->zrbh", owner_float, slot_total * factor, precision=highest
    ).reshape(steps, beam_total, head_count)
    page_out = jnp.einsum(
        "sr,zsbhd->zrbhd", owner_float, slot_out * factor[..., None], precision=highest
    ).reshape(steps, beam_total, head_count, HD)
    stats = jnp.concatenate(
        [
            page_total.astype(jnp.bfloat16),
            top_high.reshape(steps, beam_total, head_count),
            top_low.reshape(steps, beam_total, head_count),
        ],
        axis=-1,
    )
    packed = jnp.concatenate(
        [
            page_out.astype(jnp.bfloat16).reshape(steps, beam_total, head_count * HD),
            jnp.pad(stats, ((0, 0), (0, 0), (0, HD - 3 * head_count))),
        ],
        axis=-1,
    )
    packed = packed.reshape(steps, req_size, own_count, -1).transpose(1, 0, 2, 3)
    held = exchange(packed, "req", req_size, False, 5).astype(jnp.float32)
    base = head_count * HD
    held_top = held[..., base + head_count : base + 2 * head_count] + held[
        ..., base + 2 * head_count : base + 3 * head_count
    ]
    own_top = jnp.max(held_top, axis=0)
    rescale = jnp.exp(held_top - own_top)
    own_total = jnp.sum(held[..., base : base + head_count] * rescale, axis=0)
    own_out = jnp.stack(
        [
            jnp.sum(held[..., head * HD : (head + 1) * HD] * rescale[..., head : head + 1], axis=0)
            for head in range(head_count)
        ],
        axis=2,
    )

    source = own_group * BEAM + parents[0]
    attended_steps = []
    for step_index in range(steps):
        tail_keys = [pick_rows(keys_new[prior], source) for prior in range(step_index)]
        tail_values = [pick_rows(values_new[prior], source) for prior in range(step_index)]
        history_keys = jnp.stack(tail_keys + [keys_new[step_index]], axis=0)
        history_values = jnp.stack(tail_values + [values_new[step_index]], axis=0)
        own_scores = (
            jnp.einsum(
                "bhd,nbhd->bhn",
                queries_own[step_index],
                history_keys,
                preferred_element_type=jnp.float32,
            )
            * scale
        )
        top = jnp.maximum(own_top[step_index], jnp.max(own_scores, axis=2))
        page_factor = jnp.exp(own_top[step_index] - top)
        own_weights = jnp.exp(own_scores - top[..., None])
        total = own_total[step_index] * page_factor + jnp.sum(own_weights, axis=2)
        summed = own_out[step_index] * page_factor[..., None] + jnp.einsum(
            "bhn,nbhd->bhd",
            own_weights.astype(jnp.bfloat16),
            history_values,
            preferred_element_type=jnp.float32,
        )
        attended_steps.append(
            (summed / total[..., None]).astype(jnp.bfloat16).reshape(own_count, head_count * HD)
        )
    attended = jnp.stack(attended_steps)
    attended_all = exchange(attended, "req", req_size, True, 6)
    attended_msi = (
        attended_all.reshape(req_size, steps, per_own, local_rows, -1)
        .transpose(0, 2, 1, 3, 4)
        .reshape(steps * beam_total, -1)
    )
    update_partial = (
        jnp.dot(attended_msi, dense_weight, preferred_element_type=jnp.float32)
        + jnp.dot(activated_all, down_weight, preferred_element_type=jnp.float32)
    ).astype(jnp.bfloat16)
    update = jnp.sum(
        exchange(
            update_partial.reshape(mlp_size, steps * local_rows, local_width),
            "mlp",
            mlp_size,
            False,
            1,
        ).astype(jnp.float32),
        axis=0,
    )
    layer = (block + update.reshape(steps, local_rows, local_width)).astype(jnp.bfloat16)
    next_in = (row_normalize(layer.astype(jnp.float32), 4) * norm_gains[2]).astype(jnp.bfloat16)
    gathered = exchange(next_in, "mlp", mlp_size, True, 2).reshape(steps * beam_total, -1)
    next_partial = jnp.dot(gathered, next_weight, preferred_element_type=jnp.float32)
    next_out = lax.psum_scatter(
        next_partial.astype(jnp.bfloat16), "req", scatter_dimension=0, tiled=True
    )
    next_out = (
        next_out.reshape(per_own, steps, local_rows, -1)
        .transpose(1, 0, 2, 3)
        .reshape(steps, own_count, -1)
    )
    return (layer, next_out)


def solution(mesh):
    in_specs = (
        P(None, "mlp", "req"),
        P(None, "req"),
        P("req", "mlp"),
        P("req", "mlp"),
        P("mlp", "req"),
        P("mlp", "req"),
        P("req", "mlp"),
        P("req", None, "mlp"),
        P("req", None, "mlp"),
        P(),
        P(None, "req"),
        P(None, "req"),
    )
    out_specs = (P(None, "mlp", "req"), P(None, "req", "mlp"))
    return jax.shard_map(shards, mesh=mesh, in_specs=in_specs, out_specs=out_specs, check_vma=False)
```

```python
import functools
import math

import jax
import jax.numpy as jnp
from jax import lax
from jax.experimental import pallas as pl
from jax.experimental.pallas import tpu as pltpu
from jax.sharding import PartitionSpec as P

MESH = pl.DeviceIdType.MESH

HD = 128
ROT = 32
PAGE = 128
BEAM = 8
STEPS = 2


NEG_FILL = -1e30
EPSILON = 1e-05


def rotate(vectors, positions):
    half = ROT // 2
    freq = jnp.exp(jnp.arange(half, dtype=jnp.float32) * (-2.0 * math.log(10000.0) / ROT))
    angles = positions.astype(jnp.float32)[..., None] * freq
    cosine = jnp.concatenate([jnp.cos(angles), jnp.cos(angles)], axis=-1)[..., None, :]
    sine = jnp.concatenate([jnp.sin(angles), jnp.sin(angles)], axis=-1)[..., None, :]
    turned = vectors[..., :ROT]
    swapped = jnp.concatenate([-turned[..., half:], turned[..., :half]], axis=-1)
    return jnp.concatenate([turned * cosine + swapped * sine, vectors[..., ROT:]], axis=-1)


def pick_rows(table, index):
    flat = table.reshape(table.shape[0], -1)
    hot = (index.reshape(-1)[:, None] == jnp.arange(table.shape[0], dtype=jnp.int32)[None, :])
    taken = jnp.dot(hot.astype(table.dtype), flat, preferred_element_type=jnp.float32)
    return taken.astype(table.dtype).reshape(index.shape + table.shape[1:])


def rotate_rows(rows, positions, head_count):
    half = ROT // 2
    freq = jnp.exp(jnp.arange(half, dtype=jnp.float32) * (-2.0 * math.log(10000.0) / ROT))
    angles = positions.astype(jnp.float32)[:, None] * freq[None, :]
    cosine = jnp.concatenate([jnp.cos(angles), jnp.cos(angles)], axis=1)
    sine = jnp.concatenate([jnp.sin(angles), jnp.sin(angles)], axis=1)
    parts = []
    for head in range(head_count):
        base = head * HD
        turned = rows[:, base : base + ROT]
        swapped = jnp.concatenate([-turned[:, half:], turned[:, :half]], axis=1)
        parts += [turned * cosine + swapped * sine, rows[:, base + ROT : base + HD]]
    return jnp.concatenate(parts, axis=1)


def exchange_kernel(axis, n, gather, x_ref, out_ref, send_sem, recv_sem, local_sem):
    me = lax.axis_index(axis)
    barrier = pltpu.get_barrier_semaphore()
    for k in range(1, n):
        pl.semaphore_signal(
            barrier, inc=1, device_id={axis: lax.rem(me + k, n)}, device_id_type=MESH
        )
    pl.semaphore_wait(barrier, n - 1)
    local = pltpu.make_async_copy(x_ref if gather else x_ref.at[me], out_ref.at[me], local_sem)
    local.start()
    copies = []
    for k in range(1, n):
        dest = lax.rem(me + k, n)
        copy = pltpu.make_async_remote_copy(
            src_ref=x_ref if gather else x_ref.at[dest],
            dst_ref=out_ref.at[me],
            send_sem=send_sem.at[k],
            recv_sem=recv_sem.at[k],
            device_id={axis: dest},
            device_id_type=MESH,
        )
        copy.start()
        copies.append(copy)
    for copy in copies:
        copy.wait()
    local.wait()


def exchange_gelu_kernel(axis, n, x_ref, hidden_ref, out_ref, act_ref, send_sem, recv_sem, local_sem):
    me = lax.axis_index(axis)
    barrier = pltpu.get_barrier_semaphore()
    for k in range(1, n):
        pl.semaphore_signal(
            barrier, inc=1, device_id={axis: lax.rem(me + k, n)}, device_id_type=MESH
        )
    pl.semaphore_wait(barrier, n - 1)
    local = pltpu.make_async_copy(x_ref.at[me], out_ref.at[me], local_sem)
    local.start()
    copies = []
    for k in range(1, n):
        dest = lax.rem(me + k, n)
        copy = pltpu.make_async_remote_copy(
            src_ref=x_ref.at[dest],
            dst_ref=out_ref.at[me],
            send_sem=send_sem.at[k],
            recv_sem=recv_sem.at[k],
            device_id={axis: dest},
            device_id_type=MESH,
        )
        copy.start()
        copies.append(copy)
    tile = 128

    @pl.loop(0, hidden_ref.shape[0] // tile)
    def _(index):
        rows = pl.ds(pl.multiple_of(index * tile, tile), tile)
        values = hidden_ref[rows, :].astype(jnp.float32)
        gelu = 0.5 * values * (1.0 + lax.erf(values * (1.0 / math.sqrt(2.0))))
        act_ref[rows, :] = gelu.astype(act_ref.dtype)

    for copy in copies:
        copy.wait()
    local.wait()


def exchange_gelu(x, hidden, axis, n, collective_id):
    return pl.pallas_call(
        functools.partial(exchange_gelu_kernel, axis, n),
        out_shape=(
            jax.ShapeDtypeStruct(x.shape, x.dtype),
            jax.ShapeDtypeStruct(hidden.shape, jnp.bfloat16),
        ),
        in_specs=[pl.BlockSpec(memory_space=pltpu.VMEM)] * 2,
        out_specs=(pl.BlockSpec(memory_space=pltpu.VMEM),) * 2,
        scratch_shapes=[
            pltpu.SemaphoreType.DMA((n,)),
            pltpu.SemaphoreType.DMA((n,)),
            pltpu.SemaphoreType.DMA(()),
        ],
        compiler_params=pltpu.CompilerParams(
            collective_id=collective_id, has_side_effects=True
        ),
        cost_estimate=pl.CostEstimate(
            flops=20 * hidden.size,
            transcendentals=hidden.size,
            bytes_accessed=2 * n * x.size * x.dtype.itemsize + 4 * hidden.size,
        ),
    )(x, hidden)


def exchange(x, axis, n, gather, collective_id):
    shape = (n,) + (x.shape if gather else x.shape[1:])
    return pl.pallas_call(
        functools.partial(exchange_kernel, axis, n, gather),
        out_shape=jax.ShapeDtypeStruct(shape, x.dtype),
        in_specs=[pl.BlockSpec(memory_space=pltpu.VMEM)],
        out_specs=pl.BlockSpec(memory_space=pltpu.VMEM),
        scratch_shapes=[
            pltpu.SemaphoreType.DMA((n,)),
            pltpu.SemaphoreType.DMA((n,)),
            pltpu.SemaphoreType.DMA(()),
        ],
        compiler_params=pltpu.CompilerParams(
            collective_id=collective_id, has_side_effects=True
        ),
        cost_estimate=pl.CostEstimate(
            flops=0, transcendentals=0, bytes_accessed=2 * n * x.size * x.dtype.itemsize
        ),
    )(x)


def exchange_flat(x, axis, n, gather, collective_id):
    lead = () if gather else x.shape[:1]
    block_shape = x.shape if gather else x.shape[1:]
    size = math.prod(block_shape)
    padded = -(-size // 128) * 128
    flat = x.reshape(lead + (size,))
    flat = jnp.pad(flat, [(0, 0)] * len(lead) + [(0, padded - size)])
    flat = flat.reshape(lead + (padded // 128, 128))
    out = exchange(flat, axis, n, gather, collective_id)
    return out.reshape(n, padded)[:, :size].reshape((n,) + block_shape)


def row_normalize(values, collective_id):
    width = values.shape[-1]
    local_mean = jnp.mean(values, axis=-1)
    centred = values - local_mean[..., None]
    local_m2 = jnp.sum(centred * centred, axis=-1)
    stats = jnp.stack([local_mean, local_m2], axis=0)
    stats = exchange_flat(stats, "req", lax.axis_size("req"), True, collective_id)
    stats = jnp.moveaxis(stats, 1, -1)
    means = stats[..., 0]
    row_mean = jnp.mean(means, axis=0)
    spread = means - row_mean
    row_m2 = jnp.sum(stats[..., 1], axis=0) + width * jnp.sum(spread * spread, axis=0)
    row_var = row_m2 / (width * stats.shape[0])
    return (values - row_mean[..., None]) * lax.rsqrt(row_var + EPSILON)[..., None]


def shards(
    inputs,
    norm_gains,
    attn_weight,
    up_weight,
    dense_weight,
    down_weight,
    next_weight,
    cache_keys,
    cache_values,
    lengths,
    slot_table,
    parents,
):
    scale = 1.0 / math.sqrt(HD)
    highest = lax.Precision.HIGHEST
    steps, local_rows, local_width = inputs.shape
    own_count = parents.shape[1]
    request_count = lengths.shape[0]
    beam_total = request_count * BEAM
    head_count = dense_weight.shape[0] // HD
    triple_width = attn_weight.shape[1]
    slot_count = slot_table.shape[1]
    req_size = beam_total // own_count
    mlp_size = beam_total // local_rows
    offset = lax.axis_index("req") * own_count
    beam_group = jnp.arange(beam_total, dtype=jnp.int32) // BEAM
    all_positions = lengths[beam_group][None, :] + jnp.arange(steps, dtype=jnp.int32)[:, None]
    own_group = jnp.arange(own_count, dtype=jnp.int32) // BEAM
    slot_owner = slot_table[0]
    slot_pageno = slot_table[1]
    valid_owner = jnp.maximum(slot_owner, 0)
    token_pos = slot_pageno[:, None] * PAGE + jnp.arange(PAGE, dtype=jnp.int32)[None, :]
    live = (slot_owner[:, None] >= 0) & (token_pos < lengths[valid_owner][:, None])
    live_wide = live[None, :, None, None, :]
    owner_mask = slot_owner[:, None] == jnp.arange(request_count, dtype=jnp.int32)[None, :]
    owner_float = owner_mask.astype(jnp.float32)
    gather_rows = valid_owner[:, None] * BEAM + jnp.arange(BEAM, dtype=jnp.int32)[None, :]

    block = inputs.astype(jnp.float32)
    rows_all = exchange(inputs, "mlp", mlp_size, True, 0).reshape(steps * beam_total, -1)
    normed = row_normalize(rows_all.astype(jnp.float32), 3)
    attn_in = (normed * norm_gains[0]).astype(jnp.bfloat16)
    mlp_in = (normed * norm_gains[1]).astype(jnp.bfloat16)
    grouped = (
        attn_weight.reshape(local_width, head_count, 3, HD)
        .transpose(0, 2, 1, 3)
        .reshape(local_width, triple_width)
    )
    first = jnp.dot(attn_in, grouped, preferred_element_type=jnp.float32)
    second = jnp.dot(mlp_in, up_weight, preferred_element_type=jnp.float32)
    partial_sums = jnp.concatenate([first, second], axis=1)
    summed_all = lax.psum(partial_sums.astype(jnp.bfloat16), "req")
    width = head_count * HD
    row = jnp.arange(steps * beam_total, dtype=jnp.int32)
    beam_lengths = jnp.broadcast_to(lengths[:, None], (request_count, BEAM)).reshape(
        mlp_size, 1, local_rows
    )
    row_positions = (
        beam_lengths + jnp.arange(steps, dtype=jnp.int32)[None, :, None]
    ).reshape(steps * beam_total)
    queries_rows = rotate_rows(
        summed_all[:, :width].astype(jnp.float32), row_positions, head_count
    ).astype(jnp.bfloat16)
    keys_rows = rotate_rows(
        summed_all[:, width : 2 * width].astype(jnp.float32), row_positions, head_count
    ).astype(jnp.bfloat16)
    per_own = own_count // local_rows
    own_start = lax.axis_index("req") * (per_own * steps * local_rows)

    def own_of(rows):
        return (
            lax.dynamic_slice_in_dim(rows, own_start, per_own * steps * local_rows, 0)
            .reshape(per_own, steps, local_rows, -1)
            .transpose(1, 0, 2, 3)
            .reshape(steps, own_count, head_count, HD)
        )

    queries_own = own_of(queries_rows)
    keys_new = own_of(keys_rows)
    values_new = own_of(summed_all[:, 2 * width : 3 * width])

    chosen_rows = (
        (gather_rows // local_rows) * (steps * local_rows)
        + jnp.arange(steps, dtype=jnp.int32)[:, None, None] * local_rows
        + gather_rows % local_rows
    )
    chosen = pick_rows(queries_rows, chosen_rows)
    head_scores = [
        jnp.einsum(
            "zsbd,std->zsbt",
            chosen[..., head * HD : (head + 1) * HD],
            cache_keys[:, :, head * HD : (head + 1) * HD],
            preferred_element_type=jnp.float32,
        )
        for head in range(head_count)
    ]
    scores = jnp.stack(head_scores, axis=3) * scale
    masked = jnp.where(live_wide, scores, NEG_FILL)
    slot_top = jnp.max(masked, axis=4)
    weights = jnp.where(live_wide, jnp.exp(masked - slot_top[..., None]), 0.0)
    slot_total = jnp.sum(weights, axis=4)
    rounded = weights.astype(jnp.bfloat16)
    slot_out = jnp.stack(
        [
            jnp.einsum(
                "zsbt,std->zsbd",
                rounded[:, :, :, head],
                cache_values[:, :, head * HD : (head + 1) * HD],
                preferred_element_type=jnp.float32,
            )
            for head in range(head_count)
        ],
        axis=3,
    )
    request_top = jnp.max(
        jnp.where(owner_mask[None, :, :, None, None], slot_top[:, :, None], NEG_FILL), axis=1
    )
    top_high = request_top.astype(jnp.bfloat16)
    top_low = (request_top - top_high.astype(jnp.float32)).astype(jnp.bfloat16)
    request_top = top_high.astype(jnp.float32) + top_low.astype(jnp.float32)
    factor = jnp.where(
        slot_owner[None, :, None, None] >= 0,
        jnp.exp(slot_top - request_top[:, valid_owner]),
        0.0,
    )
    page_total = jnp.einsum(
        "sr,zsbh->zrbh", owner_float, slot_total * factor, precision=highest
    ).reshape(steps, beam_total, head_count)
    page_out = jnp.einsum(
        "sr,zsbhd->zrbhd", owner_float, slot_out * factor[..., None], precision=highest
    ).reshape(steps, beam_total, head_count, HD)
    stats = jnp.concatenate(
        [
            page_total.astype(jnp.bfloat16),
            top_high.reshape(steps, beam_total, head_count),
            top_low.reshape(steps, beam_total, head_count),
        ],
        axis=-1,
    )
    packed = jnp.concatenate(
        [
            page_out.astype(jnp.bfloat16).reshape(steps, beam_total, head_count * HD),
            jnp.pad(stats, ((0, 0), (0, 0), (0, HD - 3 * head_count))),
        ],
        axis=-1,
    )
    packed = packed.reshape(steps, req_size, own_count, -1).transpose(1, 0, 2, 3)
    held, activated_all = exchange_gelu(packed, summed_all[:, triple_width:], "req", req_size, 5)
    held = held.astype(jnp.float32)
    base = head_count * HD
    held_top = held[..., base + head_count : base + 2 * head_count] + held[
        ..., base + 2 * head_count : base + 3 * head_count
    ]
    own_top = jnp.max(held_top, axis=0)
    rescale = jnp.exp(held_top - own_top)
    own_total = jnp.sum(held[..., base : base + head_count] * rescale, axis=0)
    own_out = jnp.stack(
        [
            jnp.sum(held[..., head * HD : (head + 1) * HD] * rescale[..., head : head + 1], axis=0)
            for head in range(head_count)
        ],
        axis=2,
    )

    source = own_group * BEAM + parents[0]
    attended_steps = []
    for step_index in range(steps):
        tail_keys = [pick_rows(keys_new[prior], source) for prior in range(step_index)]
        tail_values = [pick_rows(values_new[prior], source) for prior in range(step_index)]
        history_keys = jnp.stack(tail_keys + [keys_new[step_index]], axis=0)
        history_values = jnp.stack(tail_values + [values_new[step_index]], axis=0)
        own_scores = (
            jnp.einsum(
                "bhd,nbhd->bhn",
                queries_own[step_index],
                history_keys,
                preferred_element_type=jnp.float32,
            )
            * scale
        )
        top = jnp.maximum(own_top[step_index], jnp.max(own_scores, axis=2))
        page_factor = jnp.exp(own_top[step_index] - top)
        own_weights = jnp.exp(own_scores - top[..., None])
        total = own_total[step_index] * page_factor + jnp.sum(own_weights, axis=2)
        summed = own_out[step_index] * page_factor[..., None] + jnp.einsum(
            "bhn,nbhd->bhd",
            own_weights.astype(jnp.bfloat16),
            history_values,
            preferred_element_type=jnp.float32,
        )
        attended_steps.append(
            (summed / total[..., None]).astype(jnp.bfloat16).reshape(own_count, head_count * HD)
        )
    attended = jnp.stack(attended_steps)
    attended_all = exchange(attended, "req", req_size, True, 6)
    attended_msi = (
        attended_all.reshape(req_size, steps, per_own, local_rows, -1)
        .transpose(0, 2, 1, 3, 4)
        .reshape(steps * beam_total, -1)
    )
    update_partial = (
        jnp.dot(attended_msi, dense_weight, preferred_element_type=jnp.float32)
        + jnp.dot(activated_all, down_weight, preferred_element_type=jnp.float32)
    ).astype(jnp.bfloat16)
    update = jnp.sum(
        exchange(
            update_partial.reshape(mlp_size, steps * local_rows, local_width),
            "mlp",
            mlp_size,
            False,
            1,
        ).astype(jnp.float32),
        axis=0,
    )
    layer = (block + update.reshape(steps, local_rows, local_width)).astype(jnp.bfloat16)
    next_in = (row_normalize(layer.astype(jnp.float32), 4) * norm_gains[2]).astype(jnp.bfloat16)
    gathered = exchange(next_in, "mlp", mlp_size, True, 2).reshape(steps * beam_total, -1)
    next_partial = jnp.dot(gathered, next_weight, preferred_element_type=jnp.float32)
    next_out = lax.psum_scatter(
        next_partial.astype(jnp.bfloat16), "req", scatter_dimension=0, tiled=True
    )
    next_out = (
        next_out.reshape(per_own, steps, local_rows, -1)
        .transpose(1, 0, 2, 3)
        .reshape(steps, own_count, -1)
    )
    return (layer, next_out)


def solution(mesh):
    in_specs = (
        P(None, "mlp", "req"),
        P(None, "req"),
        P("req", "mlp"),
        P("req", "mlp"),
        P("mlp", "req"),
        P("mlp", "req"),
        P("req", "mlp"),
        P("req", None, "mlp"),
        P("req", None, "mlp"),
        P(),
        P(None, "req"),
        P(None, "req"),
    )
    out_specs = (P(None, "mlp", "req"), P(None, "req", "mlp"))
    return jax.shard_map(shards, mesh=mesh, in_specs=in_specs, out_specs=out_specs, check_vma=False)
```

```python
import functools
import math

import jax
import jax.numpy as jnp
from jax import lax
from jax.experimental import pallas as pl
from jax.experimental.pallas import tpu as pltpu
from jax.sharding import PartitionSpec as P

MESH = pl.DeviceIdType.MESH

HD = 128
ROT = 32
PAGE = 128
BEAM = 8
STEPS = 2


NEG_FILL = -1e30
EPSILON = 1e-05


def rotate(vectors, positions):
    half = ROT // 2
    freq = jnp.exp(jnp.arange(half, dtype=jnp.float32) * (-2.0 * math.log(10000.0) / ROT))
    angles = positions.astype(jnp.float32)[..., None] * freq
    cosine = jnp.concatenate([jnp.cos(angles), jnp.cos(angles)], axis=-1)[..., None, :]
    sine = jnp.concatenate([jnp.sin(angles), jnp.sin(angles)], axis=-1)[..., None, :]
    turned = vectors[..., :ROT]
    swapped = jnp.concatenate([-turned[..., half:], turned[..., :half]], axis=-1)
    return jnp.concatenate([turned * cosine + swapped * sine, vectors[..., ROT:]], axis=-1)


def pick_rows(table, index):
    flat = table.reshape(table.shape[0], -1)
    hot = (index.reshape(-1)[:, None] == jnp.arange(table.shape[0], dtype=jnp.int32)[None, :])
    taken = jnp.dot(hot.astype(table.dtype), flat, preferred_element_type=jnp.float32)
    return taken.astype(table.dtype).reshape(index.shape + table.shape[1:])


def rotate_rows(rows, positions, head_count):
    half = ROT // 2
    freq = jnp.exp(jnp.arange(half, dtype=jnp.float32) * (-2.0 * math.log(10000.0) / ROT))
    angles = positions.astype(jnp.float32)[:, None] * freq[None, :]
    cosine = jnp.concatenate([jnp.cos(angles), jnp.cos(angles)], axis=1)
    sine = jnp.concatenate([jnp.sin(angles), jnp.sin(angles)], axis=1)
    parts = []
    for head in range(head_count):
        base = head * HD
        turned = rows[:, base : base + ROT]
        swapped = jnp.concatenate([-turned[:, half:], turned[:, :half]], axis=1)
        parts += [turned * cosine + swapped * sine, rows[:, base + ROT : base + HD]]
    return jnp.concatenate(parts, axis=1)


def exchange_kernel(axis, n, gather, x_ref, out_ref, send_sem, recv_sem, local_sem):
    me = lax.axis_index(axis)
    barrier = pltpu.get_barrier_semaphore()
    for k in range(1, n):
        pl.semaphore_signal(
            barrier, inc=1, device_id={axis: lax.rem(me + k, n)}, device_id_type=MESH
        )
    pl.semaphore_wait(barrier, n - 1)
    local = pltpu.make_async_copy(x_ref if gather else x_ref.at[me], out_ref.at[me], local_sem)
    local.start()
    copies = []
    for k in range(1, n):
        dest = lax.rem(me + k, n)
        copy = pltpu.make_async_remote_copy(
            src_ref=x_ref if gather else x_ref.at[dest],
            dst_ref=out_ref.at[me],
            send_sem=send_sem.at[k],
            recv_sem=recv_sem.at[k],
            device_id={axis: dest},
            device_id_type=MESH,
        )
        copy.start()
        copies.append(copy)
    for copy in copies:
        copy.wait()
    local.wait()


def exchange_gelu_kernel(axis, n, x_ref, hidden_ref, out_ref, act_ref, send_sem, recv_sem, local_sem):
    me = lax.axis_index(axis)
    barrier = pltpu.get_barrier_semaphore()
    for k in range(1, n):
        pl.semaphore_signal(
            barrier, inc=1, device_id={axis: lax.rem(me + k, n)}, device_id_type=MESH
        )
    pl.semaphore_wait(barrier, n - 1)
    local = pltpu.make_async_copy(x_ref.at[me], out_ref.at[me], local_sem)
    local.start()
    copies = []
    for k in range(1, n):
        dest = lax.rem(me + k, n)
        copy = pltpu.make_async_remote_copy(
            src_ref=x_ref.at[dest],
            dst_ref=out_ref.at[me],
            send_sem=send_sem.at[k],
            recv_sem=recv_sem.at[k],
            device_id={axis: dest},
            device_id_type=MESH,
        )
        copy.start()
        copies.append(copy)
    tile = 128

    @pl.loop(0, hidden_ref.shape[0] // tile)
    def _(index):
        rows = pl.ds(pl.multiple_of(index * tile, tile), tile)
        values = hidden_ref[rows, :].astype(jnp.float32)
        gelu = 0.5 * values * (1.0 + lax.erf(values * (1.0 / math.sqrt(2.0))))
        act_ref[rows, :] = gelu.astype(act_ref.dtype)

    for copy in copies:
        copy.wait()
    local.wait()


def exchange_gelu(x, hidden, axis, n, collective_id):
    return pl.pallas_call(
        functools.partial(exchange_gelu_kernel, axis, n),
        out_shape=(
            jax.ShapeDtypeStruct(x.shape, x.dtype),
            jax.ShapeDtypeStruct(hidden.shape, jnp.bfloat16),
        ),
        in_specs=[pl.BlockSpec(memory_space=pltpu.VMEM)] * 2,
        out_specs=(pl.BlockSpec(memory_space=pltpu.VMEM),) * 2,
        scratch_shapes=[
            pltpu.SemaphoreType.DMA((n,)),
            pltpu.SemaphoreType.DMA((n,)),
            pltpu.SemaphoreType.DMA(()),
        ],
        compiler_params=pltpu.CompilerParams(
            collective_id=collective_id, has_side_effects=True
        ),
        cost_estimate=pl.CostEstimate(
            flops=20 * hidden.size,
            transcendentals=hidden.size,
            bytes_accessed=2 * n * x.size * x.dtype.itemsize + 4 * hidden.size,
        ),
    )(x, hidden)


def gather_grid_kernel(axis, side, x_ref, out_ref, send_sem, recv_sem, local_sem):
    me = lax.axis_index(axis)
    row, col = me // side, me % side
    row_peers = [row * side + lax.rem(col + k, side) for k in range(1, side)]
    col_peers = [lax.rem(row + k, side) * side + col for k in range(1, side)]
    barrier = pltpu.get_barrier_semaphore()
    for peer in row_peers + col_peers:
        pl.semaphore_signal(barrier, inc=1, device_id={axis: peer}, device_id_type=MESH)
    pl.semaphore_wait(barrier, 2 * (side - 1))
    local = pltpu.make_async_copy(x_ref, out_ref.at[me], local_sem)
    local.start()
    first = []
    for k, peer in enumerate(row_peers):
        copy = pltpu.make_async_remote_copy(
            src_ref=x_ref,
            dst_ref=out_ref.at[me],
            send_sem=send_sem.at[0, k],
            recv_sem=recv_sem.at[0, k],
            device_id={axis: peer},
            device_id_type=MESH,
        )
        copy.start()
        first.append(copy)
    for copy in first:
        copy.wait()
    local.wait()
    slab = out_ref.at[pl.ds(row * side, side)]
    second = []
    for k, peer in enumerate(col_peers):
        copy = pltpu.make_async_remote_copy(
            src_ref=slab,
            dst_ref=slab,
            send_sem=send_sem.at[1, k],
            recv_sem=recv_sem.at[1, k],
            device_id={axis: peer},
            device_id_type=MESH,
        )
        copy.start()
        second.append(copy)
    for copy in second:
        copy.wait()


def gather_grid(x, axis, n, collective_id):
    side = math.isqrt(n)
    return pl.pallas_call(
        functools.partial(gather_grid_kernel, axis, side),
        out_shape=jax.ShapeDtypeStruct((n,) + x.shape, x.dtype),
        in_specs=[pl.BlockSpec(memory_space=pltpu.VMEM)],
        out_specs=pl.BlockSpec(memory_space=pltpu.VMEM),
        scratch_shapes=[
            pltpu.SemaphoreType.DMA((2, side - 1)),
            pltpu.SemaphoreType.DMA((2, side - 1)),
            pltpu.SemaphoreType.DMA(()),
        ],
        compiler_params=pltpu.CompilerParams(
            collective_id=collective_id, has_side_effects=True
        ),
        cost_estimate=pl.CostEstimate(
            flops=0, transcendentals=0, bytes_accessed=2 * n * x.size * x.dtype.itemsize
        ),
    )(x)


def exchange(x, axis, n, gather, collective_id):
    shape = (n,) + (x.shape if gather else x.shape[1:])
    return pl.pallas_call(
        functools.partial(exchange_kernel, axis, n, gather),
        out_shape=jax.ShapeDtypeStruct(shape, x.dtype),
        in_specs=[pl.BlockSpec(memory_space=pltpu.VMEM)],
        out_specs=pl.BlockSpec(memory_space=pltpu.VMEM),
        scratch_shapes=[
            pltpu.SemaphoreType.DMA((n,)),
            pltpu.SemaphoreType.DMA((n,)),
            pltpu.SemaphoreType.DMA(()),
        ],
        compiler_params=pltpu.CompilerParams(
            collective_id=collective_id, has_side_effects=True
        ),
        cost_estimate=pl.CostEstimate(
            flops=0, transcendentals=0, bytes_accessed=2 * n * x.size * x.dtype.itemsize
        ),
    )(x)


def exchange_flat(x, axis, n, gather, collective_id):
    lead = () if gather else x.shape[:1]
    block_shape = x.shape if gather else x.shape[1:]
    size = math.prod(block_shape)
    padded = -(-size // 128) * 128
    flat = x.reshape(lead + (size,))
    flat = jnp.pad(flat, [(0, 0)] * len(lead) + [(0, padded - size)])
    flat = flat.reshape(lead + (padded // 128, 128))
    out = exchange(flat, axis, n, gather, collective_id)
    return out.reshape(n, padded)[:, :size].reshape((n,) + block_shape)


def row_normalize(values, collective_id):
    width = values.shape[-1]
    local_mean = jnp.mean(values, axis=-1)
    centred = values - local_mean[..., None]
    local_m2 = jnp.sum(centred * centred, axis=-1)
    stats = jnp.stack([local_mean, local_m2], axis=0)
    stats = exchange_flat(stats, "req", lax.axis_size("req"), True, collective_id)
    stats = jnp.moveaxis(stats, 1, -1)
    means = stats[..., 0]
    row_mean = jnp.mean(means, axis=0)
    spread = means - row_mean
    row_m2 = jnp.sum(stats[..., 1], axis=0) + width * jnp.sum(spread * spread, axis=0)
    row_var = row_m2 / (width * stats.shape[0])
    return (values - row_mean[..., None]) * lax.rsqrt(row_var + EPSILON)[..., None]


def shards(
    inputs,
    norm_gains,
    attn_weight,
    up_weight,
    dense_weight,
    down_weight,
    next_weight,
    cache_keys,
    cache_values,
    lengths,
    slot_table,
    parents,
):
    scale = 1.0 / math.sqrt(HD)
    highest = lax.Precision.HIGHEST
    steps, local_rows, local_width = inputs.shape
    own_count = parents.shape[1]
    request_count = lengths.shape[0]
    beam_total = request_count * BEAM
    head_count = dense_weight.shape[0] // HD
    triple_width = attn_weight.shape[1]
    slot_count = slot_table.shape[1]
    req_size = beam_total // own_count
    mlp_size = beam_total // local_rows
    offset = lax.axis_index("req") * own_count
    beam_group = jnp.arange(beam_total, dtype=jnp.int32) // BEAM
    all_positions = lengths[beam_group][None, :] + jnp.arange(steps, dtype=jnp.int32)[:, None]
    own_group = jnp.arange(own_count, dtype=jnp.int32) // BEAM
    slot_owner = slot_table[0]
    slot_pageno = slot_table[1]
    valid_owner = jnp.maximum(slot_owner, 0)
    token_pos = slot_pageno[:, None] * PAGE + jnp.arange(PAGE, dtype=jnp.int32)[None, :]
    live = (slot_owner[:, None] >= 0) & (token_pos < lengths[valid_owner][:, None])
    live_wide = live[None, :, None, None, :]
    owner_mask = slot_owner[:, None] == jnp.arange(request_count, dtype=jnp.int32)[None, :]
    owner_float = owner_mask.astype(jnp.float32)
    gather_rows = valid_owner[:, None] * BEAM + jnp.arange(BEAM, dtype=jnp.int32)[None, :]

    block = inputs.astype(jnp.float32)
    rows_all = gather_grid(inputs, "mlp", mlp_size, 0).reshape(steps * beam_total, -1)
    normed = row_normalize(rows_all.astype(jnp.float32), 3)
    attn_in = (normed * norm_gains[0]).astype(jnp.bfloat16)
    mlp_in = (normed * norm_gains[1]).astype(jnp.bfloat16)
    grouped = (
        attn_weight.reshape(local_width, head_count, 3, HD)
        .transpose(0, 2, 1, 3)
        .reshape(local_width, triple_width)
    )
    first = jnp.dot(attn_in, grouped, preferred_element_type=jnp.float32)
    second = jnp.dot(mlp_in, up_weight, preferred_element_type=jnp.float32)
    partial_sums = jnp.concatenate([first, second], axis=1)
    summed_all = lax.psum(partial_sums.astype(jnp.bfloat16), "req")
    width = head_count * HD
    row = jnp.arange(steps * beam_total, dtype=jnp.int32)
    beam_lengths = jnp.broadcast_to(lengths[:, None], (request_count, BEAM)).reshape(
        mlp_size, 1, local_rows
    )
    row_positions = (
        beam_lengths + jnp.arange(steps, dtype=jnp.int32)[None, :, None]
    ).reshape(steps * beam_total)
    queries_rows = rotate_rows(
        summed_all[:, :width].astype(jnp.float32), row_positions, head_count
    ).astype(jnp.bfloat16)
    keys_rows = rotate_rows(
        summed_all[:, width : 2 * width].astype(jnp.float32), row_positions, head_count
    ).astype(jnp.bfloat16)
    per_own = own_count // local_rows
    own_start = lax.axis_index("req") * (per_own * steps * local_rows)

    def own_of(rows):
        return (
            lax.dynamic_slice_in_dim(rows, own_start, per_own * steps * local_rows, 0)
            .reshape(per_own, steps, local_rows, -1)
            .transpose(1, 0, 2, 3)
            .reshape(steps, own_count, head_count, HD)
        )

    queries_own = own_of(queries_rows)
    keys_new = own_of(keys_rows)
    values_new = own_of(summed_all[:, 2 * width : 3 * width])

    chosen_rows = (
        (gather_rows // local_rows) * (steps * local_rows)
        + jnp.arange(steps, dtype=jnp.int32)[:, None, None] * local_rows
        + gather_rows % local_rows
    )
    chosen = pick_rows(queries_rows, chosen_rows)
    head_scores = [
        jnp.einsum(
            "zsbd,std->zsbt",
            chosen[..., head * HD : (head + 1) * HD],
            cache_keys[:, :, head * HD : (head + 1) * HD],
            preferred_element_type=jnp.float32,
        )
        for head in range(head_count)
    ]
    scores = jnp.stack(head_scores, axis=3) * scale
    masked = jnp.where(live_wide, scores, NEG_FILL)
    slot_top = jnp.max(masked, axis=4)
    weights = jnp.where(live_wide, jnp.exp(masked - slot_top[..., None]), 0.0)
    slot_total = jnp.sum(weights, axis=4)
    rounded = weights.astype(jnp.bfloat16)
    slot_out = jnp.stack(
        [
            jnp.einsum(
                "zsbt,std->zsbd",
                rounded[:, :, :, head],
                cache_values[:, :, head * HD : (head + 1) * HD],
                preferred_element_type=jnp.float32,
            )
            for head in range(head_count)
        ],
        axis=3,
    )
    request_top = jnp.max(
        jnp.where(owner_mask[None, :, :, None, None], slot_top[:, :, None], NEG_FILL), axis=1
    )
    top_high = request_top.astype(jnp.bfloat16)
    top_low = (request_top - top_high.astype(jnp.float32)).astype(jnp.bfloat16)
    request_top = top_high.astype(jnp.float32) + top_low.astype(jnp.float32)
    factor = jnp.where(
        slot_owner[None, :, None, None] >= 0,
        jnp.exp(slot_top - request_top[:, valid_owner]),
        0.0,
    )
    page_total = jnp.einsum(
        "sr,zsbh->zrbh", owner_float, slot_total * factor, precision=highest
    ).reshape(steps, beam_total, head_count)
    page_out = jnp.einsum(
        "sr,zsbhd->zrbhd", owner_float, slot_out * factor[..., None], precision=highest
    ).reshape(steps, beam_total, head_count, HD)
    stats = jnp.concatenate(
        [
            page_total.astype(jnp.bfloat16),
            top_high.reshape(steps, beam_total, head_count),
            top_low.reshape(steps, beam_total, head_count),
        ],
        axis=-1,
    )
    packed = jnp.concatenate(
        [
            page_out.astype(jnp.bfloat16).reshape(steps, beam_total, head_count * HD),
            jnp.pad(stats, ((0, 0), (0, 0), (0, HD - 3 * head_count))),
        ],
        axis=-1,
    )
    packed = packed.reshape(steps, req_size, own_count, -1).transpose(1, 0, 2, 3)
    held, activated_all = exchange_gelu(packed, summed_all[:, triple_width:], "req", req_size, 5)
    held = held.astype(jnp.float32)
    base = head_count * HD
    held_top = held[..., base + head_count : base + 2 * head_count] + held[
        ..., base + 2 * head_count : base + 3 * head_count
    ]
    own_top = jnp.max(held_top, axis=0)
    rescale = jnp.exp(held_top - own_top)
    own_total = jnp.sum(held[..., base : base + head_count] * rescale, axis=0)
    own_out = jnp.stack(
        [
            jnp.sum(held[..., head * HD : (head + 1) * HD] * rescale[..., head : head + 1], axis=0)
            for head in range(head_count)
        ],
        axis=2,
    )

    source = own_group * BEAM + parents[0]
    attended_steps = []
    for step_index in range(steps):
        tail_keys = [pick_rows(keys_new[prior], source) for prior in range(step_index)]
        tail_values = [pick_rows(values_new[prior], source) for prior in range(step_index)]
        history_keys = jnp.stack(tail_keys + [keys_new[step_index]], axis=0)
        history_values = jnp.stack(tail_values + [values_new[step_index]], axis=0)
        own_scores = (
            jnp.einsum(
                "bhd,nbhd->bhn",
                queries_own[step_index],
                history_keys,
                preferred_element_type=jnp.float32,
            )
            * scale
        )
        top = jnp.maximum(own_top[step_index], jnp.max(own_scores, axis=2))
        page_factor = jnp.exp(own_top[step_index] - top)
        own_weights = jnp.exp(own_scores - top[..., None])
        total = own_total[step_index] * page_factor + jnp.sum(own_weights, axis=2)
        summed = own_out[step_index] * page_factor[..., None] + jnp.einsum(
            "bhn,nbhd->bhd",
            own_weights.astype(jnp.bfloat16),
            history_values,
            preferred_element_type=jnp.float32,
        )
        attended_steps.append(
            (summed / total[..., None]).astype(jnp.bfloat16).reshape(own_count, head_count * HD)
        )
    attended = jnp.stack(attended_steps)
    attended_all = exchange(attended, "req", req_size, True, 6)
    attended_msi = (
        attended_all.reshape(req_size, steps, per_own, local_rows, -1)
        .transpose(0, 2, 1, 3, 4)
        .reshape(steps * beam_total, -1)
    )
    update_partial = (
        jnp.dot(attended_msi, dense_weight, preferred_element_type=jnp.float32)
        + jnp.dot(activated_all, down_weight, preferred_element_type=jnp.float32)
    ).astype(jnp.bfloat16)
    update = jnp.sum(
        exchange(
            update_partial.reshape(mlp_size, steps * local_rows, local_width),
            "mlp",
            mlp_size,
            False,
            1,
        ).astype(jnp.float32),
        axis=0,
    )
    layer = (block + update.reshape(steps, local_rows, local_width)).astype(jnp.bfloat16)
    next_in = (row_normalize(layer.astype(jnp.float32), 4) * norm_gains[2]).astype(jnp.bfloat16)
    gathered = gather_grid(next_in, "mlp", mlp_size, 2).reshape(steps * beam_total, -1)
    next_partial = jnp.dot(gathered, next_weight, preferred_element_type=jnp.float32)
    next_out = lax.psum_scatter(
        next_partial.astype(jnp.bfloat16), "req", scatter_dimension=0, tiled=True
    )
    next_out = (
        next_out.reshape(per_own, steps, local_rows, -1)
        .transpose(1, 0, 2, 3)
        .reshape(steps, own_count, -1)
    )
    return (layer, next_out)


def solution(mesh):
    in_specs = (
        P(None, "mlp", "req"),
        P(None, "req"),
        P("req", "mlp"),
        P("req", "mlp"),
        P("mlp", "req"),
        P("mlp", "req"),
        P("req", "mlp"),
        P("req", None, "mlp"),
        P("req", None, "mlp"),
        P(),
        P(None, "req"),
        P(None, "req"),
    )
    out_specs = (P(None, "mlp", "req"), P(None, "req", "mlp"))
    return jax.shard_map(shards, mesh=mesh, in_specs=in_specs, out_specs=out_specs, check_vma=False)
```

```python
import functools
import math

import jax
import jax.numpy as jnp
from jax import lax
from jax.experimental import pallas as pl
from jax.experimental.pallas import tpu as pltpu
from jax.sharding import PartitionSpec as P

MESH = pl.DeviceIdType.MESH

HD = 128
ROT = 32
PAGE = 128
BEAM = 8
STEPS = 2


NEG_FILL = -1e30
EPSILON = 1e-05


def rotate(vectors, positions):
    half = ROT // 2
    freq = jnp.exp(jnp.arange(half, dtype=jnp.float32) * (-2.0 * math.log(10000.0) / ROT))
    angles = positions.astype(jnp.float32)[..., None] * freq
    cosine = jnp.concatenate([jnp.cos(angles), jnp.cos(angles)], axis=-1)[..., None, :]
    sine = jnp.concatenate([jnp.sin(angles), jnp.sin(angles)], axis=-1)[..., None, :]
    turned = vectors[..., :ROT]
    swapped = jnp.concatenate([-turned[..., half:], turned[..., :half]], axis=-1)
    return jnp.concatenate([turned * cosine + swapped * sine, vectors[..., ROT:]], axis=-1)


def pick_rows(table, index):
    flat = table.reshape(table.shape[0], -1)
    hot = (index.reshape(-1)[:, None] == jnp.arange(table.shape[0], dtype=jnp.int32)[None, :])
    taken = jnp.dot(hot.astype(table.dtype), flat, preferred_element_type=jnp.float32)
    return taken.astype(table.dtype).reshape(index.shape + table.shape[1:])


def rotate_rows(rows, positions, head_count):
    half = ROT // 2
    freq = jnp.exp(jnp.arange(half, dtype=jnp.float32) * (-2.0 * math.log(10000.0) / ROT))
    angles = positions.astype(jnp.float32)[:, None] * freq[None, :]
    cosine = jnp.concatenate([jnp.cos(angles), jnp.cos(angles)], axis=1)
    sine = jnp.concatenate([jnp.sin(angles), jnp.sin(angles)], axis=1)
    parts = []
    for head in range(head_count):
        base = head * HD
        turned = rows[:, base : base + ROT]
        swapped = jnp.concatenate([-turned[:, half:], turned[:, :half]], axis=1)
        parts += [turned * cosine + swapped * sine, rows[:, base + ROT : base + HD]]
    return jnp.concatenate(parts, axis=1)


def exchange_kernel(axis, n, gather, x_ref, out_ref, send_sem, recv_sem, local_sem):
    me = lax.axis_index(axis)
    barrier = pltpu.get_barrier_semaphore()
    for k in range(1, n):
        pl.semaphore_signal(
            barrier, inc=1, device_id={axis: lax.rem(me + k, n)}, device_id_type=MESH
        )
    pl.semaphore_wait(barrier, n - 1)
    local = pltpu.make_async_copy(x_ref if gather else x_ref.at[me], out_ref.at[me], local_sem)
    local.start()
    copies = []
    for k in range(1, n):
        dest = lax.rem(me + k, n)
        copy = pltpu.make_async_remote_copy(
            src_ref=x_ref if gather else x_ref.at[dest],
            dst_ref=out_ref.at[me],
            send_sem=send_sem.at[k],
            recv_sem=recv_sem.at[k],
            device_id={axis: dest},
            device_id_type=MESH,
        )
        copy.start()
        copies.append(copy)
    for copy in copies:
        copy.wait()
    local.wait()


def exchange_gelu_kernel(axis, n, x_ref, hidden_ref, out_ref, act_ref, send_sem, recv_sem, local_sem):
    me = lax.axis_index(axis)
    barrier = pltpu.get_barrier_semaphore()
    for k in range(1, n):
        pl.semaphore_signal(
            barrier, inc=1, device_id={axis: lax.rem(me + k, n)}, device_id_type=MESH
        )
    pl.semaphore_wait(barrier, n - 1)
    local = pltpu.make_async_copy(x_ref.at[me], out_ref.at[me], local_sem)
    local.start()
    copies = []
    for k in range(1, n):
        dest = lax.rem(me + k, n)
        copy = pltpu.make_async_remote_copy(
            src_ref=x_ref.at[dest],
            dst_ref=out_ref.at[me],
            send_sem=send_sem.at[k],
            recv_sem=recv_sem.at[k],
            device_id={axis: dest},
            device_id_type=MESH,
        )
        copy.start()
        copies.append(copy)
    tile = 128

    @pl.loop(0, hidden_ref.shape[0] // tile)
    def _(index):
        rows = pl.ds(pl.multiple_of(index * tile, tile), tile)
        values = hidden_ref[rows, :].astype(jnp.float32)
        gelu = 0.5 * values * (1.0 + lax.erf(values * (1.0 / math.sqrt(2.0))))
        act_ref[rows, :] = gelu.astype(act_ref.dtype)

    for copy in copies:
        copy.wait()
    local.wait()


def exchange_gelu(x, hidden, axis, n, collective_id):
    return pl.pallas_call(
        functools.partial(exchange_gelu_kernel, axis, n),
        out_shape=(
            jax.ShapeDtypeStruct(x.shape, x.dtype),
            jax.ShapeDtypeStruct(hidden.shape, jnp.bfloat16),
        ),
        in_specs=[pl.BlockSpec(memory_space=pltpu.VMEM)] * 2,
        out_specs=(pl.BlockSpec(memory_space=pltpu.VMEM),) * 2,
        scratch_shapes=[
            pltpu.SemaphoreType.DMA((n,)),
            pltpu.SemaphoreType.DMA((n,)),
            pltpu.SemaphoreType.DMA(()),
        ],
        compiler_params=pltpu.CompilerParams(
            collective_id=collective_id, has_side_effects=True
        ),
        cost_estimate=pl.CostEstimate(
            flops=20 * hidden.size,
            transcendentals=hidden.size,
            bytes_accessed=2 * n * x.size * x.dtype.itemsize + 4 * hidden.size,
        ),
    )(x, hidden)


def gather_grid_kernel(axis, side, x_ref, out_ref, send_sem, recv_sem, local_sem):
    me = lax.axis_index(axis)
    row, col = me // side, me % side
    row_peers = [row * side + lax.rem(col + k, side) for k in range(1, side)]
    col_peers = [lax.rem(row + k, side) * side + col for k in range(1, side)]
    barrier = pltpu.get_barrier_semaphore()
    for peer in row_peers + col_peers:
        pl.semaphore_signal(barrier, inc=1, device_id={axis: peer}, device_id_type=MESH)
    pl.semaphore_wait(barrier, 2 * (side - 1))
    local = pltpu.make_async_copy(x_ref, out_ref.at[me], local_sem)
    local.start()
    first = []
    for k, peer in enumerate(row_peers):
        copy = pltpu.make_async_remote_copy(
            src_ref=x_ref,
            dst_ref=out_ref.at[me],
            send_sem=send_sem.at[0, k],
            recv_sem=recv_sem.at[0, k],
            device_id={axis: peer},
            device_id_type=MESH,
        )
        copy.start()
        first.append(copy)
    for copy in first:
        copy.wait()
    local.wait()
    slab = out_ref.at[pl.ds(row * side, side)]
    second = []
    for k, peer in enumerate(col_peers):
        copy = pltpu.make_async_remote_copy(
            src_ref=slab,
            dst_ref=slab,
            send_sem=send_sem.at[1, k],
            recv_sem=recv_sem.at[1, k],
            device_id={axis: peer},
            device_id_type=MESH,
        )
        copy.start()
        second.append(copy)
    for copy in second:
        copy.wait()


def gather_grid(x, axis, n, collective_id):
    side = math.isqrt(n)
    return pl.pallas_call(
        functools.partial(gather_grid_kernel, axis, side),
        out_shape=jax.ShapeDtypeStruct((n,) + x.shape, x.dtype),
        in_specs=[pl.BlockSpec(memory_space=pltpu.VMEM)],
        out_specs=pl.BlockSpec(memory_space=pltpu.VMEM),
        scratch_shapes=[
            pltpu.SemaphoreType.DMA((2, side - 1)),
            pltpu.SemaphoreType.DMA((2, side - 1)),
            pltpu.SemaphoreType.DMA(()),
        ],
        compiler_params=pltpu.CompilerParams(
            collective_id=collective_id, has_side_effects=True
        ),
        cost_estimate=pl.CostEstimate(
            flops=0, transcendentals=0, bytes_accessed=2 * n * x.size * x.dtype.itemsize
        ),
    )(x)


def exchange(x, axis, n, gather, collective_id):
    shape = (n,) + (x.shape if gather else x.shape[1:])
    return pl.pallas_call(
        functools.partial(exchange_kernel, axis, n, gather),
        out_shape=jax.ShapeDtypeStruct(shape, x.dtype),
        in_specs=[pl.BlockSpec(memory_space=pltpu.VMEM)],
        out_specs=pl.BlockSpec(memory_space=pltpu.VMEM),
        scratch_shapes=[
            pltpu.SemaphoreType.DMA((n,)),
            pltpu.SemaphoreType.DMA((n,)),
            pltpu.SemaphoreType.DMA(()),
        ],
        compiler_params=pltpu.CompilerParams(
            collective_id=collective_id, has_side_effects=True
        ),
        cost_estimate=pl.CostEstimate(
            flops=0, transcendentals=0, bytes_accessed=2 * n * x.size * x.dtype.itemsize
        ),
    )(x)


def exchange_flat(x, axis, n, gather, collective_id):
    lead = () if gather else x.shape[:1]
    block_shape = x.shape if gather else x.shape[1:]
    size = math.prod(block_shape)
    padded = -(-size // 128) * 128
    flat = x.reshape(lead + (size,))
    flat = jnp.pad(flat, [(0, 0)] * len(lead) + [(0, padded - size)])
    flat = flat.reshape(lead + (padded // 128, 128))
    out = exchange(flat, axis, n, gather, collective_id)
    return out.reshape(n, padded)[:, :size].reshape((n,) + block_shape)


def row_normalize(values, collective_id):
    width = values.shape[-1]
    local_mean = jnp.mean(values, axis=-1)
    centred = values - local_mean[..., None]
    local_m2 = jnp.sum(centred * centred, axis=-1)
    stats = jnp.stack([local_mean, local_m2], axis=0)
    stats = exchange_flat(stats, "req", lax.axis_size("req"), True, collective_id)
    stats = jnp.moveaxis(stats, 1, -1)
    means = stats[..., 0]
    row_mean = jnp.mean(means, axis=0)
    spread = means - row_mean
    row_m2 = jnp.sum(stats[..., 1], axis=0) + width * jnp.sum(spread * spread, axis=0)
    row_var = row_m2 / (width * stats.shape[0])
    return (values - row_mean[..., None]) * lax.rsqrt(row_var + EPSILON)[..., None]


def shards(
    inputs,
    norm_gains,
    attn_weight,
    up_weight,
    dense_weight,
    down_weight,
    next_weight,
    cache_keys,
    cache_values,
    lengths,
    slot_table,
    parents,
):
    scale = 1.0 / math.sqrt(HD)
    highest = lax.Precision.HIGHEST
    steps, local_rows, local_width = inputs.shape
    own_count = parents.shape[1]
    request_count = lengths.shape[0]
    beam_total = request_count * BEAM
    head_count = dense_weight.shape[0] // HD
    triple_width = attn_weight.shape[1]
    slot_count = slot_table.shape[1]
    req_size = beam_total // own_count
    mlp_size = beam_total // local_rows
    offset = lax.axis_index("req") * own_count
    beam_group = jnp.arange(beam_total, dtype=jnp.int32) // BEAM
    all_positions = lengths[beam_group][None, :] + jnp.arange(steps, dtype=jnp.int32)[:, None]
    own_group = jnp.arange(own_count, dtype=jnp.int32) // BEAM
    slot_owner = slot_table[0]
    slot_pageno = slot_table[1]
    valid_owner = jnp.maximum(slot_owner, 0)
    token_pos = slot_pageno[:, None] * PAGE + jnp.arange(PAGE, dtype=jnp.int32)[None, :]
    live = (slot_owner[:, None] >= 0) & (token_pos < lengths[valid_owner][:, None])
    live_wide = live[None, :, None, None, :]
    owner_mask = slot_owner[:, None] == jnp.arange(request_count, dtype=jnp.int32)[None, :]
    owner_float = owner_mask.astype(jnp.float32)
    gather_rows = valid_owner[:, None] * BEAM + jnp.arange(BEAM, dtype=jnp.int32)[None, :]

    block = inputs.astype(jnp.float32)
    rows_all = gather_grid(inputs, "mlp", mlp_size, 0).reshape(steps * beam_total, -1)
    normed = row_normalize(rows_all.astype(jnp.float32), 3)
    attn_in = (normed * norm_gains[0]).astype(jnp.bfloat16)
    mlp_in = (normed * norm_gains[1]).astype(jnp.bfloat16)
    grouped = (
        attn_weight.reshape(local_width, head_count, 3, HD)
        .transpose(0, 2, 1, 3)
        .reshape(local_width, triple_width)
    )
    first = jnp.dot(attn_in, grouped, preferred_element_type=jnp.float32)
    second = jnp.dot(mlp_in, up_weight, preferred_element_type=jnp.float32)
    partial_sums = jnp.concatenate([first, second], axis=1)
    summed_all = lax.psum(partial_sums.astype(jnp.bfloat16), "req")
    width = head_count * HD
    row = jnp.arange(steps * beam_total, dtype=jnp.int32)
    beam_lengths = jnp.broadcast_to(lengths[:, None], (request_count, BEAM)).reshape(
        mlp_size, 1, local_rows
    )
    row_positions = (
        beam_lengths + jnp.arange(steps, dtype=jnp.int32)[None, :, None]
    ).reshape(steps * beam_total)
    queries_rows = rotate_rows(
        summed_all[:, :width].astype(jnp.float32), row_positions, head_count
    ).astype(jnp.bfloat16)
    keys_rows = rotate_rows(
        summed_all[:, width : 2 * width].astype(jnp.float32), row_positions, head_count
    ).astype(jnp.bfloat16)
    per_own = own_count // local_rows
    own_start = lax.axis_index("req") * (per_own * steps * local_rows)

    def own_of(rows):
        return (
            lax.dynamic_slice_in_dim(rows, own_start, per_own * steps * local_rows, 0)
            .reshape(per_own, steps, local_rows, -1)
            .transpose(1, 0, 2, 3)
            .reshape(steps, own_count, head_count, HD)
        )

    queries_own = own_of(queries_rows)
    keys_new = own_of(keys_rows)
    values_new = own_of(summed_all[:, 2 * width : 3 * width])

    chosen_rows = (
        (gather_rows // local_rows) * (steps * local_rows)
        + jnp.arange(steps, dtype=jnp.int32)[:, None, None] * local_rows
        + gather_rows % local_rows
    )
    chosen = pick_rows(queries_rows, chosen_rows)
    head_scores = [
        jnp.einsum(
            "zsbd,std->zsbt",
            chosen[..., head * HD : (head + 1) * HD],
            cache_keys[:, :, head * HD : (head + 1) * HD],
            preferred_element_type=jnp.float32,
        )
        for head in range(head_count)
    ]
    scores = jnp.stack(head_scores, axis=3) * scale
    masked = jnp.where(live_wide, scores, NEG_FILL)
    slot_top = jnp.max(masked, axis=4)
    weights = jnp.where(live_wide, jnp.exp(masked - slot_top[..., None]), 0.0)
    slot_total = jnp.sum(weights, axis=4)
    rounded = weights.astype(jnp.bfloat16)
    slot_out = jnp.stack(
        [
            jnp.einsum(
                "zsbt,std->zsbd",
                rounded[:, :, :, head],
                cache_values[:, :, head * HD : (head + 1) * HD],
                preferred_element_type=jnp.float32,
            )
            for head in range(head_count)
        ],
        axis=3,
    )
    request_top = jnp.max(
        jnp.where(owner_mask[None, :, :, None, None], slot_top[:, :, None], NEG_FILL), axis=1
    )
    top_high = request_top.astype(jnp.bfloat16)
    top_low = (request_top - top_high.astype(jnp.float32)).astype(jnp.bfloat16)
    request_top = top_high.astype(jnp.float32) + top_low.astype(jnp.float32)
    factor = jnp.where(
        slot_owner[None, :, None, None] >= 0,
        jnp.exp(slot_top - request_top[:, valid_owner]),
        0.0,
    )
    page_total = jnp.einsum(
        "sr,zsbh->zrbh", owner_float, slot_total * factor, precision=highest
    ).reshape(steps, beam_total, head_count)
    page_out = jnp.einsum(
        "sr,zsbhd->zrbhd", owner_float, slot_out * factor[..., None], precision=highest
    ).reshape(steps, beam_total, head_count, HD)
    stats = jnp.concatenate(
        [
            page_total.astype(jnp.bfloat16),
            top_high.reshape(steps, beam_total, head_count),
            top_low.reshape(steps, beam_total, head_count),
        ],
        axis=-1,
    )
    packed = jnp.concatenate(
        [
            page_out.astype(jnp.bfloat16).reshape(steps, beam_total, head_count * HD),
            jnp.pad(stats, ((0, 0), (0, 0), (0, HD - 3 * head_count))),
        ],
        axis=-1,
    )
    packed = packed.reshape(steps, req_size, own_count, -1).transpose(1, 0, 2, 3)
    held, activated_all = exchange_gelu(packed, summed_all[:, triple_width:], "req", req_size, 5)
    held = held.astype(jnp.float32)
    base = head_count * HD
    held_top = held[..., base + head_count : base + 2 * head_count] + held[
        ..., base + 2 * head_count : base + 3 * head_count
    ]
    own_top = jnp.max(held_top, axis=0)
    rescale = jnp.exp(held_top - own_top)
    own_total = jnp.sum(held[..., base : base + head_count] * rescale, axis=0)
    own_out = jnp.stack(
        [
            jnp.sum(held[..., head * HD : (head + 1) * HD] * rescale[..., head : head + 1], axis=0)
            for head in range(head_count)
        ],
        axis=2,
    )

    source = own_group * BEAM + parents[0]
    attended_steps = []
    for step_index in range(steps):
        tail_keys = [pick_rows(keys_new[prior], source) for prior in range(step_index)]
        tail_values = [pick_rows(values_new[prior], source) for prior in range(step_index)]
        history_keys = jnp.stack(tail_keys + [keys_new[step_index]], axis=0)
        history_values = jnp.stack(tail_values + [values_new[step_index]], axis=0)
        own_scores = (
            jnp.einsum(
                "bhd,nbhd->bhn",
                queries_own[step_index],
                history_keys,
                preferred_element_type=jnp.float32,
            )
            * scale
        )
        top = jnp.maximum(own_top[step_index], jnp.max(own_scores, axis=2))
        page_factor = jnp.exp(own_top[step_index] - top)
        own_weights = jnp.exp(own_scores - top[..., None])
        total = own_total[step_index] * page_factor + jnp.sum(own_weights, axis=2)
        summed = own_out[step_index] * page_factor[..., None] + jnp.einsum(
            "bhn,nbhd->bhd",
            own_weights.astype(jnp.bfloat16),
            history_values,
            preferred_element_type=jnp.float32,
        )
        attended_steps.append(
            (summed / total[..., None]).astype(jnp.bfloat16).reshape(own_count, head_count * HD)
        )
    attended = jnp.stack(attended_steps)
    attended_all = exchange(attended, "req", req_size, True, 6)
    attended_msi = (
        attended_all.reshape(req_size, steps, per_own, local_rows, -1)
        .transpose(0, 2, 1, 3, 4)
        .reshape(steps * beam_total, -1)
    )
    update_partial = (
        jnp.dot(attended_msi, dense_weight, preferred_element_type=jnp.float32)
        + jnp.dot(activated_all, down_weight, preferred_element_type=jnp.float32)
    ).astype(jnp.bfloat16)
    update = jnp.sum(
        exchange(
            update_partial.reshape(mlp_size, steps * local_rows, local_width),
            "mlp",
            mlp_size,
            False,
            1,
        ).astype(jnp.float32),
        axis=0,
    )
    layer = (block + update.reshape(steps, local_rows, local_width)).astype(jnp.bfloat16)
    next_in = (row_normalize(layer.astype(jnp.float32), 4) * norm_gains[2]).astype(jnp.bfloat16)
    gathered = gather_grid(next_in, "mlp", mlp_size, 2).reshape(steps * beam_total, -1)
    next_partial = jnp.dot(gathered, next_weight, preferred_element_type=jnp.float32)
    next_parts = exchange(
        next_partial.astype(jnp.bfloat16).reshape(req_size, -1, next_partial.shape[1]),
        "req",
        req_size,
        False,
        7,
    )
    next_out = jnp.sum(next_parts.astype(jnp.float32), axis=0).astype(jnp.bfloat16)
    next_out = (
        next_out.reshape(per_own, steps, local_rows, -1)
        .transpose(1, 0, 2, 3)
        .reshape(steps, own_count, -1)
    )
    return (layer, next_out)


def solution(mesh):
    in_specs = (
        P(None, "mlp", "req"),
        P(None, "req"),
        P("req", "mlp"),
        P("req", "mlp"),
        P("mlp", "req"),
        P("mlp", "req"),
        P("req", "mlp"),
        P("req", None, "mlp"),
        P("req", None, "mlp"),
        P(),
        P(None, "req"),
        P(None, "req"),
    )
    out_specs = (P(None, "mlp", "req"), P(None, "req", "mlp"))
    return jax.shard_map(shards, mesh=mesh, in_specs=in_specs, out_specs=out_specs, check_vma=False)
```

```python
import functools
import math

import jax
import jax.numpy as jnp
from jax import lax
from jax.experimental import pallas as pl
from jax.experimental.pallas import tpu as pltpu
from jax.sharding import PartitionSpec as P

MESH = pl.DeviceIdType.MESH

HD = 128
ROT = 32
PAGE = 128
BEAM = 8
STEPS = 2


NEG_FILL = -1e30
EPSILON = 1e-05


def rotate(vectors, positions):
    half = ROT // 2
    freq = jnp.exp(jnp.arange(half, dtype=jnp.float32) * (-2.0 * math.log(10000.0) / ROT))
    angles = positions.astype(jnp.float32)[..., None] * freq
    cosine = jnp.concatenate([jnp.cos(angles), jnp.cos(angles)], axis=-1)[..., None, :]
    sine = jnp.concatenate([jnp.sin(angles), jnp.sin(angles)], axis=-1)[..., None, :]
    turned = vectors[..., :ROT]
    swapped = jnp.concatenate([-turned[..., half:], turned[..., :half]], axis=-1)
    return jnp.concatenate([turned * cosine + swapped * sine, vectors[..., ROT:]], axis=-1)


def pick_rows(table, index):
    flat = table.reshape(table.shape[0], -1)
    hot = (index.reshape(-1)[:, None] == jnp.arange(table.shape[0], dtype=jnp.int32)[None, :])
    taken = jnp.dot(hot.astype(table.dtype), flat, preferred_element_type=jnp.float32)
    return taken.astype(table.dtype).reshape(index.shape + table.shape[1:])


def rotate_rows(rows, positions, head_count):
    half = ROT // 2
    freq = jnp.exp(jnp.arange(half, dtype=jnp.float32) * (-2.0 * math.log(10000.0) / ROT))
    angles = positions.astype(jnp.float32)[:, None] * freq[None, :]
    cosine = jnp.concatenate([jnp.cos(angles), jnp.cos(angles)], axis=1)
    sine = jnp.concatenate([jnp.sin(angles), jnp.sin(angles)], axis=1)
    parts = []
    for head in range(head_count):
        base = head * HD
        turned = rows[:, base : base + ROT]
        swapped = jnp.concatenate([-turned[:, half:], turned[:, :half]], axis=1)
        parts += [turned * cosine + swapped * sine, rows[:, base + ROT : base + HD]]
    return jnp.concatenate(parts, axis=1)


def exchange_kernel(axis, n, gather, x_ref, out_ref, send_sem, recv_sem, local_sem):
    me = lax.axis_index(axis)
    barrier = pltpu.get_barrier_semaphore()
    for k in range(1, n):
        pl.semaphore_signal(
            barrier, inc=1, device_id={axis: lax.rem(me + k, n)}, device_id_type=MESH
        )
    pl.semaphore_wait(barrier, n - 1)
    local = pltpu.make_async_copy(x_ref if gather else x_ref.at[me], out_ref.at[me], local_sem)
    local.start()
    copies = []
    for k in range(1, n):
        dest = lax.rem(me + k, n)
        copy = pltpu.make_async_remote_copy(
            src_ref=x_ref if gather else x_ref.at[dest],
            dst_ref=out_ref.at[me],
            send_sem=send_sem.at[k],
            recv_sem=recv_sem.at[k],
            device_id={axis: dest},
            device_id_type=MESH,
        )
        copy.start()
        copies.append(copy)
    for copy in copies:
        copy.wait()
    local.wait()


def exchange_gelu_kernel(axis, n, x_ref, hidden_ref, out_ref, act_ref, send_sem, recv_sem, local_sem):
    me = lax.axis_index(axis)
    barrier = pltpu.get_barrier_semaphore()
    for k in range(1, n):
        pl.semaphore_signal(
            barrier, inc=1, device_id={axis: lax.rem(me + k, n)}, device_id_type=MESH
        )
    pl.semaphore_wait(barrier, n - 1)
    local = pltpu.make_async_copy(x_ref.at[me], out_ref.at[me], local_sem)
    local.start()
    copies = []
    for k in range(1, n):
        dest = lax.rem(me + k, n)
        copy = pltpu.make_async_remote_copy(
            src_ref=x_ref.at[dest],
            dst_ref=out_ref.at[me],
            send_sem=send_sem.at[k],
            recv_sem=recv_sem.at[k],
            device_id={axis: dest},
            device_id_type=MESH,
        )
        copy.start()
        copies.append(copy)
    tile = 128

    @pl.loop(0, hidden_ref.shape[0] // tile)
    def _(index):
        rows = pl.ds(pl.multiple_of(index * tile, tile), tile)
        values = hidden_ref[rows, :].astype(jnp.float32)
        gelu = 0.5 * values * (1.0 + lax.erf(values * (1.0 / math.sqrt(2.0))))
        act_ref[rows, :] = gelu.astype(act_ref.dtype)

    for copy in copies:
        copy.wait()
    local.wait()


def exchange_gelu(x, hidden, axis, n, collective_id):
    return pl.pallas_call(
        functools.partial(exchange_gelu_kernel, axis, n),
        out_shape=(
            jax.ShapeDtypeStruct(x.shape, x.dtype),
            jax.ShapeDtypeStruct(hidden.shape, jnp.bfloat16),
        ),
        in_specs=[pl.BlockSpec(memory_space=pltpu.VMEM)] * 2,
        out_specs=(pl.BlockSpec(memory_space=pltpu.VMEM),) * 2,
        scratch_shapes=[
            pltpu.SemaphoreType.DMA((n,)),
            pltpu.SemaphoreType.DMA((n,)),
            pltpu.SemaphoreType.DMA(()),
        ],
        compiler_params=pltpu.CompilerParams(
            collective_id=collective_id, has_side_effects=True
        ),
        cost_estimate=pl.CostEstimate(
            flops=20 * hidden.size,
            transcendentals=hidden.size,
            bytes_accessed=2 * n * x.size * x.dtype.itemsize + 4 * hidden.size,
        ),
    )(x, hidden)


def gather_grid_kernel(axis, side, x_ref, out_ref, send_sem, recv_sem, local_sem):
    me = lax.axis_index(axis)
    row, col = me // side, me % side
    row_peers = [row * side + lax.rem(col + k, side) for k in range(1, side)]
    col_peers = [lax.rem(row + k, side) * side + col for k in range(1, side)]
    barrier = pltpu.get_barrier_semaphore()
    for peer in row_peers + col_peers:
        pl.semaphore_signal(barrier, inc=1, device_id={axis: peer}, device_id_type=MESH)
    pl.semaphore_wait(barrier, 2 * (side - 1))
    local = pltpu.make_async_copy(x_ref, out_ref.at[me], local_sem)
    local.start()
    first = []
    for k, peer in enumerate(row_peers):
        copy = pltpu.make_async_remote_copy(
            src_ref=x_ref,
            dst_ref=out_ref.at[me],
            send_sem=send_sem.at[0, k],
            recv_sem=recv_sem.at[0, k],
            device_id={axis: peer},
            device_id_type=MESH,
        )
        copy.start()
        first.append(copy)
    for copy in first:
        copy.wait()
    local.wait()
    slab = out_ref.at[pl.ds(row * side, side)]
    second = []
    for k, peer in enumerate(col_peers):
        copy = pltpu.make_async_remote_copy(
            src_ref=slab,
            dst_ref=slab,
            send_sem=send_sem.at[1, k],
            recv_sem=recv_sem.at[1, k],
            device_id={axis: peer},
            device_id_type=MESH,
        )
        copy.start()
        second.append(copy)
    for copy in second:
        copy.wait()


def gather_grid(x, axis, n, collective_id):
    side = math.isqrt(n)
    return pl.pallas_call(
        functools.partial(gather_grid_kernel, axis, side),
        out_shape=jax.ShapeDtypeStruct((n,) + x.shape, x.dtype),
        in_specs=[pl.BlockSpec(memory_space=pltpu.VMEM)],
        out_specs=pl.BlockSpec(memory_space=pltpu.VMEM),
        scratch_shapes=[
            pltpu.SemaphoreType.DMA((2, side - 1)),
            pltpu.SemaphoreType.DMA((2, side - 1)),
            pltpu.SemaphoreType.DMA(()),
        ],
        compiler_params=pltpu.CompilerParams(
            collective_id=collective_id, has_side_effects=True
        ),
        cost_estimate=pl.CostEstimate(
            flops=0, transcendentals=0, bytes_accessed=2 * n * x.size * x.dtype.itemsize
        ),
    )(x)


def exchange(x, axis, n, gather, collective_id):
    shape = (n,) + (x.shape if gather else x.shape[1:])
    return pl.pallas_call(
        functools.partial(exchange_kernel, axis, n, gather),
        out_shape=jax.ShapeDtypeStruct(shape, x.dtype),
        in_specs=[pl.BlockSpec(memory_space=pltpu.VMEM)],
        out_specs=pl.BlockSpec(memory_space=pltpu.VMEM),
        scratch_shapes=[
            pltpu.SemaphoreType.DMA((n,)),
            pltpu.SemaphoreType.DMA((n,)),
            pltpu.SemaphoreType.DMA(()),
        ],
        compiler_params=pltpu.CompilerParams(
            collective_id=collective_id, has_side_effects=True
        ),
        cost_estimate=pl.CostEstimate(
            flops=0, transcendentals=0, bytes_accessed=2 * n * x.size * x.dtype.itemsize
        ),
    )(x)


def exchange_flat(x, axis, n, gather, collective_id):
    lead = () if gather else x.shape[:1]
    block_shape = x.shape if gather else x.shape[1:]
    size = math.prod(block_shape)
    padded = -(-size // 128) * 128
    flat = x.reshape(lead + (size,))
    flat = jnp.pad(flat, [(0, 0)] * len(lead) + [(0, padded - size)])
    flat = flat.reshape(lead + (padded // 128, 128))
    out = exchange(flat, axis, n, gather, collective_id)
    return out.reshape(n, padded)[:, :size].reshape((n,) + block_shape)


def row_normalize(values, collective_id):
    width = values.shape[-1]
    local_mean = jnp.mean(values, axis=-1)
    centred = values - local_mean[..., None]
    local_m2 = jnp.sum(centred * centred, axis=-1)
    stats = jnp.stack([local_mean, local_m2], axis=0)
    stats = exchange_flat(stats, "req", lax.axis_size("req"), True, collective_id)
    stats = jnp.moveaxis(stats, 1, -1)
    means = stats[..., 0]
    row_mean = jnp.mean(means, axis=0)
    spread = means - row_mean
    row_m2 = jnp.sum(stats[..., 1], axis=0) + width * jnp.sum(spread * spread, axis=0)
    row_var = row_m2 / (width * stats.shape[0])
    return (values - row_mean[..., None]) * lax.rsqrt(row_var + EPSILON)[..., None]


def shards(
    inputs,
    norm_gains,
    attn_weight,
    up_weight,
    dense_weight,
    down_weight,
    next_weight,
    cache_keys,
    cache_values,
    lengths,
    slot_table,
    parents,
):
    scale = 1.0 / math.sqrt(HD)
    highest = lax.Precision.HIGHEST
    steps, local_rows, local_width = inputs.shape
    own_count = parents.shape[1]
    request_count = lengths.shape[0]
    beam_total = request_count * BEAM
    head_count = dense_weight.shape[0] // HD
    triple_width = attn_weight.shape[1]
    slot_count = slot_table.shape[1]
    req_size = beam_total // own_count
    mlp_size = beam_total // local_rows
    offset = lax.axis_index("req") * own_count
    beam_group = jnp.arange(beam_total, dtype=jnp.int32) // BEAM
    all_positions = lengths[beam_group][None, :] + jnp.arange(steps, dtype=jnp.int32)[:, None]
    own_group = jnp.arange(own_count, dtype=jnp.int32) // BEAM
    slot_owner = slot_table[0]
    slot_pageno = slot_table[1]
    valid_owner = jnp.maximum(slot_owner, 0)
    token_pos = slot_pageno[:, None] * PAGE + jnp.arange(PAGE, dtype=jnp.int32)[None, :]
    live = (slot_owner[:, None] >= 0) & (token_pos < lengths[valid_owner][:, None])
    live_wide = live[None, :, None, None, :]
    owner_mask = slot_owner[:, None] == jnp.arange(request_count, dtype=jnp.int32)[None, :]
    owner_float = owner_mask.astype(jnp.float32)
    gather_rows = valid_owner[:, None] * BEAM + jnp.arange(BEAM, dtype=jnp.int32)[None, :]

    block = inputs.astype(jnp.float32)
    rows_all = gather_grid(inputs, "mlp", mlp_size, 0).reshape(steps * beam_total, -1)
    normed = row_normalize(rows_all.astype(jnp.float32), 3)
    attn_in = (normed * norm_gains[0]).astype(jnp.bfloat16)
    mlp_in = (normed * norm_gains[1]).astype(jnp.bfloat16)
    grouped = (
        attn_weight.reshape(local_width, head_count, 3, HD)
        .transpose(0, 2, 1, 3)
        .reshape(local_width, triple_width)
    )
    first = jnp.dot(attn_in, grouped, preferred_element_type=jnp.float32)
    second = jnp.dot(mlp_in, up_weight, preferred_element_type=jnp.float32)
    partial_sums = jnp.concatenate([first, second], axis=1)
    summed_all = lax.psum(partial_sums.astype(jnp.bfloat16), "req")
    width = head_count * HD
    row = jnp.arange(steps * beam_total, dtype=jnp.int32)
    beam_lengths = jnp.broadcast_to(lengths[:, None], (request_count, BEAM)).reshape(
        mlp_size, 1, local_rows
    )
    row_positions = (
        beam_lengths + jnp.arange(steps, dtype=jnp.int32)[None, :, None]
    ).reshape(steps * beam_total)
    queries_rows = rotate_rows(
        summed_all[:, :width].astype(jnp.float32), row_positions, head_count
    ).astype(jnp.bfloat16)
    keys_rows = rotate_rows(
        summed_all[:, width : 2 * width].astype(jnp.float32), row_positions, head_count
    ).astype(jnp.bfloat16)
    per_own = own_count // local_rows
    own_start = lax.axis_index("req") * (per_own * steps * local_rows)

    def own_of(rows):
        return (
            lax.dynamic_slice_in_dim(rows, own_start, per_own * steps * local_rows, 0)
            .reshape(per_own, steps, local_rows, -1)
            .transpose(1, 0, 2, 3)
            .reshape(steps, own_count, head_count, HD)
        )

    queries_own = own_of(queries_rows)
    keys_new = own_of(keys_rows)
    values_new = own_of(summed_all[:, 2 * width : 3 * width])

    chosen_rows = (
        (gather_rows // local_rows) * (steps * local_rows)
        + jnp.arange(steps, dtype=jnp.int32)[:, None, None] * local_rows
        + gather_rows % local_rows
    )
    chosen = pick_rows(queries_rows, chosen_rows)
    head_scores = [
        jnp.einsum(
            "zsbd,std->zsbt",
            chosen[..., head * HD : (head + 1) * HD],
            cache_keys[:, :, head * HD : (head + 1) * HD],
            preferred_element_type=jnp.float32,
        )
        for head in range(head_count)
    ]
    scores = jnp.stack(head_scores, axis=3) * scale
    masked = jnp.where(live_wide, scores, NEG_FILL)
    slot_top = jnp.max(masked, axis=4)
    weights = jnp.where(live_wide, jnp.exp(masked - slot_top[..., None]), 0.0)
    slot_total = jnp.sum(weights, axis=4)
    rounded = weights.astype(jnp.bfloat16)
    slot_out = jnp.stack(
        [
            jnp.einsum(
                "zsbt,std->zsbd",
                rounded[:, :, :, head],
                cache_values[:, :, head * HD : (head + 1) * HD],
                preferred_element_type=jnp.float32,
            )
            for head in range(head_count)
        ],
        axis=3,
    )
    request_top = jnp.max(
        jnp.where(owner_mask[None, :, :, None, None], slot_top[:, :, None], NEG_FILL), axis=1
    )
    top_high = request_top.astype(jnp.bfloat16)
    top_low = (request_top - top_high.astype(jnp.float32)).astype(jnp.bfloat16)
    request_top = top_high.astype(jnp.float32) + top_low.astype(jnp.float32)
    factor = jnp.where(
        (slot_owner[None, :, None, None] >= 0) & (slot_top > 0.5 * NEG_FILL),
        jnp.exp(slot_top - request_top[:, valid_owner]),
        0.0,
    )
    page_total = jnp.einsum(
        "sr,zsbh->zrbh", owner_float, slot_total * factor, precision=highest
    ).reshape(steps, beam_total, head_count)
    page_out = jnp.einsum(
        "sr,zsbhd->zrbhd", owner_float, slot_out * factor[..., None], precision=highest
    ).reshape(steps, beam_total, head_count, HD)
    stats = jnp.concatenate(
        [
            page_total.astype(jnp.bfloat16),
            top_high.reshape(steps, beam_total, head_count),
            top_low.reshape(steps, beam_total, head_count),
        ],
        axis=-1,
    )
    packed = jnp.concatenate(
        [
            page_out.astype(jnp.bfloat16).reshape(steps, beam_total, head_count * HD),
            jnp.pad(stats, ((0, 0), (0, 0), (0, HD - 3 * head_count))),
        ],
        axis=-1,
    )
    packed = packed.reshape(steps, req_size, own_count, -1).transpose(1, 0, 2, 3)
    held, activated_all = exchange_gelu(packed, summed_all[:, triple_width:], "req", req_size, 5)
    held = held.astype(jnp.float32)
    base = head_count * HD
    held_top = held[..., base + head_count : base + 2 * head_count] + held[
        ..., base + 2 * head_count : base + 3 * head_count
    ]
    own_top = jnp.max(held_top, axis=0)
    rescale = jnp.exp(held_top - own_top)
    own_total = jnp.sum(held[..., base : base + head_count] * rescale, axis=0)
    own_out = jnp.stack(
        [
            jnp.sum(held[..., head * HD : (head + 1) * HD] * rescale[..., head : head + 1], axis=0)
            for head in range(head_count)
        ],
        axis=2,
    )

    source = own_group * BEAM + parents[0]
    attended_steps = []
    for step_index in range(steps):
        tail_keys = [pick_rows(keys_new[prior], source) for prior in range(step_index)]
        tail_values = [pick_rows(values_new[prior], source) for prior in range(step_index)]
        history_keys = jnp.stack(tail_keys + [keys_new[step_index]], axis=0)
        history_values = jnp.stack(tail_values + [values_new[step_index]], axis=0)
        own_scores = (
            jnp.einsum(
                "bhd,nbhd->bhn",
                queries_own[step_index],
                history_keys,
                preferred_element_type=jnp.float32,
            )
            * scale
        )
        top = jnp.maximum(own_top[step_index], jnp.max(own_scores, axis=2))
        page_factor = jnp.exp(own_top[step_index] - top)
        own_weights = jnp.exp(own_scores - top[..., None])
        total = own_total[step_index] * page_factor + jnp.sum(own_weights, axis=2)
        summed = own_out[step_index] * page_factor[..., None] + jnp.einsum(
            "bhn,nbhd->bhd",
            own_weights.astype(jnp.bfloat16),
            history_values,
            preferred_element_type=jnp.float32,
        )
        attended_steps.append(
            (summed / total[..., None]).astype(jnp.bfloat16).reshape(own_count, head_count * HD)
        )
    attended = jnp.stack(attended_steps)
    attended_all = exchange(attended, "req", req_size, True, 6)
    attended_msi = (
        attended_all.reshape(req_size, steps, per_own, local_rows, -1)
        .transpose(0, 2, 1, 3, 4)
        .reshape(steps * beam_total, -1)
    )
    update_partial = (
        jnp.dot(attended_msi, dense_weight, preferred_element_type=jnp.float32)
        + jnp.dot(activated_all, down_weight, preferred_element_type=jnp.float32)
    ).astype(jnp.bfloat16)
    update = jnp.sum(
        exchange(
            update_partial.reshape(mlp_size, steps * local_rows, local_width),
            "mlp",
            mlp_size,
            False,
            1,
        ).astype(jnp.float32),
        axis=0,
    )
    layer = (block + update.reshape(steps, local_rows, local_width)).astype(jnp.bfloat16)
    next_in = (row_normalize(layer.astype(jnp.float32), 4) * norm_gains[2]).astype(jnp.bfloat16)
    gathered = gather_grid(next_in, "mlp", mlp_size, 2).reshape(steps * beam_total, -1)
    next_partial = jnp.dot(gathered, next_weight, preferred_element_type=jnp.float32)
    next_out = lax.psum_scatter(
        next_partial.astype(jnp.bfloat16), "req", scatter_dimension=0, tiled=True
    )
    next_out = (
        next_out.reshape(per_own, steps, local_rows, -1)
        .transpose(1, 0, 2, 3)
        .reshape(steps, own_count, -1)
    )
    return (layer, next_out)


def solution(mesh):
    in_specs = (
        P(None, "mlp", "req"),
        P(None, "req"),
        P("req", "mlp"),
        P("req", "mlp"),
        P("mlp", "req"),
        P("mlp", "req"),
        P("req", "mlp"),
        P("req", None, "mlp"),
        P("req", None, "mlp"),
        P(),
        P(None, "req"),
        P(None, "req"),
    )
    out_specs = (P(None, "mlp", "req"), P(None, "req", "mlp"))
    return jax.shard_map(shards, mesh=mesh, in_specs=in_specs, out_specs=out_specs, check_vma=False)
```

```python
import functools
import math

import jax
import jax.numpy as jnp
from jax import lax
from jax.experimental import pallas as pl
from jax.experimental.pallas import tpu as pltpu
from jax.sharding import PartitionSpec as P

MESH = pl.DeviceIdType.MESH

HD = 128
ROT = 32
PAGE = 128
BEAM = 8
STEPS = 2


NEG_FILL = -1e30
EPSILON = 1e-05


def rotate(vectors, positions):
    half = ROT // 2
    freq = jnp.exp(jnp.arange(half, dtype=jnp.float32) * (-2.0 * math.log(10000.0) / ROT))
    angles = positions.astype(jnp.float32)[..., None] * freq
    cosine = jnp.concatenate([jnp.cos(angles), jnp.cos(angles)], axis=-1)[..., None, :]
    sine = jnp.concatenate([jnp.sin(angles), jnp.sin(angles)], axis=-1)[..., None, :]
    turned = vectors[..., :ROT]
    swapped = jnp.concatenate([-turned[..., half:], turned[..., :half]], axis=-1)
    return jnp.concatenate([turned * cosine + swapped * sine, vectors[..., ROT:]], axis=-1)


def pick_rows(table, index):
    flat = table.reshape(table.shape[0], -1)
    hot = (index.reshape(-1)[:, None] == jnp.arange(table.shape[0], dtype=jnp.int32)[None, :])
    taken = jnp.dot(hot.astype(table.dtype), flat, preferred_element_type=jnp.float32)
    return taken.astype(table.dtype).reshape(index.shape + table.shape[1:])


def rotate_rows(rows, positions, head_count):
    half = ROT // 2
    freq = jnp.exp(jnp.arange(half, dtype=jnp.float32) * (-2.0 * math.log(10000.0) / ROT))
    angles = positions.astype(jnp.float32)[:, None] * freq[None, :]
    cosine = jnp.concatenate([jnp.cos(angles), jnp.cos(angles)], axis=1)
    sine = jnp.concatenate([jnp.sin(angles), jnp.sin(angles)], axis=1)
    parts = []
    for head in range(head_count):
        base = head * HD
        turned = rows[:, base : base + ROT]
        swapped = jnp.concatenate([-turned[:, half:], turned[:, :half]], axis=1)
        parts += [turned * cosine + swapped * sine, rows[:, base + ROT : base + HD]]
    return jnp.concatenate(parts, axis=1)


def exchange_kernel(axis, n, gather, x_ref, out_ref, send_sem, recv_sem, local_sem):
    me = lax.axis_index(axis)
    barrier = pltpu.get_barrier_semaphore()
    for k in range(1, n):
        pl.semaphore_signal(
            barrier, inc=1, device_id={axis: lax.rem(me + k, n)}, device_id_type=MESH
        )
    pl.semaphore_wait(barrier, n - 1)
    local = pltpu.make_async_copy(x_ref if gather else x_ref.at[me], out_ref.at[me], local_sem)
    local.start()
    copies = []
    for k in range(1, n):
        dest = lax.rem(me + k, n)
        copy = pltpu.make_async_remote_copy(
            src_ref=x_ref if gather else x_ref.at[dest],
            dst_ref=out_ref.at[me],
            send_sem=send_sem.at[k],
            recv_sem=recv_sem.at[k],
            device_id={axis: dest},
            device_id_type=MESH,
        )
        copy.start()
        copies.append(copy)
    for copy in copies:
        copy.wait()
    local.wait()


def exchange_gelu_kernel(axis, n, x_ref, hidden_ref, out_ref, act_ref, send_sem, recv_sem, local_sem):
    me = lax.axis_index(axis)
    barrier = pltpu.get_barrier_semaphore()
    for k in range(1, n):
        pl.semaphore_signal(
            barrier, inc=1, device_id={axis: lax.rem(me + k, n)}, device_id_type=MESH
        )
    pl.semaphore_wait(barrier, n - 1)
    local = pltpu.make_async_copy(x_ref.at[me], out_ref.at[me], local_sem)
    local.start()
    copies = []
    for k in range(1, n):
        dest = lax.rem(me + k, n)
        copy = pltpu.make_async_remote_copy(
            src_ref=x_ref.at[dest],
            dst_ref=out_ref.at[me],
            send_sem=send_sem.at[k],
            recv_sem=recv_sem.at[k],
            device_id={axis: dest},
            device_id_type=MESH,
        )
        copy.start()
        copies.append(copy)
    tile = 128

    @pl.loop(0, hidden_ref.shape[0] // tile)
    def _(index):
        rows = pl.ds(pl.multiple_of(index * tile, tile), tile)
        values = hidden_ref[rows, :].astype(jnp.float32)
        gelu = 0.5 * values * (1.0 + lax.erf(values * (1.0 / math.sqrt(2.0))))
        act_ref[rows, :] = gelu.astype(act_ref.dtype)

    for copy in copies:
        copy.wait()
    local.wait()


def exchange_gelu(x, hidden, axis, n, collective_id):
    return pl.pallas_call(
        functools.partial(exchange_gelu_kernel, axis, n),
        out_shape=(
            jax.ShapeDtypeStruct(x.shape, x.dtype),
            jax.ShapeDtypeStruct(hidden.shape, jnp.bfloat16),
        ),
        in_specs=[pl.BlockSpec(memory_space=pltpu.VMEM)] * 2,
        out_specs=(pl.BlockSpec(memory_space=pltpu.VMEM),) * 2,
        scratch_shapes=[
            pltpu.SemaphoreType.DMA((n,)),
            pltpu.SemaphoreType.DMA((n,)),
            pltpu.SemaphoreType.DMA(()),
        ],
        compiler_params=pltpu.CompilerParams(
            collective_id=collective_id, has_side_effects=True
        ),
        cost_estimate=pl.CostEstimate(
            flops=20 * hidden.size,
            transcendentals=hidden.size,
            bytes_accessed=2 * n * x.size * x.dtype.itemsize + 4 * hidden.size,
        ),
    )(x, hidden)


def gather_grid_kernel(axis, side, x_ref, out_ref, send_sem, recv_sem, local_sem):
    me = lax.axis_index(axis)
    row, col = me // side, me % side
    row_peers = [row * side + lax.rem(col + k, side) for k in range(1, side)]
    col_peers = [lax.rem(row + k, side) * side + col for k in range(1, side)]
    barrier = pltpu.get_barrier_semaphore()
    for peer in row_peers + col_peers:
        pl.semaphore_signal(barrier, inc=1, device_id={axis: peer}, device_id_type=MESH)
    pl.semaphore_wait(barrier, 2 * (side - 1))
    local = pltpu.make_async_copy(x_ref, out_ref.at[me], local_sem)
    local.start()
    first = []
    for k, peer in enumerate(row_peers):
        copy = pltpu.make_async_remote_copy(
            src_ref=x_ref,
            dst_ref=out_ref.at[me],
            send_sem=send_sem.at[0, k],
            recv_sem=recv_sem.at[0, k],
            device_id={axis: peer},
            device_id_type=MESH,
        )
        copy.start()
        first.append(copy)
    for copy in first:
        copy.wait()
    local.wait()
    slab = out_ref.at[pl.ds(row * side, side)]
    second = []
    for k, peer in enumerate(col_peers):
        copy = pltpu.make_async_remote_copy(
            src_ref=slab,
            dst_ref=slab,
            send_sem=send_sem.at[1, k],
            recv_sem=recv_sem.at[1, k],
            device_id={axis: peer},
            device_id_type=MESH,
        )
        copy.start()
        second.append(copy)
    for copy in second:
        copy.wait()


def gather_grid(x, axis, n, collective_id):
    side = math.isqrt(n)
    return pl.pallas_call(
        functools.partial(gather_grid_kernel, axis, side),
        out_shape=jax.ShapeDtypeStruct((n,) + x.shape, x.dtype),
        in_specs=[pl.BlockSpec(memory_space=pltpu.VMEM)],
        out_specs=pl.BlockSpec(memory_space=pltpu.VMEM),
        scratch_shapes=[
            pltpu.SemaphoreType.DMA((2, side - 1)),
            pltpu.SemaphoreType.DMA((2, side - 1)),
            pltpu.SemaphoreType.DMA(()),
        ],
        compiler_params=pltpu.CompilerParams(
            collective_id=collective_id, has_side_effects=True
        ),
        cost_estimate=pl.CostEstimate(
            flops=0, transcendentals=0, bytes_accessed=2 * n * x.size * x.dtype.itemsize
        ),
    )(x)


def gather_matmul_kernel(axis, n, x_ref, lhs_ref, rhs_ref, out_ref, prod_ref, send_sem, recv_sem, local_sem):
    me = lax.axis_index(axis)
    barrier = pltpu.get_barrier_semaphore()
    for k in range(1, n):
        pl.semaphore_signal(
            barrier, inc=1, device_id={axis: lax.rem(me + k, n)}, device_id_type=MESH
        )
    pl.semaphore_wait(barrier, n - 1)
    local = pltpu.make_async_copy(x_ref, out_ref.at[me], local_sem)
    local.start()
    copies = []
    for k in range(1, n):
        dest = lax.rem(me + k, n)
        copy = pltpu.make_async_remote_copy(
            src_ref=x_ref,
            dst_ref=out_ref.at[me],
            send_sem=send_sem.at[k],
            recv_sem=recv_sem.at[k],
            device_id={axis: dest},
            device_id_type=MESH,
        )
        copy.start()
        copies.append(copy)
    tile = 256

    @pl.loop(0, lhs_ref.shape[0] // tile)
    def _(index):
        rows = pl.ds(pl.multiple_of(index * tile, tile), tile)
        prod_ref[rows, :] = jnp.dot(
            lhs_ref[rows, :], rhs_ref[...], preferred_element_type=jnp.float32
        )

    for copy in copies:
        copy.wait()
    local.wait()


def gather_matmul(x, lhs, rhs, axis, n, collective_id):
    return pl.pallas_call(
        functools.partial(gather_matmul_kernel, axis, n),
        out_shape=(
            jax.ShapeDtypeStruct((n,) + x.shape, x.dtype),
            jax.ShapeDtypeStruct((lhs.shape[0], rhs.shape[1]), jnp.float32),
        ),
        in_specs=[pl.BlockSpec(memory_space=pltpu.VMEM)] * 3,
        out_specs=(pl.BlockSpec(memory_space=pltpu.VMEM),) * 2,
        scratch_shapes=[
            pltpu.SemaphoreType.DMA((n,)),
            pltpu.SemaphoreType.DMA((n,)),
            pltpu.SemaphoreType.DMA(()),
        ],
        compiler_params=pltpu.CompilerParams(
            collective_id=collective_id, has_side_effects=True
        ),
        cost_estimate=pl.CostEstimate(
            flops=2 * lhs.shape[0] * lhs.shape[1] * rhs.shape[1],
            transcendentals=0,
            bytes_accessed=2 * n * x.size * x.dtype.itemsize
            + 2 * (lhs.size + rhs.size)
            + 4 * lhs.shape[0] * rhs.shape[1],
        ),
    )(x, lhs, rhs)


def exchange(x, axis, n, gather, collective_id):
    shape = (n,) + (x.shape if gather else x.shape[1:])
    return pl.pallas_call(
        functools.partial(exchange_kernel, axis, n, gather),
        out_shape=jax.ShapeDtypeStruct(shape, x.dtype),
        in_specs=[pl.BlockSpec(memory_space=pltpu.VMEM)],
        out_specs=pl.BlockSpec(memory_space=pltpu.VMEM),
        scratch_shapes=[
            pltpu.SemaphoreType.DMA((n,)),
            pltpu.SemaphoreType.DMA((n,)),
            pltpu.SemaphoreType.DMA(()),
        ],
        compiler_params=pltpu.CompilerParams(
            collective_id=collective_id, has_side_effects=True
        ),
        cost_estimate=pl.CostEstimate(
            flops=0, transcendentals=0, bytes_accessed=2 * n * x.size * x.dtype.itemsize
        ),
    )(x)


def exchange_flat(x, axis, n, gather, collective_id):
    lead = () if gather else x.shape[:1]
    block_shape = x.shape if gather else x.shape[1:]
    size = math.prod(block_shape)
    padded = -(-size // 128) * 128
    flat = x.reshape(lead + (size,))
    flat = jnp.pad(flat, [(0, 0)] * len(lead) + [(0, padded - size)])
    flat = flat.reshape(lead + (padded // 128, 128))
    out = exchange(flat, axis, n, gather, collective_id)
    return out.reshape(n, padded)[:, :size].reshape((n,) + block_shape)


def row_normalize(values, collective_id):
    width = values.shape[-1]
    local_mean = jnp.mean(values, axis=-1)
    centred = values - local_mean[..., None]
    local_m2 = jnp.sum(centred * centred, axis=-1)
    stats = jnp.stack([local_mean, local_m2], axis=0)
    stats = exchange_flat(stats, "req", lax.axis_size("req"), True, collective_id)
    stats = jnp.moveaxis(stats, 1, -1)
    means = stats[..., 0]
    row_mean = jnp.mean(means, axis=0)
    spread = means - row_mean
    row_m2 = jnp.sum(stats[..., 1], axis=0) + width * jnp.sum(spread * spread, axis=0)
    row_var = row_m2 / (width * stats.shape[0])
    return (values - row_mean[..., None]) * lax.rsqrt(row_var + EPSILON)[..., None]


def shards(
    inputs,
    norm_gains,
    attn_weight,
    up_weight,
    dense_weight,
    down_weight,
    next_weight,
    cache_keys,
    cache_values,
    lengths,
    slot_table,
    parents,
):
    scale = 1.0 / math.sqrt(HD)
    highest = lax.Precision.HIGHEST
    steps, local_rows, local_width = inputs.shape
    own_count = parents.shape[1]
    request_count = lengths.shape[0]
    beam_total = request_count * BEAM
    head_count = dense_weight.shape[0] // HD
    triple_width = attn_weight.shape[1]
    slot_count = slot_table.shape[1]
    req_size = beam_total // own_count
    mlp_size = beam_total // local_rows
    offset = lax.axis_index("req") * own_count
    beam_group = jnp.arange(beam_total, dtype=jnp.int32) // BEAM
    all_positions = lengths[beam_group][None, :] + jnp.arange(steps, dtype=jnp.int32)[:, None]
    own_group = jnp.arange(own_count, dtype=jnp.int32) // BEAM
    slot_owner = slot_table[0]
    slot_pageno = slot_table[1]
    valid_owner = jnp.maximum(slot_owner, 0)
    token_pos = slot_pageno[:, None] * PAGE + jnp.arange(PAGE, dtype=jnp.int32)[None, :]
    live = (slot_owner[:, None] >= 0) & (token_pos < lengths[valid_owner][:, None])
    live_wide = live[None, :, None, None, :]
    owner_mask = slot_owner[:, None] == jnp.arange(request_count, dtype=jnp.int32)[None, :]
    owner_float = owner_mask.astype(jnp.float32)
    gather_rows = valid_owner[:, None] * BEAM + jnp.arange(BEAM, dtype=jnp.int32)[None, :]

    block = inputs.astype(jnp.float32)
    rows_all = gather_grid(inputs, "mlp", mlp_size, 0).reshape(steps * beam_total, -1)
    normed = row_normalize(rows_all.astype(jnp.float32), 3)
    attn_in = (normed * norm_gains[0]).astype(jnp.bfloat16)
    mlp_in = (normed * norm_gains[1]).astype(jnp.bfloat16)
    grouped = (
        attn_weight.reshape(local_width, head_count, 3, HD)
        .transpose(0, 2, 1, 3)
        .reshape(local_width, triple_width)
    )
    first = jnp.dot(attn_in, grouped, preferred_element_type=jnp.float32)
    second = jnp.dot(mlp_in, up_weight, preferred_element_type=jnp.float32)
    partial_sums = jnp.concatenate([first, second], axis=1)
    summed_all = lax.psum(partial_sums.astype(jnp.bfloat16), "req")
    width = head_count * HD
    row = jnp.arange(steps * beam_total, dtype=jnp.int32)
    beam_lengths = jnp.broadcast_to(lengths[:, None], (request_count, BEAM)).reshape(
        mlp_size, 1, local_rows
    )
    row_positions = (
        beam_lengths + jnp.arange(steps, dtype=jnp.int32)[None, :, None]
    ).reshape(steps * beam_total)
    queries_rows = rotate_rows(
        summed_all[:, :width].astype(jnp.float32), row_positions, head_count
    ).astype(jnp.bfloat16)
    keys_rows = rotate_rows(
        summed_all[:, width : 2 * width].astype(jnp.float32), row_positions, head_count
    ).astype(jnp.bfloat16)
    per_own = own_count // local_rows
    own_start = lax.axis_index("req") * (per_own * steps * local_rows)

    def own_of(rows):
        return (
            lax.dynamic_slice_in_dim(rows, own_start, per_own * steps * local_rows, 0)
            .reshape(per_own, steps, local_rows, -1)
            .transpose(1, 0, 2, 3)
            .reshape(steps, own_count, head_count, HD)
        )

    queries_own = own_of(queries_rows)
    keys_new = own_of(keys_rows)
    values_new = own_of(summed_all[:, 2 * width : 3 * width])

    chosen_rows = (
        (gather_rows // local_rows) * (steps * local_rows)
        + jnp.arange(steps, dtype=jnp.int32)[:, None, None] * local_rows
        + gather_rows % local_rows
    )
    chosen = pick_rows(queries_rows, chosen_rows)
    head_scores = [
        jnp.einsum(
            "zsbd,std->zsbt",
            chosen[..., head * HD : (head + 1) * HD],
            cache_keys[:, :, head * HD : (head + 1) * HD],
            preferred_element_type=jnp.float32,
        )
        for head in range(head_count)
    ]
    scores = jnp.stack(head_scores, axis=3) * scale
    masked = jnp.where(live_wide, scores, NEG_FILL)
    slot_top = jnp.max(masked, axis=4)
    weights = jnp.where(live_wide, jnp.exp(masked - slot_top[..., None]), 0.0)
    slot_total = jnp.sum(weights, axis=4)
    rounded = weights.astype(jnp.bfloat16)
    slot_out = jnp.stack(
        [
            jnp.einsum(
                "zsbt,std->zsbd",
                rounded[:, :, :, head],
                cache_values[:, :, head * HD : (head + 1) * HD],
                preferred_element_type=jnp.float32,
            )
            for head in range(head_count)
        ],
        axis=3,
    )
    request_top = jnp.max(
        jnp.where(owner_mask[None, :, :, None, None], slot_top[:, :, None], NEG_FILL), axis=1
    )
    top_high = request_top.astype(jnp.bfloat16)
    top_low = (request_top - top_high.astype(jnp.float32)).astype(jnp.bfloat16)
    request_top = top_high.astype(jnp.float32) + top_low.astype(jnp.float32)
    factor = jnp.where(
        (slot_owner[None, :, None, None] >= 0) & (slot_top > 0.5 * NEG_FILL),
        jnp.exp(slot_top - request_top[:, valid_owner]),
        0.0,
    )
    page_total = jnp.einsum(
        "sr,zsbh->zrbh", owner_float, slot_total * factor, precision=highest
    ).reshape(steps, beam_total, head_count)
    page_out = jnp.einsum(
        "sr,zsbhd->zrbhd", owner_float, slot_out * factor[..., None], precision=highest
    ).reshape(steps, beam_total, head_count, HD)
    stats = jnp.concatenate(
        [
            page_total.astype(jnp.bfloat16),
            top_high.reshape(steps, beam_total, head_count),
            top_low.reshape(steps, beam_total, head_count),
        ],
        axis=-1,
    )
    packed = jnp.concatenate(
        [
            page_out.astype(jnp.bfloat16).reshape(steps, beam_total, head_count * HD),
            jnp.pad(stats, ((0, 0), (0, 0), (0, HD - 3 * head_count))),
        ],
        axis=-1,
    )
    packed = packed.reshape(steps, req_size, own_count, -1).transpose(1, 0, 2, 3)
    held, activated_all = exchange_gelu(packed, summed_all[:, triple_width:], "req", req_size, 5)
    held = held.astype(jnp.float32)
    base = head_count * HD
    held_top = held[..., base + head_count : base + 2 * head_count] + held[
        ..., base + 2 * head_count : base + 3 * head_count
    ]
    own_top = jnp.max(held_top, axis=0)
    rescale = jnp.exp(held_top - own_top)
    own_total = jnp.sum(held[..., base : base + head_count] * rescale, axis=0)
    own_out = jnp.stack(
        [
            jnp.sum(held[..., head * HD : (head + 1) * HD] * rescale[..., head : head + 1], axis=0)
            for head in range(head_count)
        ],
        axis=2,
    )

    source = own_group * BEAM + parents[0]
    attended_steps = []
    for step_index in range(steps):
        tail_keys = [pick_rows(keys_new[prior], source) for prior in range(step_index)]
        tail_values = [pick_rows(values_new[prior], source) for prior in range(step_index)]
        history_keys = jnp.stack(tail_keys + [keys_new[step_index]], axis=0)
        history_values = jnp.stack(tail_values + [values_new[step_index]], axis=0)
        own_scores = (
            jnp.einsum(
                "bhd,nbhd->bhn",
                queries_own[step_index],
                history_keys,
                preferred_element_type=jnp.float32,
            )
            * scale
        )
        top = jnp.maximum(own_top[step_index], jnp.max(own_scores, axis=2))
        page_factor = jnp.exp(own_top[step_index] - top)
        own_weights = jnp.exp(own_scores - top[..., None])
        total = own_total[step_index] * page_factor + jnp.sum(own_weights, axis=2)
        summed = own_out[step_index] * page_factor[..., None] + jnp.einsum(
            "bhn,nbhd->bhd",
            own_weights.astype(jnp.bfloat16),
            history_values,
            preferred_element_type=jnp.float32,
        )
        attended_steps.append(
            (summed / total[..., None]).astype(jnp.bfloat16).reshape(own_count, head_count * HD)
        )
    attended = jnp.stack(attended_steps)
    attended_all, down_part = gather_matmul(
        attended, activated_all, down_weight, "req", req_size, 6
    )
    attended_msi = (
        attended_all.reshape(req_size, steps, per_own, local_rows, -1)
        .transpose(0, 2, 1, 3, 4)
        .reshape(steps * beam_total, -1)
    )
    update_partial = (
        jnp.dot(attended_msi, dense_weight, preferred_element_type=jnp.float32) + down_part
    ).astype(jnp.bfloat16)
    update = jnp.sum(
        exchange(
            update_partial.reshape(mlp_size, steps * local_rows, local_width),
            "mlp",
            mlp_size,
            False,
            1,
        ).astype(jnp.float32),
        axis=0,
    )
    layer = (block + update.reshape(steps, local_rows, local_width)).astype(jnp.bfloat16)
    next_in = (row_normalize(layer.astype(jnp.float32), 4) * norm_gains[2]).astype(jnp.bfloat16)
    gathered = gather_grid(next_in, "mlp", mlp_size, 2).reshape(steps * beam_total, -1)
    next_partial = jnp.dot(gathered, next_weight, preferred_element_type=jnp.float32)
    next_out = lax.psum_scatter(
        next_partial.astype(jnp.bfloat16), "req", scatter_dimension=0, tiled=True
    )
    next_out = (
        next_out.reshape(per_own, steps, local_rows, -1)
        .transpose(1, 0, 2, 3)
        .reshape(steps, own_count, -1)
    )
    return (layer, next_out)


def solution(mesh):
    in_specs = (
        P(None, "mlp", "req"),
        P(None, "req"),
        P("req", "mlp"),
        P("req", "mlp"),
        P("mlp", "req"),
        P("mlp", "req"),
        P("req", "mlp"),
        P("req", None, "mlp"),
        P("req", None, "mlp"),
        P(),
        P(None, "req"),
        P(None, "req"),
    )
    out_specs = (P(None, "mlp", "req"), P(None, "req", "mlp"))
    return jax.shard_map(shards, mesh=mesh, in_specs=in_specs, out_specs=out_specs, check_vma=False)
```

```python
import functools
import math

import jax
import jax.numpy as jnp
from jax import lax
from jax.experimental import pallas as pl
from jax.experimental.pallas import tpu as pltpu
from jax.sharding import PartitionSpec as P

MESH = pl.DeviceIdType.MESH

HD = 128
ROT = 32
PAGE = 128
BEAM = 8
STEPS = 2


NEG_FILL = -1e30
EPSILON = 1e-05


def rotate(vectors, positions):
    half = ROT // 2
    freq = jnp.exp(jnp.arange(half, dtype=jnp.float32) * (-2.0 * math.log(10000.0) / ROT))
    angles = positions.astype(jnp.float32)[..., None] * freq
    cosine = jnp.concatenate([jnp.cos(angles), jnp.cos(angles)], axis=-1)[..., None, :]
    sine = jnp.concatenate([jnp.sin(angles), jnp.sin(angles)], axis=-1)[..., None, :]
    turned = vectors[..., :ROT]
    swapped = jnp.concatenate([-turned[..., half:], turned[..., :half]], axis=-1)
    return jnp.concatenate([turned * cosine + swapped * sine, vectors[..., ROT:]], axis=-1)


def pick_rows(table, index):
    flat = table.reshape(table.shape[0], -1)
    hot = (index.reshape(-1)[:, None] == jnp.arange(table.shape[0], dtype=jnp.int32)[None, :])
    taken = jnp.dot(hot.astype(table.dtype), flat, preferred_element_type=jnp.float32)
    return taken.astype(table.dtype).reshape(index.shape + table.shape[1:])


def rotate_rows(rows, positions, head_count):
    half = ROT // 2
    freq = jnp.exp(jnp.arange(half, dtype=jnp.float32) * (-2.0 * math.log(10000.0) / ROT))
    angles = positions.astype(jnp.float32)[:, None] * freq[None, :]
    cosine = jnp.concatenate([jnp.cos(angles), jnp.cos(angles)], axis=1)
    sine = jnp.concatenate([jnp.sin(angles), jnp.sin(angles)], axis=1)
    parts = []
    for head in range(head_count):
        base = head * HD
        turned = rows[:, base : base + ROT]
        swapped = jnp.concatenate([-turned[:, half:], turned[:, :half]], axis=1)
        parts += [turned * cosine + swapped * sine, rows[:, base + ROT : base + HD]]
    return jnp.concatenate(parts, axis=1)


def exchange_kernel(axis, n, gather, x_ref, out_ref, send_sem, recv_sem, local_sem):
    me = lax.axis_index(axis)
    barrier = pltpu.get_barrier_semaphore()
    for k in range(1, n):
        pl.semaphore_signal(
            barrier, inc=1, device_id={axis: lax.rem(me + k, n)}, device_id_type=MESH
        )
    pl.semaphore_wait(barrier, n - 1)
    local = pltpu.make_async_copy(x_ref if gather else x_ref.at[me], out_ref.at[me], local_sem)
    local.start()
    copies = []
    for k in range(1, n):
        dest = lax.rem(me + k, n)
        copy = pltpu.make_async_remote_copy(
            src_ref=x_ref if gather else x_ref.at[dest],
            dst_ref=out_ref.at[me],
            send_sem=send_sem.at[k],
            recv_sem=recv_sem.at[k],
            device_id={axis: dest},
            device_id_type=MESH,
        )
        copy.start()
        copies.append(copy)
    for copy in copies:
        copy.wait()
    local.wait()


def exchange_gelu_kernel(axis, n, x_ref, hidden_ref, out_ref, act_ref, send_sem, recv_sem, local_sem):
    me = lax.axis_index(axis)
    barrier = pltpu.get_barrier_semaphore()
    for k in range(1, n):
        pl.semaphore_signal(
            barrier, inc=1, device_id={axis: lax.rem(me + k, n)}, device_id_type=MESH
        )
    pl.semaphore_wait(barrier, n - 1)
    local = pltpu.make_async_copy(x_ref.at[me], out_ref.at[me], local_sem)
    local.start()
    copies = []
    for k in range(1, n):
        dest = lax.rem(me + k, n)
        copy = pltpu.make_async_remote_copy(
            src_ref=x_ref.at[dest],
            dst_ref=out_ref.at[me],
            send_sem=send_sem.at[k],
            recv_sem=recv_sem.at[k],
            device_id={axis: dest},
            device_id_type=MESH,
        )
        copy.start()
        copies.append(copy)
    tile = 128

    @pl.loop(0, hidden_ref.shape[0] // tile)
    def _(index):
        rows = pl.ds(pl.multiple_of(index * tile, tile), tile)
        values = hidden_ref[rows, :].astype(jnp.float32)
        gelu = 0.5 * values * (1.0 + lax.erf(values * (1.0 / math.sqrt(2.0))))
        act_ref[rows, :] = gelu.astype(act_ref.dtype)

    for copy in copies:
        copy.wait()
    local.wait()


def exchange_gelu(x, hidden, axis, n, collective_id):
    return pl.pallas_call(
        functools.partial(exchange_gelu_kernel, axis, n),
        out_shape=(
            jax.ShapeDtypeStruct(x.shape, x.dtype),
            jax.ShapeDtypeStruct(hidden.shape, jnp.bfloat16),
        ),
        in_specs=[pl.BlockSpec(memory_space=pltpu.VMEM)] * 2,
        out_specs=(pl.BlockSpec(memory_space=pltpu.VMEM),) * 2,
        scratch_shapes=[
            pltpu.SemaphoreType.DMA((n,)),
            pltpu.SemaphoreType.DMA((n,)),
            pltpu.SemaphoreType.DMA(()),
        ],
        compiler_params=pltpu.CompilerParams(
            collective_id=collective_id, has_side_effects=True
        ),
        cost_estimate=pl.CostEstimate(
            flops=20 * hidden.size,
            transcendentals=hidden.size,
            bytes_accessed=2 * n * x.size * x.dtype.itemsize + 4 * hidden.size,
        ),
    )(x, hidden)


def gather_grid_kernel(axis, side, x_ref, out_ref, send_sem, recv_sem, local_sem):
    me = lax.axis_index(axis)
    row, col = me // side, me % side
    row_peers = [row * side + lax.rem(col + k, side) for k in range(1, side)]
    col_peers = [lax.rem(row + k, side) * side + col for k in range(1, side)]
    barrier = pltpu.get_barrier_semaphore()
    for peer in row_peers + col_peers:
        pl.semaphore_signal(barrier, inc=1, device_id={axis: peer}, device_id_type=MESH)
    pl.semaphore_wait(barrier, 2 * (side - 1))
    local = pltpu.make_async_copy(x_ref, out_ref.at[me], local_sem)
    local.start()
    first = []
    for k, peer in enumerate(row_peers):
        copy = pltpu.make_async_remote_copy(
            src_ref=x_ref,
            dst_ref=out_ref.at[me],
            send_sem=send_sem.at[0, k],
            recv_sem=recv_sem.at[0, k],
            device_id={axis: peer},
            device_id_type=MESH,
        )
        copy.start()
        first.append(copy)
    for copy in first:
        copy.wait()
    local.wait()
    slab = out_ref.at[pl.ds(row * side, side)]
    second = []
    for k, peer in enumerate(col_peers):
        copy = pltpu.make_async_remote_copy(
            src_ref=slab,
            dst_ref=slab,
            send_sem=send_sem.at[1, k],
            recv_sem=recv_sem.at[1, k],
            device_id={axis: peer},
            device_id_type=MESH,
        )
        copy.start()
        second.append(copy)
    for copy in second:
        copy.wait()


def gather_grid(x, axis, n, collective_id):
    side = math.isqrt(n)
    return pl.pallas_call(
        functools.partial(gather_grid_kernel, axis, side),
        out_shape=jax.ShapeDtypeStruct((n,) + x.shape, x.dtype),
        in_specs=[pl.BlockSpec(memory_space=pltpu.VMEM)],
        out_specs=pl.BlockSpec(memory_space=pltpu.VMEM),
        scratch_shapes=[
            pltpu.SemaphoreType.DMA((2, side - 1)),
            pltpu.SemaphoreType.DMA((2, side - 1)),
            pltpu.SemaphoreType.DMA(()),
        ],
        compiler_params=pltpu.CompilerParams(
            collective_id=collective_id, has_side_effects=True
        ),
        cost_estimate=pl.CostEstimate(
            flops=0, transcendentals=0, bytes_accessed=2 * n * x.size * x.dtype.itemsize
        ),
    )(x)


def exchange(x, axis, n, gather, collective_id):
    shape = (n,) + (x.shape if gather else x.shape[1:])
    return pl.pallas_call(
        functools.partial(exchange_kernel, axis, n, gather),
        out_shape=jax.ShapeDtypeStruct(shape, x.dtype),
        in_specs=[pl.BlockSpec(memory_space=pltpu.VMEM)],
        out_specs=pl.BlockSpec(memory_space=pltpu.VMEM),
        scratch_shapes=[
            pltpu.SemaphoreType.DMA((n,)),
            pltpu.SemaphoreType.DMA((n,)),
            pltpu.SemaphoreType.DMA(()),
        ],
        compiler_params=pltpu.CompilerParams(
            collective_id=collective_id, has_side_effects=True
        ),
        cost_estimate=pl.CostEstimate(
            flops=0, transcendentals=0, bytes_accessed=2 * n * x.size * x.dtype.itemsize
        ),
    )(x)


def exchange_flat(x, axis, n, gather, collective_id):
    lead = () if gather else x.shape[:1]
    block_shape = x.shape if gather else x.shape[1:]
    size = math.prod(block_shape)
    padded = -(-size // 128) * 128
    flat = x.reshape(lead + (size,))
    flat = jnp.pad(flat, [(0, 0)] * len(lead) + [(0, padded - size)])
    flat = flat.reshape(lead + (padded // 128, 128))
    out = exchange(flat, axis, n, gather, collective_id)
    return out.reshape(n, padded)[:, :size].reshape((n,) + block_shape)


def row_normalize(values, collective_id):
    width = values.shape[-1]
    local_mean = jnp.mean(values, axis=-1)
    centred = values - local_mean[..., None]
    local_m2 = jnp.sum(centred * centred, axis=-1)
    stats = jnp.stack([local_mean, local_m2], axis=0)
    stats = exchange_flat(stats, "req", lax.axis_size("req"), True, collective_id)
    stats = jnp.moveaxis(stats, 1, -1)
    means = stats[..., 0]
    row_mean = jnp.mean(means, axis=0)
    spread = means - row_mean
    row_m2 = jnp.sum(stats[..., 1], axis=0) + width * jnp.sum(spread * spread, axis=0)
    row_var = row_m2 / (width * stats.shape[0])
    return (values - row_mean[..., None]) * lax.rsqrt(row_var + EPSILON)[..., None]


def shards(
    inputs,
    norm_gains,
    attn_weight,
    up_weight,
    dense_weight,
    down_weight,
    next_weight,
    cache_keys,
    cache_values,
    lengths,
    slot_table,
    parents,
):
    scale = 1.0 / math.sqrt(HD)
    highest = lax.Precision.HIGHEST
    steps, local_rows, local_width = inputs.shape
    own_count = parents.shape[1]
    request_count = lengths.shape[0]
    beam_total = request_count * BEAM
    head_count = dense_weight.shape[0] // HD
    triple_width = attn_weight.shape[1]
    slot_count = slot_table.shape[1]
    req_size = beam_total // own_count
    mlp_size = beam_total // local_rows
    offset = lax.axis_index("req") * own_count
    beam_group = jnp.arange(beam_total, dtype=jnp.int32) // BEAM
    all_positions = lengths[beam_group][None, :] + jnp.arange(steps, dtype=jnp.int32)[:, None]
    own_group = jnp.arange(own_count, dtype=jnp.int32) // BEAM
    slot_owner = slot_table[0]
    slot_pageno = slot_table[1]
    valid_owner = jnp.maximum(slot_owner, 0)
    token_pos = slot_pageno[:, None] * PAGE + jnp.arange(PAGE, dtype=jnp.int32)[None, :]
    live = (slot_owner[:, None] >= 0) & (token_pos < lengths[valid_owner][:, None])
    live_wide = live[None, :, None, None, :]
    owner_mask = slot_owner[:, None] == jnp.arange(request_count, dtype=jnp.int32)[None, :]
    owner_float = owner_mask.astype(jnp.float32)
    gather_rows = valid_owner[:, None] * BEAM + jnp.arange(BEAM, dtype=jnp.int32)[None, :]

    block = inputs.astype(jnp.float32)
    rows_all = gather_grid(inputs, "mlp", mlp_size, 0).reshape(steps * beam_total, -1)
    normed = row_normalize(rows_all.astype(jnp.float32), 3)
    attn_in = (normed * norm_gains[0]).astype(jnp.bfloat16)
    mlp_in = (normed * norm_gains[1]).astype(jnp.bfloat16)
    grouped = (
        attn_weight.reshape(local_width, head_count, 3, HD)
        .transpose(0, 2, 1, 3)
        .reshape(local_width, triple_width)
    )
    first = jnp.dot(attn_in, grouped, preferred_element_type=jnp.float32)
    second = jnp.dot(mlp_in, up_weight, preferred_element_type=jnp.float32)
    partial_sums = jnp.concatenate([first, second], axis=1)
    summed_all = lax.psum(partial_sums.astype(jnp.bfloat16), "req")
    width = head_count * HD
    row = jnp.arange(steps * beam_total, dtype=jnp.int32)
    beam_lengths = jnp.broadcast_to(lengths[:, None], (request_count, BEAM)).reshape(
        mlp_size, 1, local_rows
    )
    row_positions = (
        beam_lengths + jnp.arange(steps, dtype=jnp.int32)[None, :, None]
    ).reshape(steps * beam_total)
    queries_rows = rotate_rows(
        summed_all[:, :width].astype(jnp.float32), row_positions, head_count
    ).astype(jnp.bfloat16)
    keys_rows = rotate_rows(
        summed_all[:, width : 2 * width].astype(jnp.float32), row_positions, head_count
    ).astype(jnp.bfloat16)
    per_own = own_count // local_rows
    own_start = lax.axis_index("req") * (per_own * steps * local_rows)

    def own_of(rows):
        return (
            lax.dynamic_slice_in_dim(rows, own_start, per_own * steps * local_rows, 0)
            .reshape(per_own, steps, local_rows, -1)
            .transpose(1, 0, 2, 3)
            .reshape(steps, own_count, head_count, HD)
        )

    queries_own = own_of(queries_rows)
    keys_new = own_of(keys_rows)
    values_new = own_of(summed_all[:, 2 * width : 3 * width])

    chosen_rows = (
        (gather_rows // local_rows) * (steps * local_rows)
        + jnp.arange(steps, dtype=jnp.int32)[:, None, None] * local_rows
        + gather_rows % local_rows
    )
    chosen = pick_rows(queries_rows, chosen_rows)
    head_scores = [
        jnp.einsum(
            "zsbd,std->zsbt",
            chosen[..., head * HD : (head + 1) * HD],
            cache_keys[:, :, head * HD : (head + 1) * HD],
            preferred_element_type=jnp.float32,
        )
        for head in range(head_count)
    ]
    scores = jnp.stack(head_scores, axis=3) * scale
    masked = jnp.where(live_wide, scores, NEG_FILL)
    slot_top = jnp.max(masked, axis=4)
    weights = jnp.where(live_wide, jnp.exp(masked - slot_top[..., None]), 0.0)
    slot_total = jnp.sum(weights, axis=4)
    rounded = weights.astype(jnp.bfloat16)
    slot_out = jnp.stack(
        [
            jnp.einsum(
                "zsbt,std->zsbd",
                rounded[:, :, :, head],
                cache_values[:, :, head * HD : (head + 1) * HD],
                preferred_element_type=jnp.float32,
            )
            for head in range(head_count)
        ],
        axis=3,
    )
    request_top = jnp.max(
        jnp.where(owner_mask[None, :, :, None, None], slot_top[:, :, None], NEG_FILL), axis=1
    )
    top_high = request_top.astype(jnp.bfloat16)
    top_low = (request_top - top_high.astype(jnp.float32)).astype(jnp.bfloat16)
    request_top = top_high.astype(jnp.float32) + top_low.astype(jnp.float32)
    factor = jnp.where(
        (slot_owner[None, :, None, None] >= 0) & (slot_top > 0.5 * NEG_FILL),
        jnp.exp(slot_top - request_top[:, valid_owner]),
        0.0,
    )
    page_total = jnp.einsum(
        "sr,zsbh->zrbh", owner_float, slot_total * factor, precision=highest
    ).reshape(steps, beam_total, head_count)
    page_out = jnp.einsum(
        "sr,zsbhd->zrbhd", owner_float, slot_out * factor[..., None], precision=highest
    ).reshape(steps, beam_total, head_count, HD)
    stats = jnp.concatenate(
        [
            page_total.astype(jnp.bfloat16),
            top_high.reshape(steps, beam_total, head_count),
            top_low.reshape(steps, beam_total, head_count),
        ],
        axis=-1,
    )
    packed = jnp.concatenate(
        [
            page_out.astype(jnp.bfloat16).reshape(steps, beam_total, head_count * HD),
            jnp.pad(stats, ((0, 0), (0, 0), (0, HD - 3 * head_count))),
        ],
        axis=-1,
    )
    packed = packed.reshape(steps, req_size, own_count, -1).transpose(1, 0, 2, 3)
    held, activated_all = exchange_gelu(packed, summed_all[:, triple_width:], "req", req_size, 5)
    held = held.astype(jnp.float32)
    base = head_count * HD
    held_top = held[..., base + head_count : base + 2 * head_count] + held[
        ..., base + 2 * head_count : base + 3 * head_count
    ]
    own_top = jnp.max(held_top, axis=0)
    rescale = jnp.exp(held_top - own_top)
    own_total = jnp.sum(held[..., base : base + head_count] * rescale, axis=0)
    own_out = jnp.stack(
        [
            jnp.sum(held[..., head * HD : (head + 1) * HD] * rescale[..., head : head + 1], axis=0)
            for head in range(head_count)
        ],
        axis=2,
    )

    source = own_group * BEAM + parents[0]
    def history(table):
        empty = jnp.zeros_like(table[0])
        return jnp.stack(
            [
                jnp.stack(
                    [
                        pick_rows(table[n], source) if n < s else table[s] if n == s else empty
                        for n in range(steps)
                    ]
                )
                for s in range(steps)
            ]
        )

    filled = (
        jnp.arange(steps, dtype=jnp.int32)[None, :] <= jnp.arange(steps, dtype=jnp.int32)[:, None]
    )[:, None, None, :]
    own_scores = (
        jnp.einsum(
            "zbhd,znbhd->zbhn", queries_own, history(keys_new), preferred_element_type=jnp.float32
        )
        * scale
    )
    own_scores = jnp.where(filled, own_scores, NEG_FILL)
    top = jnp.maximum(own_top, jnp.max(own_scores, axis=3))
    page_factor = jnp.exp(own_top - top)
    own_weights = jnp.where(filled, jnp.exp(own_scores - top[..., None]), 0.0)
    total = own_total * page_factor + jnp.sum(own_weights, axis=3)
    summed = own_out * page_factor[..., None] + jnp.einsum(
        "zbhn,znbhd->zbhd",
        own_weights.astype(jnp.bfloat16),
        history(values_new),
        preferred_element_type=jnp.float32,
    )
    attended = (summed / total[..., None]).astype(jnp.bfloat16).reshape(
        steps, own_count, head_count * HD
    )
    attended_all = exchange(attended, "req", req_size, True, 6)
    attended_msi = (
        attended_all.reshape(req_size, steps, per_own, local_rows, -1)
        .transpose(0, 2, 1, 3, 4)
        .reshape(steps * beam_total, -1)
    )
    update_partial = (
        jnp.dot(attended_msi, dense_weight, preferred_element_type=jnp.float32)
        + jnp.dot(activated_all, down_weight, preferred_element_type=jnp.float32)
    ).astype(jnp.bfloat16)
    update = jnp.sum(
        exchange(
            update_partial.reshape(mlp_size, steps * local_rows, local_width),
            "mlp",
            mlp_size,
            False,
            1,
        ).astype(jnp.float32),
        axis=0,
    )
    layer = (block + update.reshape(steps, local_rows, local_width)).astype(jnp.bfloat16)
    next_in = (row_normalize(layer.astype(jnp.float32), 4) * norm_gains[2]).astype(jnp.bfloat16)
    gathered = gather_grid(next_in, "mlp", mlp_size, 2).reshape(steps * beam_total, -1)
    next_partial = jnp.dot(gathered, next_weight, preferred_element_type=jnp.float32)
    next_out = lax.psum_scatter(
        next_partial.astype(jnp.bfloat16), "req", scatter_dimension=0, tiled=True
    )
    next_out = (
        next_out.reshape(per_own, steps, local_rows, -1)
        .transpose(1, 0, 2, 3)
        .reshape(steps, own_count, -1)
    )
    return (layer, next_out)


def solution(mesh):
    in_specs = (
        P(None, "mlp", "req"),
        P(None, "req"),
        P("req", "mlp"),
        P("req", "mlp"),
        P("mlp", "req"),
        P("mlp", "req"),
        P("req", "mlp"),
        P("req", None, "mlp"),
        P("req", None, "mlp"),
        P(),
        P(None, "req"),
        P(None, "req"),
    )
    out_specs = (P(None, "mlp", "req"), P(None, "req", "mlp"))
    return jax.shard_map(shards, mesh=mesh, in_specs=in_specs, out_specs=out_specs, check_vma=False)
```

```python
import functools
import math

import jax
import jax.numpy as jnp
from jax import lax
from jax.experimental import pallas as pl
from jax.experimental.pallas import tpu as pltpu
from jax.sharding import PartitionSpec as P

MESH = pl.DeviceIdType.MESH

HD = 128
ROT = 32
PAGE = 128
BEAM = 8
STEPS = 2


NEG_FILL = -1e30
EPSILON = 1e-05


def rotate(vectors, positions):
    half = ROT // 2
    freq = jnp.exp(jnp.arange(half, dtype=jnp.float32) * (-2.0 * math.log(10000.0) / ROT))
    angles = positions.astype(jnp.float32)[..., None] * freq
    cosine = jnp.concatenate([jnp.cos(angles), jnp.cos(angles)], axis=-1)[..., None, :]
    sine = jnp.concatenate([jnp.sin(angles), jnp.sin(angles)], axis=-1)[..., None, :]
    turned = vectors[..., :ROT]
    swapped = jnp.concatenate([-turned[..., half:], turned[..., :half]], axis=-1)
    return jnp.concatenate([turned * cosine + swapped * sine, vectors[..., ROT:]], axis=-1)


def pick_rows(table, index):
    flat = table.reshape(table.shape[0], -1)
    hot = (index.reshape(-1)[:, None] == jnp.arange(table.shape[0], dtype=jnp.int32)[None, :])
    taken = jnp.dot(hot.astype(table.dtype), flat, preferred_element_type=jnp.float32)
    return taken.astype(table.dtype).reshape(index.shape + table.shape[1:])


def rotate_rows(rows, positions, head_count):
    half = ROT // 2
    freq = jnp.exp(jnp.arange(half, dtype=jnp.float32) * (-2.0 * math.log(10000.0) / ROT))
    angles = positions.astype(jnp.float32)[:, None] * freq[None, :]
    cosine = jnp.concatenate([jnp.cos(angles), jnp.cos(angles)], axis=1)
    sine = jnp.concatenate([jnp.sin(angles), jnp.sin(angles)], axis=1)
    parts = []
    for head in range(head_count):
        base = head * HD
        turned = rows[:, base : base + ROT]
        swapped = jnp.concatenate([-turned[:, half:], turned[:, :half]], axis=1)
        parts += [turned * cosine + swapped * sine, rows[:, base + ROT : base + HD]]
    return jnp.concatenate(parts, axis=1)


def exchange_kernel(axis, n, gather, x_ref, out_ref, send_sem, recv_sem, local_sem):
    me = lax.axis_index(axis)
    barrier = pltpu.get_barrier_semaphore()
    for k in range(1, n):
        pl.semaphore_signal(
            barrier, inc=1, device_id={axis: lax.rem(me + k, n)}, device_id_type=MESH
        )
    pl.semaphore_wait(barrier, n - 1)
    local = pltpu.make_async_copy(x_ref if gather else x_ref.at[me], out_ref.at[me], local_sem)
    local.start()
    copies = []
    for k in range(1, n):
        dest = lax.rem(me + k, n)
        copy = pltpu.make_async_remote_copy(
            src_ref=x_ref if gather else x_ref.at[dest],
            dst_ref=out_ref.at[me],
            send_sem=send_sem.at[k],
            recv_sem=recv_sem.at[k],
            device_id={axis: dest},
            device_id_type=MESH,
        )
        copy.start()
        copies.append(copy)
    for copy in copies:
        copy.wait()
    local.wait()


def exchange_gelu_kernel(axis, n, start, x_ref, hidden_ref, out_ref, act_ref, send_sem, recv_sem, local_sem):
    me = lax.axis_index(axis)
    barrier = pltpu.get_barrier_semaphore()
    for k in range(1, n):
        pl.semaphore_signal(
            barrier, inc=1, device_id={axis: lax.rem(me + k, n)}, device_id_type=MESH
        )
    pl.semaphore_wait(barrier, n - 1)
    local = pltpu.make_async_copy(x_ref.at[me], out_ref.at[me], local_sem)
    local.start()
    copies = []
    for k in range(1, n):
        dest = lax.rem(me + k, n)
        copy = pltpu.make_async_remote_copy(
            src_ref=x_ref.at[dest],
            dst_ref=out_ref.at[me],
            send_sem=send_sem.at[k],
            recv_sem=recv_sem.at[k],
            device_id={axis: dest},
            device_id_type=MESH,
        )
        copy.start()
        copies.append(copy)
    tile = 128

    @pl.loop(0, hidden_ref.shape[0] // tile)
    def _(index):
        rows = pl.ds(pl.multiple_of(index * tile, tile), tile)
        values = hidden_ref[rows, start : start + act_ref.shape[1]].astype(jnp.float32)
        gelu = 0.5 * values * (1.0 + lax.erf(values * (1.0 / math.sqrt(2.0))))
        act_ref[rows, :] = gelu.astype(act_ref.dtype)

    for copy in copies:
        copy.wait()
    local.wait()


def exchange_gelu(x, summed, start, axis, n, collective_id):
    hidden = jax.ShapeDtypeStruct((summed.shape[0], summed.shape[1] - start), jnp.bfloat16)
    return pl.pallas_call(
        functools.partial(exchange_gelu_kernel, axis, n, start),
        out_shape=(
            jax.ShapeDtypeStruct(x.shape, x.dtype),
            hidden,
        ),
        in_specs=[pl.BlockSpec(memory_space=pltpu.VMEM)] * 2,
        out_specs=(pl.BlockSpec(memory_space=pltpu.VMEM),) * 2,
        scratch_shapes=[
            pltpu.SemaphoreType.DMA((n,)),
            pltpu.SemaphoreType.DMA((n,)),
            pltpu.SemaphoreType.DMA(()),
        ],
        compiler_params=pltpu.CompilerParams(
            collective_id=collective_id, has_side_effects=True
        ),
        cost_estimate=pl.CostEstimate(
            flops=20 * hidden.size,
            transcendentals=hidden.size,
            bytes_accessed=2 * n * x.size * x.dtype.itemsize + 4 * hidden.size,
        ),
    )(x, summed)


def gather_grid_kernel(axis, side, x_ref, out_ref, send_sem, recv_sem, local_sem):
    me = lax.axis_index(axis)
    row, col = me // side, me % side
    row_peers = [row * side + lax.rem(col + k, side) for k in range(1, side)]
    col_peers = [lax.rem(row + k, side) * side + col for k in range(1, side)]
    barrier = pltpu.get_barrier_semaphore()
    for peer in row_peers + col_peers:
        pl.semaphore_signal(barrier, inc=1, device_id={axis: peer}, device_id_type=MESH)
    pl.semaphore_wait(barrier, 2 * (side - 1))
    local = pltpu.make_async_copy(x_ref, out_ref.at[me], local_sem)
    local.start()
    first = []
    for k, peer in enumerate(row_peers):
        copy = pltpu.make_async_remote_copy(
            src_ref=x_ref,
            dst_ref=out_ref.at[me],
            send_sem=send_sem.at[0, k],
            recv_sem=recv_sem.at[0, k],
            device_id={axis: peer},
            device_id_type=MESH,
        )
        copy.start()
        first.append(copy)
    for copy in first:
        copy.wait()
    local.wait()
    slab = out_ref.at[pl.ds(row * side, side)]
    second = []
    for k, peer in enumerate(col_peers):
        copy = pltpu.make_async_remote_copy(
            src_ref=slab,
            dst_ref=slab,
            send_sem=send_sem.at[1, k],
            recv_sem=recv_sem.at[1, k],
            device_id={axis: peer},
            device_id_type=MESH,
        )
        copy.start()
        second.append(copy)
    for copy in second:
        copy.wait()


def gather_grid(x, axis, n, collective_id):
    side = math.isqrt(n)
    return pl.pallas_call(
        functools.partial(gather_grid_kernel, axis, side),
        out_shape=jax.ShapeDtypeStruct((n,) + x.shape, x.dtype),
        in_specs=[pl.BlockSpec(memory_space=pltpu.VMEM)],
        out_specs=pl.BlockSpec(memory_space=pltpu.VMEM),
        scratch_shapes=[
            pltpu.SemaphoreType.DMA((2, side - 1)),
            pltpu.SemaphoreType.DMA((2, side - 1)),
            pltpu.SemaphoreType.DMA(()),
        ],
        compiler_params=pltpu.CompilerParams(
            collective_id=collective_id, has_side_effects=True
        ),
        cost_estimate=pl.CostEstimate(
            flops=0, transcendentals=0, bytes_accessed=2 * n * x.size * x.dtype.itemsize
        ),
    )(x)


def exchange(x, axis, n, gather, collective_id):
    shape = (n,) + (x.shape if gather else x.shape[1:])
    return pl.pallas_call(
        functools.partial(exchange_kernel, axis, n, gather),
        out_shape=jax.ShapeDtypeStruct(shape, x.dtype),
        in_specs=[pl.BlockSpec(memory_space=pltpu.VMEM)],
        out_specs=pl.BlockSpec(memory_space=pltpu.VMEM),
        scratch_shapes=[
            pltpu.SemaphoreType.DMA((n,)),
            pltpu.SemaphoreType.DMA((n,)),
            pltpu.SemaphoreType.DMA(()),
        ],
        compiler_params=pltpu.CompilerParams(
            collective_id=collective_id, has_side_effects=True
        ),
        cost_estimate=pl.CostEstimate(
            flops=0, transcendentals=0, bytes_accessed=2 * n * x.size * x.dtype.itemsize
        ),
    )(x)


def exchange_flat(x, axis, n, gather, collective_id):
    lead = () if gather else x.shape[:1]
    block_shape = x.shape if gather else x.shape[1:]
    size = math.prod(block_shape)
    padded = -(-size // 128) * 128
    flat = x.reshape(lead + (size,))
    flat = jnp.pad(flat, [(0, 0)] * len(lead) + [(0, padded - size)])
    flat = flat.reshape(lead + (padded // 128, 128))
    out = exchange(flat, axis, n, gather, collective_id)
    return out.reshape(n, padded)[:, :size].reshape((n,) + block_shape)


def row_normalize(values, collective_id):
    width = values.shape[-1]
    local_mean = jnp.mean(values, axis=-1)
    centred = values - local_mean[..., None]
    local_m2 = jnp.sum(centred * centred, axis=-1)
    stats = jnp.stack([local_mean, local_m2], axis=0)
    stats = exchange_flat(stats, "req", lax.axis_size("req"), True, collective_id)
    stats = jnp.moveaxis(stats, 1, -1)
    means = stats[..., 0]
    row_mean = jnp.mean(means, axis=0)
    spread = means - row_mean
    row_m2 = jnp.sum(stats[..., 1], axis=0) + width * jnp.sum(spread * spread, axis=0)
    row_var = row_m2 / (width * stats.shape[0])
    return (values - row_mean[..., None]) * lax.rsqrt(row_var + EPSILON)[..., None]


def shards(
    inputs,
    norm_gains,
    attn_weight,
    up_weight,
    dense_weight,
    down_weight,
    next_weight,
    cache_keys,
    cache_values,
    lengths,
    slot_table,
    parents,
):
    scale = 1.0 / math.sqrt(HD)
    highest = lax.Precision.HIGHEST
    steps, local_rows, local_width = inputs.shape
    own_count = parents.shape[1]
    request_count = lengths.shape[0]
    beam_total = request_count * BEAM
    head_count = dense_weight.shape[0] // HD
    triple_width = attn_weight.shape[1]
    slot_count = slot_table.shape[1]
    req_size = beam_total // own_count
    mlp_size = beam_total // local_rows
    offset = lax.axis_index("req") * own_count
    beam_group = jnp.arange(beam_total, dtype=jnp.int32) // BEAM
    all_positions = lengths[beam_group][None, :] + jnp.arange(steps, dtype=jnp.int32)[:, None]
    own_group = jnp.arange(own_count, dtype=jnp.int32) // BEAM
    slot_owner = slot_table[0]
    slot_pageno = slot_table[1]
    valid_owner = jnp.maximum(slot_owner, 0)
    token_pos = slot_pageno[:, None] * PAGE + jnp.arange(PAGE, dtype=jnp.int32)[None, :]
    live = (slot_owner[:, None] >= 0) & (token_pos < lengths[valid_owner][:, None])
    live_wide = live[None, :, None, None, :]
    owner_mask = slot_owner[:, None] == jnp.arange(request_count, dtype=jnp.int32)[None, :]
    owner_float = owner_mask.astype(jnp.float32)
    gather_rows = valid_owner[:, None] * BEAM + jnp.arange(BEAM, dtype=jnp.int32)[None, :]

    block = inputs.astype(jnp.float32)
    rows_all = gather_grid(inputs, "mlp", mlp_size, 0).reshape(steps * beam_total, -1)
    normed = row_normalize(rows_all.astype(jnp.float32), 3)
    attn_in = (normed * norm_gains[0]).astype(jnp.bfloat16)
    mlp_in = (normed * norm_gains[1]).astype(jnp.bfloat16)
    grouped = (
        attn_weight.reshape(local_width, head_count, 3, HD)
        .transpose(0, 2, 1, 3)
        .reshape(local_width, triple_width)
    )
    first = jnp.dot(attn_in, grouped, preferred_element_type=jnp.float32)
    second = jnp.dot(mlp_in, up_weight, preferred_element_type=jnp.float32)
    partial_sums = jnp.concatenate([first, second], axis=1)
    summed_all = lax.psum(partial_sums.astype(jnp.bfloat16), "req")
    width = head_count * HD
    row = jnp.arange(steps * beam_total, dtype=jnp.int32)
    beam_lengths = jnp.broadcast_to(lengths[:, None], (request_count, BEAM)).reshape(
        mlp_size, 1, local_rows
    )
    row_positions = (
        beam_lengths + jnp.arange(steps, dtype=jnp.int32)[None, :, None]
    ).reshape(steps * beam_total)
    queries_rows = rotate_rows(
        summed_all[:, :width].astype(jnp.float32), row_positions, head_count
    ).astype(jnp.bfloat16)
    per_own = own_count // local_rows
    own_start = lax.axis_index("req") * (per_own * steps * local_rows)

    def own_rows(rows):
        return lax.dynamic_slice_in_dim(rows, own_start, per_own * steps * local_rows, 0)

    def by_step(rows):
        return (
            rows.reshape(per_own, steps, local_rows, -1)
            .transpose(1, 0, 2, 3)
            .reshape(steps, own_count, head_count, HD)
        )

    queries_own = by_step(own_rows(queries_rows))
    keys_new = by_step(
        rotate_rows(
            own_rows(summed_all[:, width : 2 * width].astype(jnp.float32)),
            own_rows(row_positions),
            head_count,
        ).astype(jnp.bfloat16)
    )
    values_new = by_step(own_rows(summed_all[:, 2 * width : 3 * width]))

    chosen_rows = (
        (gather_rows // local_rows) * (steps * local_rows)
        + jnp.arange(steps, dtype=jnp.int32)[:, None, None] * local_rows
        + gather_rows % local_rows
    )
    chosen = pick_rows(queries_rows, chosen_rows)
    head_scores = [
        jnp.einsum(
            "zsbd,std->zsbt",
            chosen[..., head * HD : (head + 1) * HD],
            cache_keys[:, :, head * HD : (head + 1) * HD],
            preferred_element_type=jnp.float32,
        )
        for head in range(head_count)
    ]
    scores = jnp.stack(head_scores, axis=3) * scale
    masked = jnp.where(live_wide, scores, NEG_FILL)
    slot_top = jnp.max(masked, axis=4)
    weights = jnp.where(live_wide, jnp.exp(masked - slot_top[..., None]), 0.0)
    slot_total = jnp.sum(weights, axis=4)
    rounded = weights.astype(jnp.bfloat16)
    slot_out = jnp.stack(
        [
            jnp.einsum(
                "zsbt,std->zsbd",
                rounded[:, :, :, head],
                cache_values[:, :, head * HD : (head + 1) * HD],
                preferred_element_type=jnp.float32,
            )
            for head in range(head_count)
        ],
        axis=3,
    )
    request_top = jnp.max(
        jnp.where(owner_mask[None, :, :, None, None], slot_top[:, :, None], NEG_FILL), axis=1
    )
    top_high = request_top.astype(jnp.bfloat16)
    top_low = (request_top - top_high.astype(jnp.float32)).astype(jnp.bfloat16)
    request_top = top_high.astype(jnp.float32) + top_low.astype(jnp.float32)
    factor = jnp.where(
        (slot_owner[None, :, None, None] >= 0) & (slot_top > 0.5 * NEG_FILL),
        jnp.exp(slot_top - request_top[:, valid_owner]),
        0.0,
    )
    page_total = jnp.einsum(
        "sr,zsbh->zrbh", owner_float, slot_total * factor, precision=highest
    ).reshape(steps, beam_total, head_count)
    page_out = jnp.einsum(
        "sr,zsbhd->zrbhd", owner_float, slot_out * factor[..., None], precision=highest
    ).reshape(steps, beam_total, head_count, HD)
    stats = jnp.concatenate(
        [
            page_total.astype(jnp.bfloat16),
            top_high.reshape(steps, beam_total, head_count),
            top_low.reshape(steps, beam_total, head_count),
        ],
        axis=-1,
    )
    packed = jnp.concatenate(
        [
            page_out.astype(jnp.bfloat16).reshape(steps, beam_total, head_count * HD),
            jnp.pad(stats, ((0, 0), (0, 0), (0, HD - 3 * head_count))),
        ],
        axis=-1,
    )
    packed = packed.reshape(steps, req_size, own_count, -1).transpose(1, 0, 2, 3)
    held, activated_all = exchange_gelu(packed, summed_all, triple_width, "req", req_size, 5)
    held = held.astype(jnp.float32)
    base = head_count * HD
    held_top = held[..., base + head_count : base + 2 * head_count] + held[
        ..., base + 2 * head_count : base + 3 * head_count
    ]
    own_top = jnp.max(held_top, axis=0)
    rescale = jnp.exp(held_top - own_top)
    own_total = jnp.sum(held[..., base : base + head_count] * rescale, axis=0)
    own_out = jnp.stack(
        [
            jnp.sum(held[..., head * HD : (head + 1) * HD] * rescale[..., head : head + 1], axis=0)
            for head in range(head_count)
        ],
        axis=2,
    )

    source = own_group * BEAM + parents[0]
    def history(table):
        empty = jnp.zeros_like(table[0])
        return jnp.stack(
            [
                jnp.stack(
                    [
                        pick_rows(table[n], source) if n < s else table[s] if n == s else empty
                        for n in range(steps)
                    ]
                )
                for s in range(steps)
            ]
        )

    filled = (
        jnp.arange(steps, dtype=jnp.int32)[None, :] <= jnp.arange(steps, dtype=jnp.int32)[:, None]
    )[:, None, None, :]
    own_scores = (
        jnp.einsum(
            "zbhd,znbhd->zbhn", queries_own, history(keys_new), preferred_element_type=jnp.float32
        )
        * scale
    )
    own_scores = jnp.where(filled, own_scores, NEG_FILL)
    top = jnp.maximum(own_top, jnp.max(own_scores, axis=3))
    page_factor = jnp.exp(own_top - top)
    own_weights = jnp.where(filled, jnp.exp(own_scores - top[..., None]), 0.0)
    total = own_total * page_factor + jnp.sum(own_weights, axis=3)
    summed = own_out * page_factor[..., None] + jnp.einsum(
        "zbhn,znbhd->zbhd",
        own_weights.astype(jnp.bfloat16),
        history(values_new),
        preferred_element_type=jnp.float32,
    )
    attended = (summed / total[..., None]).astype(jnp.bfloat16).reshape(
        steps, own_count, head_count * HD
    )
    attended_all = exchange(attended, "req", req_size, True, 6)
    attended_msi = (
        attended_all.reshape(req_size, steps, per_own, local_rows, -1)
        .transpose(0, 2, 1, 3, 4)
        .reshape(steps * beam_total, -1)
    )
    update_partial = (
        jnp.dot(attended_msi, dense_weight, preferred_element_type=jnp.float32)
        + jnp.dot(activated_all, down_weight, preferred_element_type=jnp.float32)
    ).astype(jnp.bfloat16)
    update = jnp.sum(
        exchange(
            update_partial.reshape(mlp_size, steps * local_rows, local_width),
            "mlp",
            mlp_size,
            False,
            1,
        ).astype(jnp.float32),
        axis=0,
    )
    layer = (block + update.reshape(steps, local_rows, local_width)).astype(jnp.bfloat16)
    next_in = (row_normalize(layer.astype(jnp.float32), 4) * norm_gains[2]).astype(jnp.bfloat16)
    gathered = gather_grid(next_in, "mlp", mlp_size, 2).reshape(steps * beam_total, -1)
    next_partial = jnp.dot(gathered, next_weight, preferred_element_type=jnp.float32)
    next_out = lax.psum_scatter(
        next_partial.astype(jnp.bfloat16), "req", scatter_dimension=0, tiled=True
    )
    next_out = (
        next_out.reshape(per_own, steps, local_rows, -1)
        .transpose(1, 0, 2, 3)
        .reshape(steps, own_count, -1)
    )
    return (layer, next_out)


def solution(mesh):
    in_specs = (
        P(None, "mlp", "req"),
        P(None, "req"),
        P("req", "mlp"),
        P("req", "mlp"),
        P("mlp", "req"),
        P("mlp", "req"),
        P("req", "mlp"),
        P("req", None, "mlp"),
        P("req", None, "mlp"),
        P(),
        P(None, "req"),
        P(None, "req"),
    )
    out_specs = (P(None, "mlp", "req"), P(None, "req", "mlp"))
    return jax.shard_map(shards, mesh=mesh, in_specs=in_specs, out_specs=out_specs, check_vma=False)
```

```python
import functools
import math

import jax
import jax.numpy as jnp
from jax import lax
from jax.experimental import pallas as pl
from jax.experimental.pallas import tpu as pltpu
from jax.sharding import PartitionSpec as P

MESH = pl.DeviceIdType.MESH

HD = 128
ROT = 32
PAGE = 128
BEAM = 8
STEPS = 2


NEG_FILL = -1e30
EPSILON = 1e-05


def rotate(vectors, positions):
    half = ROT // 2
    freq = jnp.exp(jnp.arange(half, dtype=jnp.float32) * (-2.0 * math.log(10000.0) / ROT))
    angles = positions.astype(jnp.float32)[..., None] * freq
    cosine = jnp.concatenate([jnp.cos(angles), jnp.cos(angles)], axis=-1)[..., None, :]
    sine = jnp.concatenate([jnp.sin(angles), jnp.sin(angles)], axis=-1)[..., None, :]
    turned = vectors[..., :ROT]
    swapped = jnp.concatenate([-turned[..., half:], turned[..., :half]], axis=-1)
    return jnp.concatenate([turned * cosine + swapped * sine, vectors[..., ROT:]], axis=-1)


def pick_rows(table, index):
    flat = table.reshape(table.shape[0], -1)
    hot = (index.reshape(-1)[:, None] == jnp.arange(table.shape[0], dtype=jnp.int32)[None, :])
    taken = jnp.dot(hot.astype(table.dtype), flat, preferred_element_type=jnp.float32)
    return taken.astype(table.dtype).reshape(index.shape + table.shape[1:])


def rotate_rows(rows, positions, head_count):
    half = ROT // 2
    freq = jnp.exp(jnp.arange(half, dtype=jnp.float32) * (-2.0 * math.log(10000.0) / ROT))
    angles = positions.astype(jnp.float32)[:, None] * freq[None, :]
    cosine = jnp.concatenate([jnp.cos(angles), jnp.cos(angles)], axis=1)
    sine = jnp.concatenate([jnp.sin(angles), jnp.sin(angles)], axis=1)
    parts = []
    for head in range(head_count):
        base = head * HD
        turned = rows[:, base : base + ROT]
        swapped = jnp.concatenate([-turned[:, half:], turned[:, :half]], axis=1)
        parts += [turned * cosine + swapped * sine, rows[:, base + ROT : base + HD]]
    return jnp.concatenate(parts, axis=1)


def exchange_kernel(axis, n, gather, x_ref, out_ref, send_sem, recv_sem, local_sem):
    me = lax.axis_index(axis)
    barrier = pltpu.get_barrier_semaphore()
    for k in range(1, n):
        pl.semaphore_signal(
            barrier, inc=1, device_id={axis: lax.rem(me + k, n)}, device_id_type=MESH
        )
    pl.semaphore_wait(barrier, n - 1)
    local = pltpu.make_async_copy(x_ref if gather else x_ref.at[me], out_ref.at[me], local_sem)
    local.start()
    copies = []
    for k in range(1, n):
        dest = lax.rem(me + k, n)
        copy = pltpu.make_async_remote_copy(
            src_ref=x_ref if gather else x_ref.at[dest],
            dst_ref=out_ref.at[me],
            send_sem=send_sem.at[k],
            recv_sem=recv_sem.at[k],
            device_id={axis: dest},
            device_id_type=MESH,
        )
        copy.start()
        copies.append(copy)
    for copy in copies:
        copy.wait()
    local.wait()


def exchange_gelu_kernel(
    axis, n, gather, start, first_row, x_ref, hidden_ref, out_ref, act_ref, send_sem, recv_sem, local_sem
):
    me = lax.axis_index(axis)
    barrier = pltpu.get_barrier_semaphore()
    for k in range(1, n):
        pl.semaphore_signal(
            barrier, inc=1, device_id={axis: lax.rem(me + k, n)}, device_id_type=MESH
        )
    pl.semaphore_wait(barrier, n - 1)
    local = pltpu.make_async_copy(x_ref if gather else x_ref.at[me], out_ref.at[me], local_sem)
    local.start()
    copies = []
    for k in range(1, n):
        dest = lax.rem(me + k, n)
        copy = pltpu.make_async_remote_copy(
            src_ref=x_ref if gather else x_ref.at[dest],
            dst_ref=out_ref.at[me],
            send_sem=send_sem.at[k],
            recv_sem=recv_sem.at[k],
            device_id={axis: dest},
            device_id_type=MESH,
        )
        copy.start()
        copies.append(copy)
    tile = 128

    @pl.loop(0, act_ref.shape[0] // tile)
    def _(index):
        rows = pl.ds(pl.multiple_of(index * tile, tile), tile)
        source = pl.ds(pl.multiple_of(first_row + index * tile, tile), tile)
        values = hidden_ref[source, start : start + act_ref.shape[1]].astype(jnp.float32)
        gelu = 0.5 * values * (1.0 + lax.erf(values * (1.0 / math.sqrt(2.0))))
        act_ref[rows, :] = gelu.astype(act_ref.dtype)

    for copy in copies:
        copy.wait()
    local.wait()


def exchange_gelu(x, summed, start, first_row, row_count, axis, n, gather, collective_id):
    hidden = jax.ShapeDtypeStruct((row_count, summed.shape[1] - start), jnp.bfloat16)
    shape = (n,) + (x.shape if gather else x.shape[1:])
    return pl.pallas_call(
        functools.partial(exchange_gelu_kernel, axis, n, gather, start, first_row),
        out_shape=(
            jax.ShapeDtypeStruct(shape, x.dtype),
            hidden,
        ),
        in_specs=[pl.BlockSpec(memory_space=pltpu.VMEM)] * 2,
        out_specs=(pl.BlockSpec(memory_space=pltpu.VMEM),) * 2,
        scratch_shapes=[
            pltpu.SemaphoreType.DMA((n,)),
            pltpu.SemaphoreType.DMA((n,)),
            pltpu.SemaphoreType.DMA(()),
        ],
        compiler_params=pltpu.CompilerParams(
            collective_id=collective_id, has_side_effects=True
        ),
        cost_estimate=pl.CostEstimate(
            flops=20 * hidden.size,
            transcendentals=hidden.size,
            bytes_accessed=2 * n * x.size * x.dtype.itemsize + 4 * hidden.size,
        ),
    )(x, summed)


def gather_grid_kernel(axis, side, x_ref, out_ref, send_sem, recv_sem, local_sem):
    me = lax.axis_index(axis)
    row, col = me // side, me % side
    row_peers = [row * side + lax.rem(col + k, side) for k in range(1, side)]
    col_peers = [lax.rem(row + k, side) * side + col for k in range(1, side)]
    barrier = pltpu.get_barrier_semaphore()
    for peer in row_peers + col_peers:
        pl.semaphore_signal(barrier, inc=1, device_id={axis: peer}, device_id_type=MESH)
    pl.semaphore_wait(barrier, 2 * (side - 1))
    local = pltpu.make_async_copy(x_ref, out_ref.at[me], local_sem)
    local.start()
    first = []
    for k, peer in enumerate(row_peers):
        copy = pltpu.make_async_remote_copy(
            src_ref=x_ref,
            dst_ref=out_ref.at[me],
            send_sem=send_sem.at[0, k],
            recv_sem=recv_sem.at[0, k],
            device_id={axis: peer},
            device_id_type=MESH,
        )
        copy.start()
        first.append(copy)
    for copy in first:
        copy.wait()
    local.wait()
    slab = out_ref.at[pl.ds(row * side, side)]
    second = []
    for k, peer in enumerate(col_peers):
        copy = pltpu.make_async_remote_copy(
            src_ref=slab,
            dst_ref=slab,
            send_sem=send_sem.at[1, k],
            recv_sem=recv_sem.at[1, k],
            device_id={axis: peer},
            device_id_type=MESH,
        )
        copy.start()
        second.append(copy)
    for copy in second:
        copy.wait()


def gather_grid(x, axis, n, collective_id):
    side = math.isqrt(n)
    return pl.pallas_call(
        functools.partial(gather_grid_kernel, axis, side),
        out_shape=jax.ShapeDtypeStruct((n,) + x.shape, x.dtype),
        in_specs=[pl.BlockSpec(memory_space=pltpu.VMEM)],
        out_specs=pl.BlockSpec(memory_space=pltpu.VMEM),
        scratch_shapes=[
            pltpu.SemaphoreType.DMA((2, side - 1)),
            pltpu.SemaphoreType.DMA((2, side - 1)),
            pltpu.SemaphoreType.DMA(()),
        ],
        compiler_params=pltpu.CompilerParams(
            collective_id=collective_id, has_side_effects=True
        ),
        cost_estimate=pl.CostEstimate(
            flops=0, transcendentals=0, bytes_accessed=2 * n * x.size * x.dtype.itemsize
        ),
    )(x)


def exchange(x, axis, n, gather, collective_id):
    shape = (n,) + (x.shape if gather else x.shape[1:])
    return pl.pallas_call(
        functools.partial(exchange_kernel, axis, n, gather),
        out_shape=jax.ShapeDtypeStruct(shape, x.dtype),
        in_specs=[pl.BlockSpec(memory_space=pltpu.VMEM)],
        out_specs=pl.BlockSpec(memory_space=pltpu.VMEM),
        scratch_shapes=[
            pltpu.SemaphoreType.DMA((n,)),
            pltpu.SemaphoreType.DMA((n,)),
            pltpu.SemaphoreType.DMA(()),
        ],
        compiler_params=pltpu.CompilerParams(
            collective_id=collective_id, has_side_effects=True
        ),
        cost_estimate=pl.CostEstimate(
            flops=0, transcendentals=0, bytes_accessed=2 * n * x.size * x.dtype.itemsize
        ),
    )(x)


def exchange_flat(x, axis, n, gather, collective_id):
    lead = () if gather else x.shape[:1]
    block_shape = x.shape if gather else x.shape[1:]
    size = math.prod(block_shape)
    padded = -(-size // 128) * 128
    flat = x.reshape(lead + (size,))
    flat = jnp.pad(flat, [(0, 0)] * len(lead) + [(0, padded - size)])
    flat = flat.reshape(lead + (padded // 128, 128))
    out = exchange(flat, axis, n, gather, collective_id)
    return out.reshape(n, padded)[:, :size].reshape((n,) + block_shape)


def row_normalize(values, collective_id):
    width = values.shape[-1]
    local_mean = jnp.mean(values, axis=-1)
    centred = values - local_mean[..., None]
    local_m2 = jnp.sum(centred * centred, axis=-1)
    stats = jnp.stack([local_mean, local_m2], axis=0)
    stats = exchange_flat(stats, "req", lax.axis_size("req"), True, collective_id)
    stats = jnp.moveaxis(stats, 1, -1)
    means = stats[..., 0]
    row_mean = jnp.mean(means, axis=0)
    spread = means - row_mean
    row_m2 = jnp.sum(stats[..., 1], axis=0) + width * jnp.sum(spread * spread, axis=0)
    row_var = row_m2 / (width * stats.shape[0])
    return (values - row_mean[..., None]) * lax.rsqrt(row_var + EPSILON)[..., None]


def shards(
    inputs,
    norm_gains,
    attn_weight,
    up_weight,
    dense_weight,
    down_weight,
    next_weight,
    cache_keys,
    cache_values,
    lengths,
    slot_table,
    parents,
):
    scale = 1.0 / math.sqrt(HD)
    highest = lax.Precision.HIGHEST
    steps, local_rows, local_width = inputs.shape
    own_count = parents.shape[1]
    request_count = lengths.shape[0]
    beam_total = request_count * BEAM
    head_count = dense_weight.shape[0] // HD
    triple_width = attn_weight.shape[1]
    slot_count = slot_table.shape[1]
    req_size = beam_total // own_count
    mlp_size = beam_total // local_rows
    offset = lax.axis_index("req") * own_count
    beam_group = jnp.arange(beam_total, dtype=jnp.int32) // BEAM
    all_positions = lengths[beam_group][None, :] + jnp.arange(steps, dtype=jnp.int32)[:, None]
    own_group = jnp.arange(own_count, dtype=jnp.int32) // BEAM
    slot_owner = slot_table[0]
    slot_pageno = slot_table[1]
    valid_owner = jnp.maximum(slot_owner, 0)
    token_pos = slot_pageno[:, None] * PAGE + jnp.arange(PAGE, dtype=jnp.int32)[None, :]
    live = (slot_owner[:, None] >= 0) & (token_pos < lengths[valid_owner][:, None])
    live_wide = live[None, :, None, None, :]
    owner_mask = slot_owner[:, None] == jnp.arange(request_count, dtype=jnp.int32)[None, :]
    owner_float = owner_mask.astype(jnp.float32)
    gather_rows = valid_owner[:, None] * BEAM + jnp.arange(BEAM, dtype=jnp.int32)[None, :]

    block = inputs.astype(jnp.float32)
    rows_all = gather_grid(inputs, "mlp", mlp_size, 0).reshape(steps * beam_total, -1)
    normed = row_normalize(rows_all.astype(jnp.float32), 3)
    attn_in = (normed * norm_gains[0]).astype(jnp.bfloat16)
    mlp_in = (normed * norm_gains[1]).astype(jnp.bfloat16)
    grouped = (
        attn_weight.reshape(local_width, head_count, 3, HD)
        .transpose(0, 2, 1, 3)
        .reshape(local_width, triple_width)
    )
    first = jnp.dot(attn_in, grouped, preferred_element_type=jnp.float32)
    second = jnp.dot(mlp_in, up_weight, preferred_element_type=jnp.float32)
    partial_sums = jnp.concatenate([first, second], axis=1)
    summed_all = lax.psum(partial_sums.astype(jnp.bfloat16), "req")
    width = head_count * HD
    row = jnp.arange(steps * beam_total, dtype=jnp.int32)
    beam_lengths = jnp.broadcast_to(lengths[:, None], (request_count, BEAM)).reshape(
        mlp_size, 1, local_rows
    )
    row_positions = (
        beam_lengths + jnp.arange(steps, dtype=jnp.int32)[None, :, None]
    ).reshape(steps * beam_total)
    queries_rows = rotate_rows(
        summed_all[:, :width].astype(jnp.float32), row_positions, head_count
    ).astype(jnp.bfloat16)
    per_own = own_count // local_rows
    own_start = lax.axis_index("req") * (per_own * steps * local_rows)

    def own_rows(rows):
        return lax.dynamic_slice_in_dim(rows, own_start, per_own * steps * local_rows, 0)

    def by_step(rows):
        return (
            rows.reshape(per_own, steps, local_rows, -1)
            .transpose(1, 0, 2, 3)
            .reshape(steps, own_count, head_count, HD)
        )

    queries_own = by_step(own_rows(queries_rows))
    keys_new = by_step(
        rotate_rows(
            own_rows(summed_all[:, width : 2 * width].astype(jnp.float32)),
            own_rows(row_positions),
            head_count,
        ).astype(jnp.bfloat16)
    )
    values_new = by_step(own_rows(summed_all[:, 2 * width : 3 * width]))

    chosen_rows = (
        (gather_rows // local_rows) * (steps * local_rows)
        + jnp.arange(steps, dtype=jnp.int32)[:, None, None] * local_rows
        + gather_rows % local_rows
    )
    chosen = pick_rows(queries_rows, chosen_rows)
    head_scores = [
        jnp.einsum(
            "zsbd,std->zsbt",
            chosen[..., head * HD : (head + 1) * HD],
            cache_keys[:, :, head * HD : (head + 1) * HD],
            preferred_element_type=jnp.float32,
        )
        for head in range(head_count)
    ]
    scores = jnp.stack(head_scores, axis=3) * scale
    masked = jnp.where(live_wide, scores, NEG_FILL)
    slot_top = jnp.max(masked, axis=4)
    weights = jnp.where(live_wide, jnp.exp(masked - slot_top[..., None]), 0.0)
    slot_total = jnp.sum(weights, axis=4)
    rounded = weights.astype(jnp.bfloat16)
    slot_out = jnp.stack(
        [
            jnp.einsum(
                "zsbt,std->zsbd",
                rounded[:, :, :, head],
                cache_values[:, :, head * HD : (head + 1) * HD],
                preferred_element_type=jnp.float32,
            )
            for head in range(head_count)
        ],
        axis=3,
    )
    request_top = jnp.max(
        jnp.where(owner_mask[None, :, :, None, None], slot_top[:, :, None], NEG_FILL), axis=1
    )
    top_high = request_top.astype(jnp.bfloat16)
    top_low = (request_top - top_high.astype(jnp.float32)).astype(jnp.bfloat16)
    request_top = top_high.astype(jnp.float32) + top_low.astype(jnp.float32)
    factor = jnp.where(
        (slot_owner[None, :, None, None] >= 0) & (slot_top > 0.5 * NEG_FILL),
        jnp.exp(slot_top - request_top[:, valid_owner]),
        0.0,
    )
    page_total = jnp.einsum(
        "sr,zsbh->zrbh", owner_float, slot_total * factor, precision=highest
    ).reshape(steps, beam_total, head_count)
    page_out = jnp.einsum(
        "sr,zsbhd->zrbhd", owner_float, slot_out * factor[..., None], precision=highest
    ).reshape(steps, beam_total, head_count, HD)
    stats = jnp.concatenate(
        [
            page_total.astype(jnp.bfloat16),
            top_high.reshape(steps, beam_total, head_count),
            top_low.reshape(steps, beam_total, head_count),
        ],
        axis=-1,
    )
    packed = jnp.concatenate(
        [
            page_out.astype(jnp.bfloat16).reshape(steps, beam_total, head_count * HD),
            jnp.pad(stats, ((0, 0), (0, 0), (0, HD - 3 * head_count))),
        ],
        axis=-1,
    )
    packed = packed.reshape(steps, req_size, own_count, -1).transpose(1, 0, 2, 3)
    split_row = steps * beam_total // 2
    held, activated_first = exchange_gelu(
        packed, summed_all, triple_width, 0, split_row, "req", req_size, False, 5
    )
    held = held.astype(jnp.float32)
    base = head_count * HD
    held_top = held[..., base + head_count : base + 2 * head_count] + held[
        ..., base + 2 * head_count : base + 3 * head_count
    ]
    own_top = jnp.max(held_top, axis=0)
    rescale = jnp.exp(held_top - own_top)
    own_total = jnp.sum(held[..., base : base + head_count] * rescale, axis=0)
    own_out = jnp.stack(
        [
            jnp.sum(held[..., head * HD : (head + 1) * HD] * rescale[..., head : head + 1], axis=0)
            for head in range(head_count)
        ],
        axis=2,
    )

    source = own_group * BEAM + parents[0]
    def history(table):
        empty = jnp.zeros_like(table[0])
        return jnp.stack(
            [
                jnp.stack(
                    [
                        pick_rows(table[n], source) if n < s else table[s] if n == s else empty
                        for n in range(steps)
                    ]
                )
                for s in range(steps)
            ]
        )

    filled = (
        jnp.arange(steps, dtype=jnp.int32)[None, :] <= jnp.arange(steps, dtype=jnp.int32)[:, None]
    )[:, None, None, :]
    own_scores = (
        jnp.einsum(
            "zbhd,znbhd->zbhn", queries_own, history(keys_new), preferred_element_type=jnp.float32
        )
        * scale
    )
    own_scores = jnp.where(filled, own_scores, NEG_FILL)
    top = jnp.maximum(own_top, jnp.max(own_scores, axis=3))
    page_factor = jnp.exp(own_top - top)
    own_weights = jnp.where(filled, jnp.exp(own_scores - top[..., None]), 0.0)
    total = own_total * page_factor + jnp.sum(own_weights, axis=3)
    summed = own_out * page_factor[..., None] + jnp.einsum(
        "zbhn,znbhd->zbhd",
        own_weights.astype(jnp.bfloat16),
        history(values_new),
        preferred_element_type=jnp.float32,
    )
    attended = (summed / total[..., None]).astype(jnp.bfloat16).reshape(
        steps, own_count, head_count * HD
    )
    attended_all, activated_second = exchange_gelu(
        attended, summed_all, triple_width, split_row, split_row, "req", req_size, True, 6
    )
    activated_all = jnp.concatenate([activated_first, activated_second], axis=0)
    attended_msi = (
        attended_all.reshape(req_size, steps, per_own, local_rows, -1)
        .transpose(0, 2, 1, 3, 4)
        .reshape(steps * beam_total, -1)
    )
    update_partial = (
        jnp.dot(attended_msi, dense_weight, preferred_element_type=jnp.float32)
        + jnp.dot(activated_all, down_weight, preferred_element_type=jnp.float32)
    ).astype(jnp.bfloat16)
    update = jnp.sum(
        exchange(
            update_partial.reshape(mlp_size, steps * local_rows, local_width),
            "mlp",
            mlp_size,
            False,
            1,
        ).astype(jnp.float32),
        axis=0,
    )
    layer = (block + update.reshape(steps, local_rows, local_width)).astype(jnp.bfloat16)
    next_in = (row_normalize(layer.astype(jnp.float32), 4) * norm_gains[2]).astype(jnp.bfloat16)
    gathered = gather_grid(next_in, "mlp", mlp_size, 2).reshape(steps * beam_total, -1)
    next_partial = jnp.dot(gathered, next_weight, preferred_element_type=jnp.float32)
    next_out = lax.psum_scatter(
        next_partial.astype(jnp.bfloat16), "req", scatter_dimension=0, tiled=True
    )
    next_out = (
        next_out.reshape(per_own, steps, local_rows, -1)
        .transpose(1, 0, 2, 3)
        .reshape(steps, own_count, -1)
    )
    return (layer, next_out)


def solution(mesh):
    in_specs = (
        P(None, "mlp", "req"),
        P(None, "req"),
        P("req", "mlp"),
        P("req", "mlp"),
        P("mlp", "req"),
        P("mlp", "req"),
        P("req", "mlp"),
        P("req", None, "mlp"),
        P("req", None, "mlp"),
        P(),
        P(None, "req"),
        P(None, "req"),
    )
    out_specs = (P(None, "mlp", "req"), P(None, "req", "mlp"))
    return jax.shard_map(shards, mesh=mesh, in_specs=in_specs, out_specs=out_specs, check_vma=False)
```

```python
import functools
import math

import jax
import jax.numpy as jnp
from jax import lax
from jax.experimental import pallas as pl
from jax.experimental.pallas import tpu as pltpu
from jax.sharding import PartitionSpec as P

MESH = pl.DeviceIdType.MESH

HD = 128
ROT = 32
PAGE = 128
BEAM = 8
STEPS = 2


NEG_FILL = -1e30
EPSILON = 1e-05


def rotate(vectors, positions):
    half = ROT // 2
    freq = jnp.exp(jnp.arange(half, dtype=jnp.float32) * (-2.0 * math.log(10000.0) / ROT))
    angles = positions.astype(jnp.float32)[..., None] * freq
    cosine = jnp.concatenate([jnp.cos(angles), jnp.cos(angles)], axis=-1)[..., None, :]
    sine = jnp.concatenate([jnp.sin(angles), jnp.sin(angles)], axis=-1)[..., None, :]
    turned = vectors[..., :ROT]
    swapped = jnp.concatenate([-turned[..., half:], turned[..., :half]], axis=-1)
    return jnp.concatenate([turned * cosine + swapped * sine, vectors[..., ROT:]], axis=-1)


def pick_rows(table, index):
    flat = table.reshape(table.shape[0], -1)
    hot = (index.reshape(-1)[:, None] == jnp.arange(table.shape[0], dtype=jnp.int32)[None, :])
    taken = jnp.dot(hot.astype(table.dtype), flat, preferred_element_type=jnp.float32)
    return taken.astype(table.dtype).reshape(index.shape + table.shape[1:])


def rotate_rows(rows, positions, head_count):
    half = ROT // 2
    freq = jnp.exp(jnp.arange(half, dtype=jnp.float32) * (-2.0 * math.log(10000.0) / ROT))
    angles = positions.astype(jnp.float32)[:, None] * freq[None, :]
    cosine = jnp.concatenate([jnp.cos(angles), jnp.cos(angles)], axis=1)
    sine = jnp.concatenate([jnp.sin(angles), jnp.sin(angles)], axis=1)
    parts = []
    for head in range(head_count):
        base = head * HD
        turned = rows[:, base : base + ROT]
        swapped = jnp.concatenate([-turned[:, half:], turned[:, :half]], axis=1)
        parts += [turned * cosine + swapped * sine, rows[:, base + ROT : base + HD]]
    return jnp.concatenate(parts, axis=1)


def exchange_kernel(axis, n, gather, x_ref, out_ref, send_sem, recv_sem, local_sem):
    me = lax.axis_index(axis)
    barrier = pltpu.get_barrier_semaphore()
    for k in range(1, n):
        pl.semaphore_signal(
            barrier, inc=1, device_id={axis: lax.rem(me + k, n)}, device_id_type=MESH
        )
    pl.semaphore_wait(barrier, n - 1)
    local = pltpu.make_async_copy(x_ref if gather else x_ref.at[me], out_ref.at[me], local_sem)
    local.start()
    copies = []
    for k in range(1, n):
        dest = lax.rem(me + k, n)
        copy = pltpu.make_async_remote_copy(
            src_ref=x_ref if gather else x_ref.at[dest],
            dst_ref=out_ref.at[me],
            send_sem=send_sem.at[k],
            recv_sem=recv_sem.at[k],
            device_id={axis: dest},
            device_id_type=MESH,
        )
        copy.start()
        copies.append(copy)
    for copy in copies:
        copy.wait()
    local.wait()


def exchange_gelu_kernel(axis, n, start, x_ref, hidden_ref, out_ref, act_ref, send_sem, recv_sem, local_sem):
    me = lax.axis_index(axis)
    barrier = pltpu.get_barrier_semaphore()
    for k in range(1, n):
        pl.semaphore_signal(
            barrier, inc=1, device_id={axis: lax.rem(me + k, n)}, device_id_type=MESH
        )
    pl.semaphore_wait(barrier, n - 1)
    local = pltpu.make_async_copy(x_ref.at[me], out_ref.at[me], local_sem)
    local.start()
    copies = []
    for k in range(1, n):
        dest = lax.rem(me + k, n)
        copy = pltpu.make_async_remote_copy(
            src_ref=x_ref.at[dest],
            dst_ref=out_ref.at[me],
            send_sem=send_sem.at[k],
            recv_sem=recv_sem.at[k],
            device_id={axis: dest},
            device_id_type=MESH,
        )
        copy.start()
        copies.append(copy)
    tile = 128

    @pl.loop(0, hidden_ref.shape[0] // tile)
    def _(index):
        rows = pl.ds(pl.multiple_of(index * tile, tile), tile)
        values = hidden_ref[rows, start : start + act_ref.shape[1]].astype(jnp.float32)
        gelu = 0.5 * values * (1.0 + lax.erf(values * (1.0 / math.sqrt(2.0))))
        act_ref[rows, :] = gelu.astype(act_ref.dtype)

    for copy in copies:
        copy.wait()
    local.wait()


def exchange_gelu(x, summed, start, axis, n, collective_id):
    hidden = jax.ShapeDtypeStruct((summed.shape[0], summed.shape[1] - start), jnp.bfloat16)
    return pl.pallas_call(
        functools.partial(exchange_gelu_kernel, axis, n, start),
        out_shape=(
            jax.ShapeDtypeStruct(x.shape, x.dtype),
            hidden,
        ),
        in_specs=[pl.BlockSpec(memory_space=pltpu.VMEM)] * 2,
        out_specs=(pl.BlockSpec(memory_space=pltpu.VMEM),) * 2,
        scratch_shapes=[
            pltpu.SemaphoreType.DMA((n,)),
            pltpu.SemaphoreType.DMA((n,)),
            pltpu.SemaphoreType.DMA(()),
        ],
        compiler_params=pltpu.CompilerParams(
            collective_id=collective_id, has_side_effects=True
        ),
        cost_estimate=pl.CostEstimate(
            flops=20 * hidden.size,
            transcendentals=hidden.size,
            bytes_accessed=2 * n * x.size * x.dtype.itemsize + 4 * hidden.size,
        ),
    )(x, summed)


def gather_grid_kernel(axis, side, x_ref, out_ref, send_sem, recv_sem, local_sem):
    me = lax.axis_index(axis)
    row, col = me // side, me % side
    row_peers = [row * side + lax.rem(col + k, side) for k in range(1, side)]
    col_peers = [lax.rem(row + k, side) * side + col for k in range(1, side)]
    barrier = pltpu.get_barrier_semaphore()
    for peer in row_peers + col_peers:
        pl.semaphore_signal(barrier, inc=1, device_id={axis: peer}, device_id_type=MESH)
    pl.semaphore_wait(barrier, 2 * (side - 1))
    local = pltpu.make_async_copy(x_ref, out_ref.at[me], local_sem)
    local.start()
    first = []
    for k, peer in enumerate(row_peers):
        copy = pltpu.make_async_remote_copy(
            src_ref=x_ref,
            dst_ref=out_ref.at[me],
            send_sem=send_sem.at[0, k],
            recv_sem=recv_sem.at[0, k],
            device_id={axis: peer},
            device_id_type=MESH,
        )
        copy.start()
        first.append(copy)
    for copy in first:
        copy.wait()
    local.wait()
    slab = out_ref.at[pl.ds(row * side, side)]
    second = []
    for k, peer in enumerate(col_peers):
        copy = pltpu.make_async_remote_copy(
            src_ref=slab,
            dst_ref=slab,
            send_sem=send_sem.at[1, k],
            recv_sem=recv_sem.at[1, k],
            device_id={axis: peer},
            device_id_type=MESH,
        )
        copy.start()
        second.append(copy)
    for copy in second:
        copy.wait()


def gather_grid(x, axis, n, collective_id):
    side = math.isqrt(n)
    return pl.pallas_call(
        functools.partial(gather_grid_kernel, axis, side),
        out_shape=jax.ShapeDtypeStruct((n,) + x.shape, x.dtype),
        in_specs=[pl.BlockSpec(memory_space=pltpu.VMEM)],
        out_specs=pl.BlockSpec(memory_space=pltpu.VMEM),
        scratch_shapes=[
            pltpu.SemaphoreType.DMA((2, side - 1)),
            pltpu.SemaphoreType.DMA((2, side - 1)),
            pltpu.SemaphoreType.DMA(()),
        ],
        compiler_params=pltpu.CompilerParams(
            collective_id=collective_id, has_side_effects=True
        ),
        cost_estimate=pl.CostEstimate(
            flops=0, transcendentals=0, bytes_accessed=2 * n * x.size * x.dtype.itemsize
        ),
    )(x)


def exchange(x, axis, n, gather, collective_id):
    shape = (n,) + (x.shape if gather else x.shape[1:])
    return pl.pallas_call(
        functools.partial(exchange_kernel, axis, n, gather),
        out_shape=jax.ShapeDtypeStruct(shape, x.dtype),
        in_specs=[pl.BlockSpec(memory_space=pltpu.VMEM)],
        out_specs=pl.BlockSpec(memory_space=pltpu.VMEM),
        scratch_shapes=[
            pltpu.SemaphoreType.DMA((n,)),
            pltpu.SemaphoreType.DMA((n,)),
            pltpu.SemaphoreType.DMA(()),
        ],
        compiler_params=pltpu.CompilerParams(
            collective_id=collective_id, has_side_effects=True
        ),
        cost_estimate=pl.CostEstimate(
            flops=0, transcendentals=0, bytes_accessed=2 * n * x.size * x.dtype.itemsize
        ),
    )(x)


def exchange_flat(x, axis, n, gather, collective_id):
    lead = () if gather else x.shape[:1]
    block_shape = x.shape if gather else x.shape[1:]
    size = math.prod(block_shape)
    padded = -(-size // 128) * 128
    flat = x.reshape(lead + (size,))
    flat = jnp.pad(flat, [(0, 0)] * len(lead) + [(0, padded - size)])
    flat = flat.reshape(lead + (padded // 128, 128))
    out = exchange(flat, axis, n, gather, collective_id)
    return out.reshape(n, padded)[:, :size].reshape((n,) + block_shape)


def row_normalize(values, collective_id):
    width = values.shape[-1]
    local_mean = jnp.mean(values, axis=-1)
    centred = values - local_mean[..., None]
    local_m2 = jnp.sum(centred * centred, axis=-1)
    stats = jnp.stack([local_mean, local_m2], axis=0)
    stats = exchange_flat(stats, "req", lax.axis_size("req"), True, collective_id)
    stats = jnp.moveaxis(stats, 1, -1)
    means = stats[..., 0]
    row_mean = jnp.mean(means, axis=0)
    spread = means - row_mean
    row_m2 = jnp.sum(stats[..., 1], axis=0) + width * jnp.sum(spread * spread, axis=0)
    row_var = row_m2 / (width * stats.shape[0])
    return (values - row_mean[..., None]) * lax.rsqrt(row_var + EPSILON)[..., None]


def shards(
    inputs,
    norm_gains,
    attn_weight,
    up_weight,
    dense_weight,
    down_weight,
    next_weight,
    cache_keys,
    cache_values,
    lengths,
    slot_table,
    parents,
):
    scale = 1.0 / math.sqrt(HD)
    highest = lax.Precision.HIGHEST
    steps, local_rows, local_width = inputs.shape
    own_count = parents.shape[1]
    request_count = lengths.shape[0]
    beam_total = request_count * BEAM
    head_count = dense_weight.shape[0] // HD
    triple_width = attn_weight.shape[1]
    slot_count = slot_table.shape[1]
    req_size = beam_total // own_count
    mlp_size = beam_total // local_rows
    offset = lax.axis_index("req") * own_count
    beam_group = jnp.arange(beam_total, dtype=jnp.int32) // BEAM
    all_positions = lengths[beam_group][None, :] + jnp.arange(steps, dtype=jnp.int32)[:, None]
    own_group = jnp.arange(own_count, dtype=jnp.int32) // BEAM
    slot_owner = slot_table[0]
    slot_pageno = slot_table[1]
    valid_owner = jnp.maximum(slot_owner, 0)
    token_pos = slot_pageno[:, None] * PAGE + jnp.arange(PAGE, dtype=jnp.int32)[None, :]
    live = (slot_owner[:, None] >= 0) & (token_pos < lengths[valid_owner][:, None])
    live_wide = live[None, :, None, None, :]
    owner_mask = slot_owner[:, None] == jnp.arange(request_count, dtype=jnp.int32)[None, :]
    owner_float = owner_mask.astype(jnp.float32)
    gather_rows = valid_owner[:, None] * BEAM + jnp.arange(BEAM, dtype=jnp.int32)[None, :]

    block = inputs.astype(jnp.float32)
    rows_all = exchange(inputs, "mlp", mlp_size, True, 0).reshape(steps * beam_total, -1)
    normed = row_normalize(rows_all.astype(jnp.float32), 3)
    attn_in = (normed * norm_gains[0]).astype(jnp.bfloat16)
    mlp_in = (normed * norm_gains[1]).astype(jnp.bfloat16)
    grouped = (
        attn_weight.reshape(local_width, head_count, 3, HD)
        .transpose(0, 2, 1, 3)
        .reshape(local_width, triple_width)
    )
    first = jnp.dot(attn_in, grouped, preferred_element_type=jnp.float32)
    second = jnp.dot(mlp_in, up_weight, preferred_element_type=jnp.float32)
    partial_sums = jnp.concatenate([first, second], axis=1)
    summed_all = lax.psum(partial_sums.astype(jnp.bfloat16), "req")
    width = head_count * HD
    row = jnp.arange(steps * beam_total, dtype=jnp.int32)
    beam_lengths = jnp.broadcast_to(lengths[:, None], (request_count, BEAM)).reshape(
        mlp_size, 1, local_rows
    )
    row_positions = (
        beam_lengths + jnp.arange(steps, dtype=jnp.int32)[None, :, None]
    ).reshape(steps * beam_total)
    queries_rows = rotate_rows(
        summed_all[:, :width].astype(jnp.float32), row_positions, head_count
    ).astype(jnp.bfloat16)
    per_own = own_count // local_rows
    own_start = lax.axis_index("req") * (per_own * steps * local_rows)

    def own_rows(rows):
        return lax.dynamic_slice_in_dim(rows, own_start, per_own * steps * local_rows, 0)

    def by_step(rows):
        return (
            rows.reshape(per_own, steps, local_rows, -1)
            .transpose(1, 0, 2, 3)
            .reshape(steps, own_count, head_count, HD)
        )

    queries_own = by_step(own_rows(queries_rows))
    keys_new = by_step(
        rotate_rows(
            own_rows(summed_all[:, width : 2 * width].astype(jnp.float32)),
            own_rows(row_positions),
            head_count,
        ).astype(jnp.bfloat16)
    )
    values_new = by_step(own_rows(summed_all[:, 2 * width : 3 * width]))

    chosen_rows = (
        (gather_rows // local_rows) * (steps * local_rows)
        + jnp.arange(steps, dtype=jnp.int32)[:, None, None] * local_rows
        + gather_rows % local_rows
    )
    chosen = pick_rows(queries_rows, chosen_rows)
    head_scores = [
        jnp.einsum(
            "zsbd,std->zsbt",
            chosen[..., head * HD : (head + 1) * HD],
            cache_keys[:, :, head * HD : (head + 1) * HD],
            preferred_element_type=jnp.float32,
        )
        for head in range(head_count)
    ]
    scores = jnp.stack(head_scores, axis=3) * scale
    masked = jnp.where(live_wide, scores, NEG_FILL)
    slot_top = jnp.max(masked, axis=4)
    weights = jnp.where(live_wide, jnp.exp(masked - slot_top[..., None]), 0.0)
    slot_total = jnp.sum(weights, axis=4)
    rounded = weights.astype(jnp.bfloat16)
    slot_out = jnp.stack(
        [
            jnp.einsum(
                "zsbt,std->zsbd",
                rounded[:, :, :, head],
                cache_values[:, :, head * HD : (head + 1) * HD],
                preferred_element_type=jnp.float32,
            )
            for head in range(head_count)
        ],
        axis=3,
    )
    request_top = jnp.max(
        jnp.where(owner_mask[None, :, :, None, None], slot_top[:, :, None], NEG_FILL), axis=1
    )
    top_high = request_top.astype(jnp.bfloat16)
    top_low = (request_top - top_high.astype(jnp.float32)).astype(jnp.bfloat16)
    request_top = top_high.astype(jnp.float32) + top_low.astype(jnp.float32)
    factor = jnp.where(
        (slot_owner[None, :, None, None] >= 0) & (slot_top > 0.5 * NEG_FILL),
        jnp.exp(slot_top - request_top[:, valid_owner]),
        0.0,
    )
    page_total = jnp.einsum(
        "sr,zsbh->zrbh", owner_float, slot_total * factor, precision=highest
    ).reshape(steps, beam_total, head_count)
    page_out = jnp.einsum(
        "sr,zsbhd->zrbhd", owner_float, slot_out * factor[..., None], precision=highest
    ).reshape(steps, beam_total, head_count, HD)
    stats = jnp.concatenate(
        [
            page_total.astype(jnp.bfloat16),
            top_high.reshape(steps, beam_total, head_count),
            top_low.reshape(steps, beam_total, head_count),
        ],
        axis=-1,
    )
    packed = jnp.concatenate(
        [
            page_out.astype(jnp.bfloat16).reshape(steps, beam_total, head_count * HD),
            jnp.pad(stats, ((0, 0), (0, 0), (0, HD - 3 * head_count))),
        ],
        axis=-1,
    )
    packed = packed.reshape(steps, req_size, own_count, -1).transpose(1, 0, 2, 3)
    held, activated_all = exchange_gelu(packed, summed_all, triple_width, "req", req_size, 5)
    held = held.astype(jnp.float32)
    base = head_count * HD
    held_top = held[..., base + head_count : base + 2 * head_count] + held[
        ..., base + 2 * head_count : base + 3 * head_count
    ]
    own_top = jnp.max(held_top, axis=0)
    rescale = jnp.exp(held_top - own_top)
    own_total = jnp.sum(held[..., base : base + head_count] * rescale, axis=0)
    own_out = jnp.stack(
        [
            jnp.sum(held[..., head * HD : (head + 1) * HD] * rescale[..., head : head + 1], axis=0)
            for head in range(head_count)
        ],
        axis=2,
    )

    source = own_group * BEAM + parents[0]
    def history(table):
        empty = jnp.zeros_like(table[0])
        return jnp.stack(
            [
                jnp.stack(
                    [
                        pick_rows(table[n], source) if n < s else table[s] if n == s else empty
                        for n in range(steps)
                    ]
                )
                for s in range(steps)
            ]
        )

    filled = (
        jnp.arange(steps, dtype=jnp.int32)[None, :] <= jnp.arange(steps, dtype=jnp.int32)[:, None]
    )[:, None, None, :]
    own_scores = (
        jnp.einsum(
            "zbhd,znbhd->zbhn", queries_own, history(keys_new), preferred_element_type=jnp.float32
        )
        * scale
    )
    own_scores = jnp.where(filled, own_scores, NEG_FILL)
    top = jnp.maximum(own_top, jnp.max(own_scores, axis=3))
    page_factor = jnp.exp(own_top - top)
    own_weights = jnp.where(filled, jnp.exp(own_scores - top[..., None]), 0.0)
    total = own_total * page_factor + jnp.sum(own_weights, axis=3)
    summed = own_out * page_factor[..., None] + jnp.einsum(
        "zbhn,znbhd->zbhd",
        own_weights.astype(jnp.bfloat16),
        history(values_new),
        preferred_element_type=jnp.float32,
    )
    attended = (summed / total[..., None]).astype(jnp.bfloat16).reshape(
        steps, own_count, head_count * HD
    )
    attended_all = exchange(attended, "req", req_size, True, 6)
    attended_msi = (
        attended_all.reshape(req_size, steps, per_own, local_rows, -1)
        .transpose(0, 2, 1, 3, 4)
        .reshape(steps * beam_total, -1)
    )
    update_partial = (
        jnp.dot(attended_msi, dense_weight, preferred_element_type=jnp.float32)
        + jnp.dot(activated_all, down_weight, preferred_element_type=jnp.float32)
    ).astype(jnp.bfloat16)
    update = jnp.sum(
        exchange(
            update_partial.reshape(mlp_size, steps * local_rows, local_width),
            "mlp",
            mlp_size,
            False,
            1,
        ).astype(jnp.float32),
        axis=0,
    )
    layer = (block + update.reshape(steps, local_rows, local_width)).astype(jnp.bfloat16)
    next_in = (row_normalize(layer.astype(jnp.float32), 4) * norm_gains[2]).astype(jnp.bfloat16)
    gathered = exchange(next_in, "mlp", mlp_size, True, 2).reshape(steps * beam_total, -1)
    next_partial = jnp.dot(gathered, next_weight, preferred_element_type=jnp.float32)
    next_out = lax.psum_scatter(
        next_partial.astype(jnp.bfloat16), "req", scatter_dimension=0, tiled=True
    )
    next_out = (
        next_out.reshape(per_own, steps, local_rows, -1)
        .transpose(1, 0, 2, 3)
        .reshape(steps, own_count, -1)
    )
    return (layer, next_out)


def solution(mesh):
    in_specs = (
        P(None, "mlp", "req"),
        P(None, "req"),
        P("req", "mlp"),
        P("req", "mlp"),
        P("mlp", "req"),
        P("mlp", "req"),
        P("req", "mlp"),
        P("req", None, "mlp"),
        P("req", None, "mlp"),
        P(),
        P(None, "req"),
        P(None, "req"),
    )
    out_specs = (P(None, "mlp", "req"), P(None, "req", "mlp"))
    return jax.shard_map(shards, mesh=mesh, in_specs=in_specs, out_specs=out_specs, check_vma=False)
```

```python
import functools
import math

import jax
import jax.numpy as jnp
from jax import lax
from jax.experimental import pallas as pl
from jax.experimental.pallas import tpu as pltpu
from jax.sharding import PartitionSpec as P

MESH = pl.DeviceIdType.MESH

HD = 128
ROT = 32
PAGE = 128
BEAM = 8
STEPS = 2


NEG_FILL = -1e30
EPSILON = 1e-05


def rotate(vectors, positions):
    half = ROT // 2
    freq = jnp.exp(jnp.arange(half, dtype=jnp.float32) * (-2.0 * math.log(10000.0) / ROT))
    angles = positions.astype(jnp.float32)[..., None] * freq
    cosine = jnp.concatenate([jnp.cos(angles), jnp.cos(angles)], axis=-1)[..., None, :]
    sine = jnp.concatenate([jnp.sin(angles), jnp.sin(angles)], axis=-1)[..., None, :]
    turned = vectors[..., :ROT]
    swapped = jnp.concatenate([-turned[..., half:], turned[..., :half]], axis=-1)
    return jnp.concatenate([turned * cosine + swapped * sine, vectors[..., ROT:]], axis=-1)


def pick_rows(table, index):
    flat = table.reshape(table.shape[0], -1)
    hot = (index.reshape(-1)[:, None] == jnp.arange(table.shape[0], dtype=jnp.int32)[None, :])
    taken = jnp.dot(hot.astype(table.dtype), flat, preferred_element_type=jnp.float32)
    return taken.astype(table.dtype).reshape(index.shape + table.shape[1:])


def rotate_rows(rows, positions, head_count):
    half = ROT // 2
    freq = jnp.exp(jnp.arange(half, dtype=jnp.float32) * (-2.0 * math.log(10000.0) / ROT))
    angles = positions.astype(jnp.float32)[:, None] * freq[None, :]
    cosine = jnp.concatenate([jnp.cos(angles), jnp.cos(angles)], axis=1)
    sine = jnp.concatenate([jnp.sin(angles), jnp.sin(angles)], axis=1)
    parts = []
    for head in range(head_count):
        base = head * HD
        turned = rows[:, base : base + ROT]
        swapped = jnp.concatenate([-turned[:, half:], turned[:, :half]], axis=1)
        parts += [turned * cosine + swapped * sine, rows[:, base + ROT : base + HD]]
    return jnp.concatenate(parts, axis=1)


def exchange_kernel(axis, n, gather, x_ref, out_ref, send_sem, recv_sem, local_sem):
    me = lax.axis_index(axis)
    barrier = pltpu.get_barrier_semaphore()
    for k in range(1, n):
        pl.semaphore_signal(
            barrier, inc=1, device_id={axis: lax.rem(me + k, n)}, device_id_type=MESH
        )
    pl.semaphore_wait(barrier, n - 1)
    local = pltpu.make_async_copy(x_ref if gather else x_ref.at[me], out_ref.at[me], local_sem)
    local.start()
    copies = []
    for k in range(1, n):
        dest = lax.rem(me + k, n)
        copy = pltpu.make_async_remote_copy(
            src_ref=x_ref if gather else x_ref.at[dest],
            dst_ref=out_ref.at[me],
            send_sem=send_sem.at[k],
            recv_sem=recv_sem.at[k],
            device_id={axis: dest},
            device_id_type=MESH,
        )
        copy.start()
        copies.append(copy)
    for copy in copies:
        copy.wait()
    local.wait()


def exchange_gelu_kernel(axis, n, start, x_ref, hidden_ref, out_ref, act_ref, send_sem, recv_sem, local_sem):
    me = lax.axis_index(axis)
    barrier = pltpu.get_barrier_semaphore()
    for k in range(1, n):
        pl.semaphore_signal(
            barrier, inc=1, device_id={axis: lax.rem(me + k, n)}, device_id_type=MESH
        )
    pl.semaphore_wait(barrier, n - 1)
    local = pltpu.make_async_copy(x_ref.at[me], out_ref.at[me], local_sem)
    local.start()
    copies = []
    for k in range(1, n):
        dest = lax.rem(me + k, n)
        copy = pltpu.make_async_remote_copy(
            src_ref=x_ref.at[dest],
            dst_ref=out_ref.at[me],
            send_sem=send_sem.at[k],
            recv_sem=recv_sem.at[k],
            device_id={axis: dest},
            device_id_type=MESH,
        )
        copy.start()
        copies.append(copy)
    tile = 128

    @pl.loop(0, hidden_ref.shape[0] // tile)
    def _(index):
        rows = pl.ds(pl.multiple_of(index * tile, tile), tile)
        values = hidden_ref[rows, start : start + act_ref.shape[1]].astype(jnp.float32)
        gelu = 0.5 * values * (1.0 + lax.erf(values * (1.0 / math.sqrt(2.0))))
        act_ref[rows, :] = gelu.astype(act_ref.dtype)

    for copy in copies:
        copy.wait()
    local.wait()


def exchange_gelu(x, summed, start, axis, n, collective_id):
    hidden = jax.ShapeDtypeStruct((summed.shape[0], summed.shape[1] - start), jnp.bfloat16)
    return pl.pallas_call(
        functools.partial(exchange_gelu_kernel, axis, n, start),
        out_shape=(
            jax.ShapeDtypeStruct(x.shape, x.dtype),
            hidden,
        ),
        in_specs=[pl.BlockSpec(memory_space=pltpu.VMEM)] * 2,
        out_specs=(pl.BlockSpec(memory_space=pltpu.VMEM),) * 2,
        scratch_shapes=[
            pltpu.SemaphoreType.DMA((n,)),
            pltpu.SemaphoreType.DMA((n,)),
            pltpu.SemaphoreType.DMA(()),
        ],
        compiler_params=pltpu.CompilerParams(
            collective_id=collective_id, has_side_effects=True
        ),
        cost_estimate=pl.CostEstimate(
            flops=20 * hidden.size,
            transcendentals=hidden.size,
            bytes_accessed=2 * n * x.size * x.dtype.itemsize + 4 * hidden.size,
        ),
    )(x, summed)


def gather_grid_kernel(axis, side, x_ref, out_ref, send_sem, recv_sem, local_sem):
    me = lax.axis_index(axis)
    row, col = me // side, me % side
    row_peers = [row * side + lax.rem(col + k, side) for k in range(1, side)]
    col_peers = [lax.rem(row + k, side) * side + col for k in range(1, side)]
    barrier = pltpu.get_barrier_semaphore()
    for peer in row_peers + col_peers:
        pl.semaphore_signal(barrier, inc=1, device_id={axis: peer}, device_id_type=MESH)
    pl.semaphore_wait(barrier, 2 * (side - 1))
    local = pltpu.make_async_copy(x_ref, out_ref.at[me], local_sem)
    local.start()
    first = []
    for k, peer in enumerate(row_peers):
        copy = pltpu.make_async_remote_copy(
            src_ref=x_ref,
            dst_ref=out_ref.at[me],
            send_sem=send_sem.at[0, k],
            recv_sem=recv_sem.at[0, k],
            device_id={axis: peer},
            device_id_type=MESH,
        )
        copy.start()
        first.append(copy)
    for copy in first:
        copy.wait()
    local.wait()
    slab = out_ref.at[pl.ds(row * side, side)]
    second = []
    for k, peer in enumerate(col_peers):
        copy = pltpu.make_async_remote_copy(
            src_ref=slab,
            dst_ref=slab,
            send_sem=send_sem.at[1, k],
            recv_sem=recv_sem.at[1, k],
            device_id={axis: peer},
            device_id_type=MESH,
        )
        copy.start()
        second.append(copy)
    for copy in second:
        copy.wait()


def gather_grid(x, axis, n, collective_id):
    side = math.isqrt(n)
    return pl.pallas_call(
        functools.partial(gather_grid_kernel, axis, side),
        out_shape=jax.ShapeDtypeStruct((n,) + x.shape, x.dtype),
        in_specs=[pl.BlockSpec(memory_space=pltpu.VMEM)],
        out_specs=pl.BlockSpec(memory_space=pltpu.VMEM),
        scratch_shapes=[
            pltpu.SemaphoreType.DMA((2, side - 1)),
            pltpu.SemaphoreType.DMA((2, side - 1)),
            pltpu.SemaphoreType.DMA(()),
        ],
        compiler_params=pltpu.CompilerParams(
            collective_id=collective_id, has_side_effects=True
        ),
        cost_estimate=pl.CostEstimate(
            flops=0, transcendentals=0, bytes_accessed=2 * n * x.size * x.dtype.itemsize
        ),
    )(x)


def exchange(x, axis, n, gather, collective_id):
    shape = (n,) + (x.shape if gather else x.shape[1:])
    return pl.pallas_call(
        functools.partial(exchange_kernel, axis, n, gather),
        out_shape=jax.ShapeDtypeStruct(shape, x.dtype),
        in_specs=[pl.BlockSpec(memory_space=pltpu.VMEM)],
        out_specs=pl.BlockSpec(memory_space=pltpu.VMEM),
        scratch_shapes=[
            pltpu.SemaphoreType.DMA((n,)),
            pltpu.SemaphoreType.DMA((n,)),
            pltpu.SemaphoreType.DMA(()),
        ],
        compiler_params=pltpu.CompilerParams(
            collective_id=collective_id, has_side_effects=True
        ),
        cost_estimate=pl.CostEstimate(
            flops=0, transcendentals=0, bytes_accessed=2 * n * x.size * x.dtype.itemsize
        ),
    )(x)


def exchange_flat(x, axis, n, gather, collective_id):
    lead = () if gather else x.shape[:1]
    block_shape = x.shape if gather else x.shape[1:]
    size = math.prod(block_shape)
    padded = -(-size // 128) * 128
    flat = x.reshape(lead + (size,))
    flat = jnp.pad(flat, [(0, 0)] * len(lead) + [(0, padded - size)])
    flat = flat.reshape(lead + (padded // 128, 128))
    out = exchange(flat, axis, n, gather, collective_id)
    return out.reshape(n, padded)[:, :size].reshape((n,) + block_shape)


def row_normalize(values, collective_id):
    width = values.shape[-1]
    local_mean = jnp.mean(values, axis=-1)
    centred = values - local_mean[..., None]
    local_m2 = jnp.sum(centred * centred, axis=-1)
    stats = jnp.stack([local_mean, local_m2], axis=0)
    stats = exchange_flat(stats, "req", lax.axis_size("req"), True, collective_id)
    stats = jnp.moveaxis(stats, 1, -1)
    means = stats[..., 0]
    row_mean = jnp.mean(means, axis=0)
    spread = means - row_mean
    row_m2 = jnp.sum(stats[..., 1], axis=0) + width * jnp.sum(spread * spread, axis=0)
    row_var = row_m2 / (width * stats.shape[0])
    return (values - row_mean[..., None]) * lax.rsqrt(row_var + EPSILON)[..., None]


def shards(
    inputs,
    norm_gains,
    attn_weight,
    up_weight,
    dense_weight,
    down_weight,
    next_weight,
    cache_keys,
    cache_values,
    lengths,
    slot_table,
    parents,
):
    scale = 1.0 / math.sqrt(HD)
    highest = lax.Precision.HIGHEST
    steps, local_rows, local_width = inputs.shape
    own_count = parents.shape[1]
    request_count = lengths.shape[0]
    beam_total = request_count * BEAM
    head_count = dense_weight.shape[0] // HD
    triple_width = attn_weight.shape[1]
    slot_count = slot_table.shape[1]
    req_size = beam_total // own_count
    mlp_size = beam_total // local_rows
    offset = lax.axis_index("req") * own_count
    beam_group = jnp.arange(beam_total, dtype=jnp.int32) // BEAM
    all_positions = lengths[beam_group][None, :] + jnp.arange(steps, dtype=jnp.int32)[:, None]
    own_group = jnp.arange(own_count, dtype=jnp.int32) // BEAM
    slot_owner = slot_table[0]
    slot_pageno = slot_table[1]
    valid_owner = jnp.maximum(slot_owner, 0)
    token_pos = slot_pageno[:, None] * PAGE + jnp.arange(PAGE, dtype=jnp.int32)[None, :]
    live = (slot_owner[:, None] >= 0) & (token_pos < lengths[valid_owner][:, None])
    live_wide = live[None, :, None, None, :]
    owner_mask = slot_owner[:, None] == jnp.arange(request_count, dtype=jnp.int32)[None, :]
    owner_float = owner_mask.astype(jnp.float32)
    gather_rows = valid_owner[:, None] * BEAM + jnp.arange(BEAM, dtype=jnp.int32)[None, :]

    block = inputs.astype(jnp.float32)
    rows_all = gather_grid(inputs, "mlp", mlp_size, 0).reshape(steps * beam_total, -1)
    normed = row_normalize(rows_all.astype(jnp.float32), 3)
    attn_in = (normed * norm_gains[0]).astype(jnp.bfloat16)
    mlp_in = (normed * norm_gains[1]).astype(jnp.bfloat16)
    grouped = (
        attn_weight.reshape(local_width, head_count, 3, HD)
        .transpose(0, 2, 1, 3)
        .reshape(local_width, triple_width)
    )
    first = jnp.dot(attn_in, grouped, preferred_element_type=jnp.float32)
    second = jnp.dot(mlp_in, up_weight, preferred_element_type=jnp.float32)
    partial_sums = jnp.concatenate([first, second], axis=1)
    summed_all = lax.psum(partial_sums.astype(jnp.bfloat16), "req")
    width = head_count * HD
    row = jnp.arange(steps * beam_total, dtype=jnp.int32)
    beam_lengths = jnp.broadcast_to(lengths[:, None], (request_count, BEAM)).reshape(
        mlp_size, 1, local_rows
    )
    row_positions = (
        beam_lengths + jnp.arange(steps, dtype=jnp.int32)[None, :, None]
    ).reshape(steps * beam_total)
    queries_rows = rotate_rows(
        summed_all[:, :width].astype(jnp.float32), row_positions, head_count
    ).astype(jnp.bfloat16)
    per_own = own_count // local_rows
    own_start = lax.axis_index("req") * (per_own * steps * local_rows)

    def own_rows(rows):
        return lax.dynamic_slice_in_dim(rows, own_start, per_own * steps * local_rows, 0)

    def by_step(rows):
        return (
            rows.reshape(per_own, steps, local_rows, -1)
            .transpose(1, 0, 2, 3)
            .reshape(steps, own_count, head_count, HD)
        )

    queries_own = by_step(own_rows(queries_rows))
    keys_new = by_step(
        rotate_rows(
            own_rows(summed_all[:, width : 2 * width].astype(jnp.float32)),
            own_rows(row_positions),
            head_count,
        ).astype(jnp.bfloat16)
    )
    values_new = by_step(own_rows(summed_all[:, 2 * width : 3 * width]))

    chosen_rows = (
        (gather_rows // local_rows) * (steps * local_rows)
        + jnp.arange(steps, dtype=jnp.int32)[:, None, None] * local_rows
        + gather_rows % local_rows
    )
    chosen = pick_rows(queries_rows, chosen_rows)
    head_scores = [
        jnp.einsum(
            "zsbd,std->zsbt",
            chosen[..., head * HD : (head + 1) * HD],
            cache_keys[:, :, head * HD : (head + 1) * HD],
            preferred_element_type=jnp.float32,
        )
        for head in range(head_count)
    ]
    scores = jnp.stack(head_scores, axis=3) * scale
    masked = jnp.where(live_wide, scores, NEG_FILL)
    slot_top = jnp.max(masked, axis=4)
    weights = jnp.where(live_wide, jnp.exp(masked - slot_top[..., None]), 0.0)
    slot_total = jnp.sum(weights, axis=4)
    rounded = weights.astype(jnp.bfloat16)
    slot_out = jnp.stack(
        [
            jnp.einsum(
                "zsbt,std->zsbd",
                rounded[:, :, :, head],
                cache_values[:, :, head * HD : (head + 1) * HD],
                preferred_element_type=jnp.float32,
            )
            for head in range(head_count)
        ],
        axis=3,
    )
    request_top = jnp.max(
        jnp.where(owner_mask[None, :, :, None, None], slot_top[:, :, None], NEG_FILL), axis=1
    )
    top_high = request_top.astype(jnp.bfloat16)
    top_low = (request_top - top_high.astype(jnp.float32)).astype(jnp.bfloat16)
    request_top = top_high.astype(jnp.float32) + top_low.astype(jnp.float32)
    factor = jnp.where(
        (slot_owner[None, :, None, None] >= 0) & (slot_top > 0.5 * NEG_FILL),
        jnp.exp(slot_top - request_top[:, valid_owner]),
        0.0,
    )
    page_total = jnp.einsum(
        "sr,zsbh->zrbh", owner_float, slot_total * factor, precision=highest
    ).reshape(steps, beam_total, head_count)
    page_out = jnp.einsum(
        "sr,zsbhd->zrbhd", owner_float, slot_out * factor[..., None], precision=highest
    ).reshape(steps, beam_total, head_count, HD)
    stats = jnp.concatenate(
        [
            page_total.astype(jnp.bfloat16),
            top_high.reshape(steps, beam_total, head_count),
            top_low.reshape(steps, beam_total, head_count),
        ],
        axis=-1,
    )
    packed = jnp.concatenate(
        [
            page_out.astype(jnp.bfloat16).reshape(steps, beam_total, head_count * HD),
            jnp.pad(stats, ((0, 0), (0, 0), (0, HD - 3 * head_count))),
        ],
        axis=-1,
    )
    packed = packed.reshape(steps, req_size, own_count, -1).transpose(1, 0, 2, 3)
    held, activated_all = exchange_gelu(packed, summed_all, triple_width, "req", req_size, 5)
    held = held.astype(jnp.float32)
    base = head_count * HD
    held_top = held[..., base + head_count : base + 2 * head_count] + held[
        ..., base + 2 * head_count : base + 3 * head_count
    ]
    own_top = jnp.max(held_top, axis=0)
    rescale = jnp.exp(held_top - own_top)
    own_total = jnp.sum(held[..., base : base + head_count] * rescale, axis=0)
    own_out = jnp.stack(
        [
            jnp.sum(held[..., head * HD : (head + 1) * HD] * rescale[..., head : head + 1], axis=0)
            for head in range(head_count)
        ],
        axis=2,
    )

    source = own_group * BEAM + parents[0]
    def history(table):
        empty = jnp.zeros_like(table[0])
        return jnp.stack(
            [
                jnp.stack(
                    [
                        pick_rows(table[n], source) if n < s else table[s] if n == s else empty
                        for n in range(steps)
                    ]
                )
                for s in range(steps)
            ]
        )

    filled = (
        jnp.arange(steps, dtype=jnp.int32)[None, :] <= jnp.arange(steps, dtype=jnp.int32)[:, None]
    )[:, None, None, :]
    own_scores = (
        jnp.einsum(
            "zbhd,znbhd->zbhn", queries_own, history(keys_new), preferred_element_type=jnp.float32
        )
        * scale
    )
    own_scores = jnp.where(filled, own_scores, NEG_FILL)
    top = jnp.maximum(own_top, jnp.max(own_scores, axis=3))
    page_factor = jnp.exp(own_top - top)
    own_weights = jnp.where(filled, jnp.exp(own_scores - top[..., None]), 0.0)
    total = own_total * page_factor + jnp.sum(own_weights, axis=3)
    summed = own_out * page_factor[..., None] + jnp.einsum(
        "zbhn,znbhd->zbhd",
        own_weights.astype(jnp.bfloat16),
        history(values_new),
        preferred_element_type=jnp.float32,
    )
    attended = (summed / total[..., None]).astype(jnp.bfloat16).reshape(
        steps, own_count, head_count * HD
    )
    attended_all = exchange(attended, "req", req_size, True, 6)
    attended_msi = (
        attended_all.reshape(req_size, steps, per_own, local_rows, -1)
        .transpose(0, 2, 1, 3, 4)
        .reshape(steps * beam_total, -1)
    )
    update_partial = (
        jnp.dot(attended_msi, dense_weight, preferred_element_type=jnp.float32)
        + jnp.dot(activated_all, down_weight, preferred_element_type=jnp.float32)
    ).astype(jnp.bfloat16)
    update = jnp.sum(
        exchange(
            update_partial.reshape(mlp_size, steps * local_rows, local_width),
            "mlp",
            mlp_size,
            False,
            1,
        ).astype(jnp.float32),
        axis=0,
    )
    layer = (block + update.reshape(steps, local_rows, local_width)).astype(jnp.bfloat16)
    next_in = (row_normalize(layer.astype(jnp.float32), 4) * norm_gains[2]).astype(jnp.bfloat16)
    gathered = gather_grid(next_in, "mlp", mlp_size, 2).reshape(steps * beam_total, -1)
    next_partial = jnp.dot(gathered, next_weight, preferred_element_type=jnp.float32)
    next_parts = exchange(
        next_partial.astype(jnp.bfloat16).reshape(req_size, -1, next_partial.shape[1]),
        "req",
        req_size,
        False,
        7,
    )
    next_out = jnp.sum(next_parts.astype(jnp.float32), axis=0).astype(jnp.bfloat16)
    next_out = (
        next_out.reshape(per_own, steps, local_rows, -1)
        .transpose(1, 0, 2, 3)
        .reshape(steps, own_count, -1)
    )
    return (layer, next_out)


def solution(mesh):
    in_specs = (
        P(None, "mlp", "req"),
        P(None, "req"),
        P("req", "mlp"),
        P("req", "mlp"),
        P("mlp", "req"),
        P("mlp", "req"),
        P("req", "mlp"),
        P("req", None, "mlp"),
        P("req", None, "mlp"),
        P(),
        P(None, "req"),
        P(None, "req"),
    )
    out_specs = (P(None, "mlp", "req"), P(None, "req", "mlp"))
    return jax.shard_map(shards, mesh=mesh, in_specs=in_specs, out_specs=out_specs, check_vma=False)
```
